256 devices in a mesh: kern: 4 (over x_lo, core), tile: 64 (over z, y, x_hi).
Axes of the slice: x: 4 (x_hi: 2, x_lo: 2; x = x_hi * 2 + x_lo), y: 4, z: 8, core: 2. Of those that a mesh axis runs over, the one named last changes fastest.
Arguments:
- mask: int32 [2048, 512], P('tile'), may hold values 0 or 1
- kernels: bfloat16 [24, 2, 64, 64], replicated, may hold values from -0.09375 to 0.09375
- socs_weights: float32 [24], replicated, may hold values from 0.02 to 0.3
- quencher: float32 [2048, 512], P('tile', 'kern'), may hold values from 0.1 to 0.6
Outputs:
- intensity: float32 [2048, 512], P('tile', 'kern')
- acid_final: float32 [2048, 512], P('tile', 'kern')
- base_final: float32 [2048, 512], P('tile', 'kern')
The draws below stay inside these ranges and needn't reach their ends.
All inputs are finite; a program needn't handle non-finite values. No bound on the sum of `mask` on one device may be relied on, other than what follows from the above.
Results may differ from the reference program's by a relative error of at most 0.0003.
Values sent between devices are 32-bit elements; how exact they have to be, the bound alone decides.
A program may use at most 128 MiB of HBM per device.

```python
import math
import jax
import jax.numpy as jnp
from jax import lax

K = 24
AMBIT = 64
STEPS = 8
ROWS = 2048
COLS = 512


def touch_ends(array, own_key, least, top_value):
    longest = array.shape.index(max(array.shape))
    spots = []
    for shift in (0, 1):
        where = [jax.random.randint(jax.random.fold_in(own_key, axis), (), 0, length) for axis, length in enumerate(array.shape)]
        where[longest] = (where[longest] + shift) % array.shape[longest]
        spots.append(tuple(where))
    return array.at[spots[0]].set(least).at[spots[1]].set(top_value)


def level_of(own_key, extent, cuts, least, top_value):
    level, own = 1.0, jax.random.fold_in(own_key, 6)
    for axis_at, parts in cuts:
        heights = jnp.exp(jax.random.uniform(jax.random.fold_in(own, axis_at), (parts,), jnp.float32, least / len(cuts), top_value / len(cuts)))
        level = level * jnp.repeat(heights, extent[axis_at] // parts).reshape([-1 if axis == axis_at else 1 for axis in range(len(extent))])
    return level


def bell_draw(key, extent, scale, reach, dtype=jnp.bfloat16):
    return jnp.clip(scale * jax.random.normal(key, extent, jnp.float32), -reach, reach).astype(dtype)


def setup_inputs(seed: int = 0) -> dict:
    streams_of = jax.random.split(jax.random.key(seed), 5)
    mask = touch_ends((jax.random.randint(streams_of[0], (ROWS, COLS), 0, 2) < 1).astype(jnp.int32), jax.random.fold_in(streams_of[0], 1), 0, 1)
    kernels = bell_draw(streams_of[1], (K, 2, AMBIT, AMBIT), (AMBIT * AMBIT) ** -0.5, 0.09375)
    socs_weights = jnp.clip(jnp.exp(jax.random.uniform(streams_of[2], (K,), jnp.float32, math.log(0.02), math.log(0.3))), 0.02, 0.3)
    quencher = jnp.clip(0.1 + 0.5 * jax.random.uniform(streams_of[3], (ROWS, COLS), jnp.float32) ** level_of(streams_of[3], (ROWS, COLS), ((0, 64), (1, 4)), -0.2, 0.2), 0.1, 0.6)
    return {"mask": mask, "kernels": kernels, "socs_weights": socs_weights, "quencher": quencher}


DIFFUSE_ACID = 0.2
DIFFUSE_BASE = 0.1
QUENCH_RATE = 0.5
EXPOSURE = 0.35


def react(padded):
    middle = padded[:, 1:-1, 1:-1]
    spread = padded[:, :-2, 1:-1] + padded[:, 2:, 1:-1] + padded[:, 1:-1, :-2] + padded[:, 1:-1, 2:] - 4.0 * middle
    quenched = QUENCH_RATE * middle[0] * middle[1]
    acid_next = middle[0] + DIFFUSE_ACID * spread[0] - quenched
    base_next = middle[1] + DIFFUSE_BASE * spread[1] - quenched
    return jnp.stack([acid_next, base_next], axis=0)


def reference(mask, kernels, socs_weights, quencher):
    total_rows = mask.shape[0]
    total_cols = mask.shape[1]
    half_ambit = AMBIT // 2
    frame = (total_rows + AMBIT, total_cols + AMBIT)
    mask_field = jnp.zeros(frame, jnp.float32).at[:total_rows, :total_cols].set(mask.astype(jnp.float32))
    mask_spectrum = jnp.fft.rfft2(mask_field)

    def add_kernel(carry, member):
        kernel_pair, weight = member
        placed = jnp.zeros((2,) + frame, jnp.float32).at[:, :AMBIT, :AMBIT].set(kernel_pair.astype(jnp.float32))
        placed = jnp.roll(placed, (-half_ambit, -half_ambit), axis=(1, 2))
        spectrum = jnp.conj(jnp.fft.rfft2(placed))
        fields = jnp.fft.irfft2(mask_spectrum[None] * spectrum, s=frame)[:, :total_rows, :total_cols]
        return carry + weight * jnp.sum(fields * fields, axis=0), weight

    intensity = lax.scan(add_kernel, jnp.zeros((total_rows, total_cols), jnp.float32), (kernels, socs_weights))[0]
    acid = 1.0 - jnp.exp(-EXPOSURE * intensity)
    resist_state = jnp.stack([acid, quencher], axis=0)
    for step_index in range(STEPS):
        resist_state = react(jnp.pad(resist_state, ((0, 0), (1, 1), (1, 1))))
    return intensity, resist_state[0], resist_state[1]
```

```python
import jax
import jax.numpy as jnp
from jax import lax
from jax.sharding import PartitionSpec as P

STEPS = 8


DIFFUSE_ACID = 0.2
DIFFUSE_BASE = 0.1
QUENCH_RATE = 0.5
EXPOSURE = 0.35


def shifted(value, axis, steps):
    count = lax.axis_size(axis)
    leading, last = (max(0, -steps), min(count, count - steps))
    return lax.ppermute(value, axis, [(source, source + steps) for source in range(leading, last)])


def padded_2(block, sides, width):
    for axis, dim in sides:
        count = lax.axis_size(axis)
        forward = [(i, i + 1) for i in range(count - 1)]
        backward = [(target, source) for source, target in forward]
        low = lax.ppermute(
            lax.slice_in_dim(block, block.shape[dim] - width, None, axis=dim), axis, forward
        )
        high = lax.ppermute(lax.slice_in_dim(block, 0, width, axis=dim), axis, backward)
        block = jnp.concatenate([low, block, high], axis=dim)
    return block


def react(padded):
    middle = padded[:, 1:-1, 1:-1]
    spread = (
        padded[:, :-2, 1:-1]
        + padded[:, 2:, 1:-1]
        + padded[:, 1:-1, :-2]
        + padded[:, 1:-1, 2:]
        - 4.0 * middle
    )
    quenched = QUENCH_RATE * middle[0] * middle[1]
    acid_next = middle[0] + DIFFUSE_ACID * spread[0] - quenched
    base_next = middle[1] + DIFFUSE_BASE * spread[1] - quenched
    return jnp.stack([acid_next, base_next], axis=0)


def band_table(ambit_size):
    tap_ids = lax.iota(jnp.int32, ambit_size)
    input_ids = lax.iota(jnp.int32, 2 * ambit_size)
    output_ids = lax.iota(jnp.int32, ambit_size)
    offsets = input_ids[None, :, None] - output_ids[None, None, :]
    return (offsets == tap_ids[:, None, None]).astype(jnp.bfloat16)


def field_band(mask_rows, kernel_group, ambit_size, edge_rows):
    column_blocks = (mask_rows.shape[1] - ambit_size) // ambit_size
    padded_rows = jnp.pad(mask_rows, ((edge_rows, edge_rows), (0, 0)))
    total_padded = padded_rows.shape[0]
    halves = padded_rows.reshape(total_padded, column_blocks + 1, ambit_size)
    windows = jnp.concatenate([halves[:, :-1], halves[:, 1:]], axis=2)
    band_rows = total_padded - ambit_size
    kernel_count = kernel_group.shape[0]
    selector = band_table(ambit_size)
    accumulated = jnp.zeros((band_rows * column_blocks, kernel_count * 2 * ambit_size), jnp.float32)
    for group_index in range(ambit_size // 8):
        first = group_index * 8
        stacked = jnp.stack(
            [windows[first + offset : first + offset + band_rows] for offset in range(8)], axis=2
        )
        left_side = stacked.reshape(band_rows * column_blocks, 16 * ambit_size)
        taps = kernel_group[:, :, first : first + 8, :]
        banded_taps = jnp.einsum(
            "kprb,bco->rckpo", taps, selector, preferred_element_type=jnp.float32
        ).astype(jnp.bfloat16)
        right_side = banded_taps.reshape(16 * ambit_size, kernel_count * 2 * ambit_size)
        accumulated = accumulated + jnp.dot(
            left_side, right_side, preferred_element_type=jnp.float32
        )
    banded = accumulated.reshape(band_rows, column_blocks, kernel_count, 2, ambit_size)
    banded = jnp.transpose(banded, (2, 3, 0, 1, 4))
    return banded.reshape(kernel_count, 2, band_rows, column_blocks * ambit_size)


def on_device(mask, kernels, socs_weights, quencher):
    ambit_size = kernels.shape[2]
    half_ambit = ambit_size // 2
    kern_count = lax.axis_size("kern")
    kern_index = lax.axis_index("kern")
    local_rows = mask.shape[0]
    padded_mask = jnp.pad(mask.astype(jnp.bfloat16), ((0, 0), (half_ambit, half_ambit)))
    per_group = kernels.shape[0] // kern_count
    own_kernels = lax.dynamic_slice_in_dim(kernels, kern_index * per_group, per_group, 0)
    own_weights = lax.dynamic_slice_in_dim(socs_weights, kern_index * per_group, per_group, 0)
    fields = field_band(padded_mask, own_kernels, ambit_size, ambit_size)
    upper_rim = fields[:, :, :half_ambit]
    lower_rim = fields[:, :, local_rows + half_ambit :]
    centre = fields[:, :, half_ambit : local_rows + half_ambit]
    from_above = shifted(lower_rim, "tile", 1)
    from_below = shifted(upper_rim, "tile", -1)
    centre = centre + from_above
    centre = centre + from_below
    squared = centre[:, 0] * centre[:, 0] + centre[:, 1] * centre[:, 1]
    partial_value = jnp.sum(own_weights[:, None, None] * squared, axis=0)
    intensity = lax.psum_scatter(partial_value, "kern", scatter_dimension=1, tiled=True)
    acid = 1.0 - jnp.exp(-EXPOSURE * intensity)
    resist_state = jnp.stack([acid, quencher], axis=0)
    resist_state = padded_2(resist_state, (("kern", 2), ("tile", 1)), STEPS)
    rows_total = local_rows * lax.axis_size("tile")
    cols_total = intensity.shape[1] * kern_count
    row_origin = lax.axis_index("tile") * local_rows
    col_origin = kern_index * intensity.shape[1]
    for step_index in range(STEPS):
        resist_state = react(resist_state)
        reach = STEPS - step_index - 1
        if reach:
            height, width = resist_state.shape[1], resist_state.shape[2]
            rows = row_origin - reach + lax.broadcasted_iota(jnp.int32, (height, width), 0)
            cols = col_origin - reach + lax.broadcasted_iota(jnp.int32, (height, width), 1)
            inside = (rows >= 0) & (rows < rows_total) & (cols >= 0) & (cols < cols_total)
            resist_state = jnp.where(inside[None], resist_state, 0.0)
    return (intensity, resist_state[0], resist_state[1])


def solution(mesh):
    placed = (P("tile", None), P(), P(), P("tile", "kern"))
    return jax.shard_map(
        on_device,
        mesh=mesh,
        in_specs=placed,
        out_specs=(P("tile", "kern"), P("tile", "kern"), P("tile", "kern")),
        check_vma=False,
    )
```

```python
import functools

import jax
import jax.numpy as jnp
from jax import lax
from jax.experimental import pallas as pl
from jax.experimental.pallas import tpu as pltpu
from jax.sharding import PartitionSpec as P

STEPS = 8


DIFFUSE_ACID = 0.2
DIFFUSE_BASE = 0.1
QUENCH_RATE = 0.5
EXPOSURE = 0.35

BLOCKS = 8
TAP_GROUP = 8


def shifted(value, axis, steps):
    count = lax.axis_size(axis)
    leading, last = (max(0, -steps), min(count, count - steps))
    return lax.ppermute(value, axis, [(source, source + steps) for source in range(leading, last)])


def padded_2(block, sides, width):
    for axis, dim in sides:
        count = lax.axis_size(axis)
        forward = [(i, i + 1) for i in range(count - 1)]
        backward = [(target, source) for source, target in forward]
        low = lax.ppermute(
            lax.slice_in_dim(block, block.shape[dim] - width, None, axis=dim), axis, forward
        )
        high = lax.ppermute(lax.slice_in_dim(block, 0, width, axis=dim), axis, backward)
        block = jnp.concatenate([low, block, high], axis=dim)
    return block


def react(padded):
    middle = padded[:, 1:-1, 1:-1]
    spread = (
        padded[:, :-2, 1:-1]
        + padded[:, 2:, 1:-1]
        + padded[:, 1:-1, :-2]
        + padded[:, 1:-1, 2:]
        - 4.0 * middle
    )
    quenched = QUENCH_RATE * middle[0] * middle[1]
    acid_next = middle[0] + DIFFUSE_ACID * spread[0] - quenched
    base_next = middle[1] + DIFFUSE_BASE * spread[1] - quenched
    return jnp.stack([acid_next, base_next], axis=0)


def toeplitz_taps(kernels, window, width):
    ambit = kernels.shape[-1]
    tap_ids = lax.iota(jnp.int32, ambit)
    input_ids = lax.iota(jnp.int32, window)
    output_ids = lax.iota(jnp.int32, width)
    offsets = input_ids[None, :, None] - output_ids[None, None, :]
    selector = (offsets == tap_ids[:, None, None]).astype(jnp.bfloat16)
    taps = jnp.einsum(
        "kpab,bco->ackpo", kernels, selector, preferred_element_type=jnp.float32
    ).astype(jnp.bfloat16)
    return taps.reshape(kernels.shape[2] * window, -1)


def field_kernel(x_ref, t_ref, o_ref, *, out_rows, window):
    step = pl.program_id(0)

    @pl.when(step == 0)
    def _():
        o_ref[...] = jnp.zeros_like(o_ref)

    pieces = []
    for offset in range(TAP_GROUP):
        tap = step * TAP_GROUP + offset
        start = pl.multiple_of(tap * BLOCKS, BLOCKS)
        pieces.append(x_ref[pl.ds(start, out_rows * BLOCKS), :].astype(jnp.bfloat16))
    left = jnp.concatenate(pieces, axis=1)
    o_ref[...] += jnp.dot(left, t_ref[...], preferred_element_type=jnp.float32)


def fields_of(windows, taps, out_rows, window, ambit):
    width_n = taps.shape[1]
    m_rows = out_rows * BLOCKS
    groups = ambit // TAP_GROUP

    return pl.pallas_call(
        functools.partial(field_kernel, out_rows=out_rows, window=window),
        out_shape=jax.ShapeDtypeStruct((m_rows, width_n), jnp.float32),
        grid=(groups,),
        in_specs=[
            pl.BlockSpec(windows.shape, lambda g: (0, 0)),
            pl.BlockSpec((TAP_GROUP * window, width_n), lambda g: (g, 0)),
        ],
        out_specs=pl.BlockSpec((m_rows, width_n), lambda g: (0, 0)),
        compiler_params=pltpu.CompilerParams(vmem_limit_bytes=48 * 1024 * 1024),
        cost_estimate=pl.CostEstimate(
            flops=2 * m_rows * ambit * window * width_n,
            transcendentals=0,
            bytes_accessed=taps.size * 2 + m_rows * width_n * 4,
        ),
    )(windows, taps)


def on_device(mask, kernels, socs_weights, quencher):
    ambit = kernels.shape[2]
    half_ambit = ambit // 2
    kern_count = lax.axis_size("kern")
    kern_index = lax.axis_index("kern")
    tile_index = lax.axis_index("tile")
    local_rows = mask.shape[0]
    local_cols = quencher.shape[1]
    halo = STEPS
    out_rows = local_rows + 2 * halo
    out_cols = local_cols + 2 * halo
    width = out_cols // BLOCKS
    window = 128

    base = padded_2(quencher[None], (("kern", 2), ("tile", 1)), halo)[0]

    reach = halo + half_ambit - local_rows
    up2 = shifted(mask[local_rows - reach :], "tile", 2)
    up1 = shifted(mask, "tile", 1)
    down1 = shifted(mask, "tile", -1)
    down2 = shifted(mask[:reach], "tile", -2)
    rows = jnp.concatenate([up2, up1, mask, down1, down2], axis=0).astype(jnp.float32)
    lead = halo + half_ambit
    span = width * (BLOCKS - 1) + window
    total_cols = mask.shape[1]
    padded = jnp.pad(rows, ((0, 0), (lead, span + local_cols * kern_count - total_cols)))
    cols = lax.dynamic_slice_in_dim(padded, kern_index * local_cols, span, axis=1)
    windows = jnp.stack(
        [cols[:, width * block : width * block + window] for block in range(BLOCKS)], axis=1
    )
    windows = windows.reshape(-1, window)

    taps = toeplitz_taps(kernels, window, width)
    fields = fields_of(windows, taps, out_rows, window, ambit)
    fields = fields.reshape(out_rows, BLOCKS, kernels.shape[0], 2, width)
    squared = fields[:, :, :, 0] ** 2 + fields[:, :, :, 1] ** 2
    intensity_ext = jnp.sum(squared * socs_weights[None, None, :, None], axis=2)
    intensity_ext = intensity_ext.reshape(out_rows, out_cols)
    intensity = intensity_ext[halo : halo + local_rows, halo : halo + local_cols]

    rows_total = local_rows * lax.axis_size("tile")
    cols_total = local_cols * kern_count
    row_origin = tile_index * local_rows
    col_origin = kern_index * local_cols

    def inside(reach_now, height, width_now):
        r = row_origin - reach_now + lax.broadcasted_iota(jnp.int32, (height, width_now), 0)
        c = col_origin - reach_now + lax.broadcasted_iota(jnp.int32, (height, width_now), 1)
        return (r >= 0) & (r < rows_total) & (c >= 0) & (c < cols_total)

    acid = 1.0 - jnp.exp(-EXPOSURE * intensity_ext)
    acid = jnp.where(inside(halo, out_rows, out_cols), acid, 0.0)
    resist_state = jnp.stack([acid, base], axis=0)
    for step_index in range(STEPS):
        resist_state = react(resist_state)
        reach_now = STEPS - step_index - 1
        if reach_now:
            keep = inside(reach_now, resist_state.shape[1], resist_state.shape[2])
            resist_state = jnp.where(keep[None], resist_state, 0.0)
    return (intensity, resist_state[0], resist_state[1])


def solution(mesh):
    placed = (P("tile", None), P(), P(), P("tile", "kern"))
    return jax.shard_map(
        on_device,
        mesh=mesh,
        in_specs=placed,
        out_specs=(P("tile", "kern"), P("tile", "kern"), P("tile", "kern")),
        check_vma=False,
    )
```

```python
import functools

import jax
import jax.numpy as jnp
from jax import lax
from jax.experimental import pallas as pl
from jax.experimental.pallas import tpu as pltpu
from jax.sharding import PartitionSpec as P

STEPS = 8


DIFFUSE_ACID = 0.2
DIFFUSE_BASE = 0.1
QUENCH_RATE = 0.5
EXPOSURE = 0.35

BLOCKS = 8
TAP_GROUP = 8


def shifted(value, axis, steps):
    count = lax.axis_size(axis)
    leading, last = (max(0, -steps), min(count, count - steps))
    return lax.ppermute(value, axis, [(source, source + steps) for source in range(leading, last)])


def padded_2(block, sides, width):
    for axis, dim in sides:
        count = lax.axis_size(axis)
        forward = [(i, i + 1) for i in range(count - 1)]
        backward = [(target, source) for source, target in forward]
        low = lax.ppermute(
            lax.slice_in_dim(block, block.shape[dim] - width, None, axis=dim), axis, forward
        )
        high = lax.ppermute(lax.slice_in_dim(block, 0, width, axis=dim), axis, backward)
        block = jnp.concatenate([low, block, high], axis=dim)
    return block


def react(padded):
    middle = padded[:, 1:-1, 1:-1]
    spread = (
        padded[:, :-2, 1:-1]
        + padded[:, 2:, 1:-1]
        + padded[:, 1:-1, :-2]
        + padded[:, 1:-1, 2:]
        - 4.0 * middle
    )
    quenched = QUENCH_RATE * middle[0] * middle[1]
    acid_next = middle[0] + DIFFUSE_ACID * spread[0] - quenched
    base_next = middle[1] + DIFFUSE_BASE * spread[1] - quenched
    return jnp.stack([acid_next, base_next], axis=0)


def toeplitz_selector(ambit, window, width):
    tap_ids = lax.iota(jnp.int32, ambit)
    input_ids = lax.iota(jnp.int32, window)
    output_ids = lax.iota(jnp.int32, width)
    offsets = input_ids[None, None, :] - output_ids[None, :, None]
    selector = (offsets == tap_ids[:, None, None]).astype(jnp.bfloat16)
    return selector.reshape(ambit, width * window)


def field_kernel(x_ref, k_ref, sel_ref, w_ref, s_ref, o_ref, acc_ref, *, out_rows, pairs, window):
    step = pl.program_id(0)
    width = sel_ref.shape[1] // window

    @pl.when(step == 0)
    def _():
        acc_ref[...] = jnp.zeros_like(acc_ref)

    kernel_rows = k_ref[pl.ds(pl.multiple_of(step * TAP_GROUP * pairs, pairs), TAP_GROUP * pairs), :]
    taps = jnp.dot(kernel_rows, sel_ref[...], preferred_element_type=jnp.float32).astype(
        jnp.bfloat16
    )
    pieces = []
    columns = []
    for offset in range(TAP_GROUP):
        tap = step * TAP_GROUP + offset
        start = pl.multiple_of(tap * BLOCKS, BLOCKS)
        pieces.append(x_ref[pl.ds(start, out_rows * BLOCKS), :].astype(jnp.bfloat16))
        columns.append(
            jnp.concatenate(
                [
                    taps[offset * pairs : (offset + 1) * pairs, o * window : (o + 1) * window]
                    for o in range(width)
                ],
                axis=0,
            )
        )
    left = jnp.concatenate(pieces, axis=1)
    right = jnp.concatenate(columns, axis=1)
    acc_ref[...] += lax.dot_general(
        left, right, (((1,), (1,)), ((), ())), preferred_element_type=jnp.float32
    )

    @pl.when(step == pl.num_programs(0) - 1)
    def _():
        field = acc_ref[...]
        weighted = field * field * w_ref[...]
        o_ref[...] = jnp.dot(
            weighted, s_ref[...], precision=lax.Precision.HIGHEST,
            preferred_element_type=jnp.float32,
        )


def intensity_of(windows, kernel_rows, selector, lane_weights, summer, out_rows, ambit):
    window = windows.shape[1]
    width = summer.shape[1]
    pairs = kernel_rows.shape[0] // ambit
    width_n = pairs * width
    m_rows = out_rows * BLOCKS
    groups = ambit // TAP_GROUP

    return pl.pallas_call(
        functools.partial(field_kernel, out_rows=out_rows, pairs=pairs, window=window),
        out_shape=jax.ShapeDtypeStruct((m_rows, width), jnp.float32),
        grid=(groups,),
        in_specs=[
            pl.BlockSpec(windows.shape, lambda g: (0, 0)),
            pl.BlockSpec(kernel_rows.shape, lambda g: (0, 0)),
            pl.BlockSpec(selector.shape, lambda g: (0, 0)),
            pl.BlockSpec(lane_weights.shape, lambda g: (0, 0)),
            pl.BlockSpec(summer.shape, lambda g: (0, 0)),
        ],
        out_specs=pl.BlockSpec((m_rows, width), lambda g: (0, 0)),
        scratch_shapes=[pltpu.VMEM((m_rows, width_n), jnp.float32)],
        compiler_params=pltpu.CompilerParams(vmem_limit_bytes=48 * 1024 * 1024),
        cost_estimate=pl.CostEstimate(
            flops=2 * m_rows * ambit * window * width_n,
            transcendentals=0,
            bytes_accessed=windows.size * 4 + kernel_rows.size * 2,
        ),
    )(windows, kernel_rows, selector, lane_weights, summer)


def on_device(mask, kernels, socs_weights, quencher):
    ambit = kernels.shape[2]
    half_ambit = ambit // 2
    kern_count = lax.axis_size("kern")
    kern_index = lax.axis_index("kern")
    tile_index = lax.axis_index("tile")
    local_rows = mask.shape[0]
    local_cols = quencher.shape[1]
    halo = STEPS
    out_rows = local_rows + 2 * halo
    out_cols = local_cols + 2 * halo
    width = out_cols // BLOCKS
    window = 128

    base = padded_2(quencher[None], (("kern", 2), ("tile", 1)), halo)[0]

    reach = halo + half_ambit - local_rows
    up2 = shifted(mask[local_rows - reach :], "tile", 2)
    up1 = shifted(mask, "tile", 1)
    down1 = shifted(mask, "tile", -1)
    down2 = shifted(mask[:reach], "tile", -2)
    rows = jnp.concatenate([up2, up1, mask, down1, down2], axis=0).astype(jnp.float32)
    lead = halo + half_ambit
    span = width * (BLOCKS - 1) + window
    total_cols = mask.shape[1]
    padded = jnp.pad(rows, ((0, 0), (lead, span + local_cols * kern_count - total_cols)))
    cols = lax.dynamic_slice_in_dim(padded, kern_index * local_cols, span, axis=1)
    windows = jnp.stack(
        [cols[:, width * block : width * block + window] for block in range(BLOCKS)], axis=1
    )
    windows = windows.reshape(-1, window)

    pairs = kernels.shape[0] * kernels.shape[1]
    kernel_rows = jnp.transpose(kernels, (2, 0, 1, 3)).reshape(ambit * pairs, ambit)
    selector = toeplitz_selector(ambit, window, width)
    lane_weights = jnp.broadcast_to(
        socs_weights[None, :, None], (width, kernels.shape[0], kernels.shape[1])
    ).reshape(1, width * pairs)
    summer = (
        lax.iota(jnp.int32, width * pairs)[:, None] // pairs == lax.iota(jnp.int32, width)[None, :]
    ).astype(jnp.float32)
    intensity_ext = intensity_of(
        windows, kernel_rows, selector, lane_weights, summer, out_rows, ambit
    )
    intensity_ext = intensity_ext.reshape(out_rows, out_cols)
    intensity = intensity_ext[halo : halo + local_rows, halo : halo + local_cols]

    rows_total = local_rows * lax.axis_size("tile")
    cols_total = local_cols * kern_count
    row_origin = tile_index * local_rows
    col_origin = kern_index * local_cols

    def inside(reach_now, height, width_now):
        r = row_origin - reach_now + lax.broadcasted_iota(jnp.int32, (height, width_now), 0)
        c = col_origin - reach_now + lax.broadcasted_iota(jnp.int32, (height, width_now), 1)
        return (r >= 0) & (r < rows_total) & (c >= 0) & (c < cols_total)

    acid = 1.0 - jnp.exp(-EXPOSURE * intensity_ext)
    acid = jnp.where(inside(halo, out_rows, out_cols), acid, 0.0)
    resist_state = jnp.stack([acid, base], axis=0)
    for step_index in range(STEPS):
        resist_state = react(resist_state)
        reach_now = STEPS - step_index - 1
        if reach_now:
            keep = inside(reach_now, resist_state.shape[1], resist_state.shape[2])
            resist_state = jnp.where(keep[None], resist_state, 0.0)
    return (intensity, resist_state[0], resist_state[1])


def solution(mesh):
    placed = (P("tile", None), P(), P(), P("tile", "kern"))
    return jax.shard_map(
        on_device,
        mesh=mesh,
        in_specs=placed,
        out_specs=(P("tile", "kern"), P("tile", "kern"), P("tile", "kern")),
        check_vma=False,
    )
```

```python
import functools

import jax
import jax.numpy as jnp
from jax import lax
from jax.experimental import pallas as pl
from jax.experimental.pallas import tpu as pltpu
from jax.sharding import PartitionSpec as P

STEPS = 8


DIFFUSE_ACID = 0.2
DIFFUSE_BASE = 0.1
QUENCH_RATE = 0.5
EXPOSURE = 0.35

BLOCKS = 8
TAP_GROUP = 8


def shifted(value, axis, steps):
    count = lax.axis_size(axis)
    leading, last = (max(0, -steps), min(count, count - steps))
    return lax.ppermute(value, axis, [(source, source + steps) for source in range(leading, last)])


def padded_2(block, sides, width):
    for axis, dim in sides:
        count = lax.axis_size(axis)
        forward = [(i, i + 1) for i in range(count - 1)]
        backward = [(target, source) for source, target in forward]
        low = lax.ppermute(
            lax.slice_in_dim(block, block.shape[dim] - width, None, axis=dim), axis, forward
        )
        high = lax.ppermute(lax.slice_in_dim(block, 0, width, axis=dim), axis, backward)
        block = jnp.concatenate([low, block, high], axis=dim)
    return block


def react(padded):
    middle = padded[:, 1:-1, 1:-1]
    spread = (
        padded[:, :-2, 1:-1]
        + padded[:, 2:, 1:-1]
        + padded[:, 1:-1, :-2]
        + padded[:, 1:-1, 2:]
        - 4.0 * middle
    )
    quenched = QUENCH_RATE * middle[0] * middle[1]
    acid_next = middle[0] + DIFFUSE_ACID * spread[0] - quenched
    base_next = middle[1] + DIFFUSE_BASE * spread[1] - quenched
    return jnp.stack([acid_next, base_next], axis=0)


def toeplitz_selector(ambit, window, width):
    tap_ids = lax.iota(jnp.int32, ambit)
    input_ids = lax.iota(jnp.int32, window)
    output_ids = lax.iota(jnp.int32, width)
    offsets = input_ids[None, None, :] - output_ids[None, :, None]
    selector = (offsets == tap_ids[:, None, None]).astype(jnp.bfloat16)
    return selector.reshape(ambit, width * window)


def field_kernel(x_ref, k_ref, sel_ref, w_ref, s_ref, o_ref, acc_ref, *, out_rows, pairs, window):
    step = pl.program_id(0)
    width = sel_ref.shape[1] // window

    @pl.when(step == 0)
    def _():
        acc_ref[...] = jnp.zeros_like(acc_ref)

    kernel_rows = k_ref[pl.ds(pl.multiple_of(step * TAP_GROUP * pairs, pairs), TAP_GROUP * pairs), :]
    taps = jnp.dot(kernel_rows, sel_ref[...], preferred_element_type=jnp.float32).astype(
        jnp.bfloat16
    )
    pieces = []
    columns = []
    for offset in range(TAP_GROUP):
        tap = step * TAP_GROUP + offset
        start = pl.multiple_of(tap * BLOCKS, BLOCKS)
        pieces.append(x_ref[pl.ds(start, out_rows * BLOCKS), :].astype(jnp.bfloat16))
        columns.append(
            jnp.concatenate(
                [
                    taps[offset * pairs : (offset + 1) * pairs, o * window : (o + 1) * window]
                    for o in range(width)
                ],
                axis=0,
            )
        )
    left = jnp.concatenate(pieces, axis=1)
    right = jnp.concatenate(columns, axis=1)
    acc_ref[...] += lax.dot_general(
        left, right, (((1,), (1,)), ((), ())), preferred_element_type=jnp.float32
    )

    @pl.when(step == pl.num_programs(0) - 1)
    def _():
        field = acc_ref[...]
        weighted = field * field * w_ref[...]
        o_ref[...] = jnp.dot(
            weighted, s_ref[...], precision=lax.Precision.HIGHEST,
            preferred_element_type=jnp.float32,
        )


def intensity_of(windows, kernel_rows, selector, lane_weights, summer, out_rows, ambit):
    window = windows.shape[1]
    width = summer.shape[1]
    pairs = kernel_rows.shape[0] // ambit
    width_n = pairs * width
    m_rows = out_rows * BLOCKS
    groups = ambit // TAP_GROUP

    return pl.pallas_call(
        functools.partial(field_kernel, out_rows=out_rows, pairs=pairs, window=window),
        out_shape=jax.ShapeDtypeStruct((m_rows, width), jnp.float32),
        grid=(groups,),
        in_specs=[
            pl.BlockSpec(windows.shape, lambda g: (0, 0)),
            pl.BlockSpec(kernel_rows.shape, lambda g: (0, 0)),
            pl.BlockSpec(selector.shape, lambda g: (0, 0)),
            pl.BlockSpec(lane_weights.shape, lambda g: (0, 0)),
            pl.BlockSpec(summer.shape, lambda g: (0, 0)),
        ],
        out_specs=pl.BlockSpec((m_rows, width), lambda g: (0, 0)),
        scratch_shapes=[pltpu.VMEM((m_rows, width_n), jnp.float32)],
        compiler_params=pltpu.CompilerParams(vmem_limit_bytes=48 * 1024 * 1024),
        cost_estimate=pl.CostEstimate(
            flops=2 * m_rows * ambit * window * width_n,
            transcendentals=0,
            bytes_accessed=windows.size * 4 + kernel_rows.size * 2,
        ),
    )(windows, kernel_rows, selector, lane_weights, summer)


MASK_FROM = ((-1, 0), (1, 0), (-2, 0), (2, 0))
QUENCH_FROM = ((-1, -1), (-1, 0), (-1, 1), (0, -1), (0, 1), (1, -1), (1, 0), (1, 1))


def exchange_kernel(mask_ref, q_ref, mask_out, q_out, mask_slots, q_slots, send_sems, recv_sems):
    tile = lax.axis_index("tile")
    kern = lax.axis_index("kern")
    tiles = lax.axis_size("tile")
    kerns = lax.axis_size("kern")

    def exists(dt, dq):
        return (tile + dt >= 0) & (tile + dt < tiles) & (kern + dq >= 0) & (kern + dq < kerns)

    def device(dt, dq):
        return {"tile": tile + dt, "kern": kern + dq}

    barrier = pltpu.get_barrier_semaphore()
    partners = sorted(set(MASK_FROM) | set(QUENCH_FROM))
    count = jnp.int32(0)
    for dt, dq in partners:
        here = exists(dt, dq)

        @pl.when(here)
        def _():
            pl.semaphore_signal(
                barrier, 1, device_id=device(dt, dq), device_id_type=pl.DeviceIdType.MESH
            )

        count = count + here.astype(jnp.int32)
    pl.semaphore_wait(barrier, count)

    plan = [(mask_ref, mask_slots, slot, offset) for slot, offset in enumerate(MASK_FROM)]
    plan += [(q_ref, q_slots, slot, offset) for slot, offset in enumerate(QUENCH_FROM)]
    copies = []
    for index, (source, slots, slot, (dt, dq)) in enumerate(plan):
        copy = pltpu.make_async_remote_copy(
            src_ref=source,
            dst_ref=slots.at[slot],
            send_sem=send_sems.at[index],
            recv_sem=recv_sems.at[index],
            device_id=device(-dt, -dq),
            device_id_type=pl.DeviceIdType.MESH,
        )

        @pl.when(exists(-dt, -dq))
        def _():
            copy.start()

        copies.append(copy)
    for copy, (source, slots, slot, (dt, dq)) in zip(copies, plan):

        @pl.when(exists(-dt, -dq))
        def _():
            copy.wait_send()

        @pl.when(exists(dt, dq))
        def _():
            copy.wait_recv()

    for out, slots, offsets in ((mask_out, mask_slots, MASK_FROM), (q_out, q_slots, QUENCH_FROM)):
        for slot, (dt, dq) in enumerate(offsets):
            here = exists(dt, dq)

            @pl.when(here)
            def _():
                out[slot] = slots[slot]

            @pl.when(jnp.logical_not(here))
            def _():
                out[slot] = jnp.zeros(out.shape[1:], out.dtype)


def exchange(mask, quencher):
    mask_shape = (len(MASK_FROM),) + mask.shape
    q_shape = (len(QUENCH_FROM),) + quencher.shape
    vmem = pl.BlockSpec(memory_space=pltpu.VMEM)
    return pl.pallas_call(
        exchange_kernel,
        out_shape=(
            jax.ShapeDtypeStruct(mask_shape, mask.dtype),
            jax.ShapeDtypeStruct(q_shape, quencher.dtype),
        ),
        in_specs=[vmem, vmem],
        out_specs=(vmem, vmem),
        scratch_shapes=[
            pltpu.VMEM(mask_shape, mask.dtype),
            pltpu.VMEM(q_shape, quencher.dtype),
            pltpu.SemaphoreType.DMA((len(MASK_FROM) + len(QUENCH_FROM),)),
            pltpu.SemaphoreType.DMA((len(MASK_FROM) + len(QUENCH_FROM),)),
        ],
        compiler_params=pltpu.CompilerParams(collective_id=0, has_side_effects=True),
    )(mask, quencher)


def on_device(mask, kernels, socs_weights, quencher):
    ambit = kernels.shape[2]
    half_ambit = ambit // 2
    kern_count = lax.axis_size("kern")
    kern_index = lax.axis_index("kern")
    tile_index = lax.axis_index("tile")
    local_rows = mask.shape[0]
    local_cols = quencher.shape[1]
    halo = STEPS
    out_rows = local_rows + 2 * halo
    out_cols = local_cols + 2 * halo
    width = out_cols // BLOCKS
    window = 128

    mask_from, q_from = exchange(mask, quencher)
    top = jnp.concatenate(
        [q_from[0][-halo:, -halo:], q_from[1][-halo:], q_from[2][-halo:, :halo]], axis=1
    )
    middle = jnp.concatenate([q_from[3][:, -halo:], quencher, q_from[4][:, :halo]], axis=1)
    bottom = jnp.concatenate(
        [q_from[5][:halo, -halo:], q_from[6][:halo], q_from[7][:halo, :halo]], axis=1
    )
    base = jnp.concatenate([top, middle, bottom], axis=0)

    reach = halo + half_ambit - local_rows
    rows = jnp.concatenate(
        [mask_from[2][local_rows - reach :], mask_from[0], mask, mask_from[1], mask_from[3][:reach]],
        axis=0,
    ).astype(jnp.float32)
    lead = halo + half_ambit
    span = width * (BLOCKS - 1) + window
    total_cols = mask.shape[1]
    padded = jnp.pad(rows, ((0, 0), (lead, span + local_cols * kern_count - total_cols)))
    cols = lax.dynamic_slice_in_dim(padded, kern_index * local_cols, span, axis=1)
    windows = jnp.stack(
        [cols[:, width * block : width * block + window] for block in range(BLOCKS)], axis=1
    )
    windows = windows.reshape(-1, window)

    pairs = kernels.shape[0] * kernels.shape[1]
    kernel_rows = jnp.transpose(kernels, (2, 0, 1, 3)).reshape(ambit * pairs, ambit)
    selector = toeplitz_selector(ambit, window, width)
    lane_weights = jnp.broadcast_to(
        socs_weights[None, :, None], (width, kernels.shape[0], kernels.shape[1])
    ).reshape(1, width * pairs)
    summer = (
        lax.iota(jnp.int32, width * pairs)[:, None] // pairs == lax.iota(jnp.int32, width)[None, :]
    ).astype(jnp.float32)
    intensity_ext = intensity_of(
        windows, kernel_rows, selector, lane_weights, summer, out_rows, ambit
    )
    intensity_ext = intensity_ext.reshape(out_rows, out_cols)
    intensity = intensity_ext[halo : halo + local_rows, halo : halo + local_cols]

    rows_total = local_rows * lax.axis_size("tile")
    cols_total = local_cols * kern_count
    row_origin = tile_index * local_rows
    col_origin = kern_index * local_cols

    def inside(reach_now, height, width_now):
        r = row_origin - reach_now + lax.broadcasted_iota(jnp.int32, (height, width_now), 0)
        c = col_origin - reach_now + lax.broadcasted_iota(jnp.int32, (height, width_now), 1)
        return (r >= 0) & (r < rows_total) & (c >= 0) & (c < cols_total)

    acid = 1.0 - jnp.exp(-EXPOSURE * intensity_ext)
    acid = jnp.where(inside(halo, out_rows, out_cols), acid, 0.0)
    resist_state = jnp.stack([acid, base], axis=0)
    for step_index in range(STEPS):
        resist_state = react(resist_state)
        reach_now = STEPS - step_index - 1
        if reach_now:
            keep = inside(reach_now, resist_state.shape[1], resist_state.shape[2])
            resist_state = jnp.where(keep[None], resist_state, 0.0)
    return (intensity, resist_state[0], resist_state[1])


def solution(mesh):
    placed = (P("tile", None), P(), P(), P("tile", "kern"))
    return jax.shard_map(
        on_device,
        mesh=mesh,
        in_specs=placed,
        out_specs=(P("tile", "kern"), P("tile", "kern"), P("tile", "kern")),
        check_vma=False,
    )
```

```python
import functools

import jax
import jax.numpy as jnp
from jax import lax
from jax.experimental import pallas as pl
from jax.experimental.pallas import tpu as pltpu
from jax.sharding import PartitionSpec as P

STEPS = 8


DIFFUSE_ACID = 0.2
DIFFUSE_BASE = 0.1
QUENCH_RATE = 0.5
EXPOSURE = 0.35

BLOCKS = 8
TAP_GROUP = 8


def shifted(value, axis, steps):
    count = lax.axis_size(axis)
    leading, last = (max(0, -steps), min(count, count - steps))
    return lax.ppermute(value, axis, [(source, source + steps) for source in range(leading, last)])


def padded_2(block, sides, width):
    for axis, dim in sides:
        count = lax.axis_size(axis)
        forward = [(i, i + 1) for i in range(count - 1)]
        backward = [(target, source) for source, target in forward]
        low = lax.ppermute(
            lax.slice_in_dim(block, block.shape[dim] - width, None, axis=dim), axis, forward
        )
        high = lax.ppermute(lax.slice_in_dim(block, 0, width, axis=dim), axis, backward)
        block = jnp.concatenate([low, block, high], axis=dim)
    return block


def react(padded):
    middle = padded[:, 1:-1, 1:-1]
    spread = (
        padded[:, :-2, 1:-1]
        + padded[:, 2:, 1:-1]
        + padded[:, 1:-1, :-2]
        + padded[:, 1:-1, 2:]
        - 4.0 * middle
    )
    quenched = QUENCH_RATE * middle[0] * middle[1]
    acid_next = middle[0] + DIFFUSE_ACID * spread[0] - quenched
    base_next = middle[1] + DIFFUSE_BASE * spread[1] - quenched
    return jnp.stack([acid_next, base_next], axis=0)


def toeplitz_selector(ambit, window, width):
    tap_ids = lax.iota(jnp.int32, ambit)
    input_ids = lax.iota(jnp.int32, window)
    output_ids = lax.iota(jnp.int32, width)
    offsets = input_ids[None, None, :] - output_ids[None, :, None]
    selector = (offsets == tap_ids[:, None, None]).astype(jnp.bfloat16)
    return selector.reshape(ambit, width * window)


def spread_of(value):
    rows, lanes = value.shape
    up = pltpu.roll(value, 1, 0)
    down = pltpu.roll(value, rows - 1, 0)
    left = pltpu.roll(value, 1, 1)
    right = pltpu.roll(value, lanes - 1, 1)
    return up + down + left + right - 4.0 * value


def field_kernel(
    x_ref, k_ref, sel_ref, w_ref, s_ref, keep_ref, base_ref,
    i_out, a_out, b_out, acc_ref, red_ref, *, out_rows, pairs, window, halo,
):
    step = pl.program_id(0)
    width = sel_ref.shape[1] // window

    @pl.when(step == 0)
    def _():
        acc_ref[...] = jnp.zeros_like(acc_ref)

    kernel_rows = k_ref[pl.ds(pl.multiple_of(step * TAP_GROUP * pairs, pairs), TAP_GROUP * pairs), :]
    taps = jnp.dot(kernel_rows, sel_ref[...], preferred_element_type=jnp.float32).astype(
        jnp.bfloat16
    )
    pieces = []
    columns = []
    for offset in range(TAP_GROUP):
        tap = step * TAP_GROUP + offset
        start = pl.multiple_of(tap * BLOCKS, BLOCKS)
        pieces.append(x_ref[pl.ds(start, out_rows * BLOCKS), :].astype(jnp.bfloat16))
        columns.append(
            jnp.concatenate(
                [
                    taps[offset * pairs : (offset + 1) * pairs, o * window : (o + 1) * window]
                    for o in range(width)
                ],
                axis=0,
            )
        )
    left = jnp.concatenate(pieces, axis=1)
    right = jnp.concatenate(columns, axis=1)
    acc_ref[...] += lax.dot_general(
        left, right, (((1,), (1,)), ((), ())), preferred_element_type=jnp.float32
    )

    @pl.when(step == pl.num_programs(0) - 1)
    def _():
        lanes = keep_ref.shape[1]
        field = acc_ref[...]
        weighted = field * field * w_ref[...]
        red_ref[...] = jnp.dot(
            weighted, s_ref[...], precision=lax.Precision.HIGHEST,
            preferred_element_type=jnp.float32,
        )
        intensity = jnp.zeros((out_rows, lanes), jnp.float32)
        for block in range(BLOCKS):
            part = red_ref[pl.ds(block, out_rows, stride=BLOCKS), :]
            part = jnp.concatenate([part, jnp.zeros_like(part)], axis=1)
            intensity = intensity + pltpu.roll(part, width * block, 1) if block else part
        keep = keep_ref[...] > 0.5
        acid = jnp.where(keep, 1.0 - jnp.exp(-EXPOSURE * intensity), 0.0)
        base = base_ref[...]
        for _ in range(STEPS):
            quenched = QUENCH_RATE * acid * base
            acid_next = acid + DIFFUSE_ACID * spread_of(acid) - quenched
            base_next = base + DIFFUSE_BASE * spread_of(base) - quenched
            acid = jnp.where(keep, acid_next, 0.0)
            base = jnp.where(keep, base_next, 0.0)
        rows, cols = i_out.shape
        for out, value in ((i_out, intensity), (a_out, acid), (b_out, base)):
            out[...] = pltpu.roll(value, lanes - halo, 1)[halo : halo + rows, :cols]


def resist_of(windows, kernel_rows, selector, lane_weights, summer, keep, base, out_rows, ambit, halo, local):
    window = windows.shape[1]
    width = selector.shape[1] // window
    pairs = kernel_rows.shape[0] // ambit
    width_n = pairs * width
    m_rows = out_rows * BLOCKS
    groups = ambit // TAP_GROUP
    whole = lambda g: (0, 0)
    out = jax.ShapeDtypeStruct(local, jnp.float32)

    return pl.pallas_call(
        functools.partial(field_kernel, out_rows=out_rows, pairs=pairs, window=window, halo=halo),
        out_shape=(out, out, out),
        grid=(groups,),
        in_specs=[
            pl.BlockSpec(windows.shape, whole),
            pl.BlockSpec(kernel_rows.shape, whole),
            pl.BlockSpec(selector.shape, whole),
            pl.BlockSpec(lane_weights.shape, whole),
            pl.BlockSpec(summer.shape, whole),
            pl.BlockSpec(keep.shape, whole),
            pl.BlockSpec(base.shape, whole),
        ],
        out_specs=(pl.BlockSpec(local, whole),) * 3,
        scratch_shapes=[
            pltpu.VMEM((m_rows, width_n), jnp.float32),
            pltpu.VMEM((m_rows, summer.shape[1]), jnp.float32),
        ],
        compiler_params=pltpu.CompilerParams(vmem_limit_bytes=48 * 1024 * 1024),
        cost_estimate=pl.CostEstimate(
            flops=2 * m_rows * ambit * window * width_n,
            transcendentals=0,
            bytes_accessed=windows.size * 4 + kernel_rows.size * 2,
        ),
    )(windows, kernel_rows, selector, lane_weights, summer, keep, base)


MASK_FROM = ((-1, 0), (1, 0), (-2, 0), (2, 0))
QUENCH_FROM = ((-1, -1), (-1, 0), (-1, 1), (0, -1), (0, 1), (1, -1), (1, 0), (1, 1))


def exchange_kernel(mask_ref, q_ref, mask_out, q_out, mask_slots, q_slots, send_sems, recv_sems):
    tile = lax.axis_index("tile")
    kern = lax.axis_index("kern")
    tiles = lax.axis_size("tile")
    kerns = lax.axis_size("kern")

    def exists(dt, dq):
        return (tile + dt >= 0) & (tile + dt < tiles) & (kern + dq >= 0) & (kern + dq < kerns)

    def device(dt, dq):
        return {"tile": tile + dt, "kern": kern + dq}

    barrier = pltpu.get_barrier_semaphore()
    partners = sorted(set(MASK_FROM) | set(QUENCH_FROM))
    count = jnp.int32(0)
    for dt, dq in partners:
        here = exists(dt, dq)

        @pl.when(here)
        def _():
            pl.semaphore_signal(
                barrier, 1, device_id=device(dt, dq), device_id_type=pl.DeviceIdType.MESH
            )

        count = count + here.astype(jnp.int32)
    pl.semaphore_wait(barrier, count)

    plan = [(mask_ref, mask_slots, slot, offset) for slot, offset in enumerate(MASK_FROM)]
    plan += [(q_ref, q_slots, slot, offset) for slot, offset in enumerate(QUENCH_FROM)]
    copies = []
    for index, (source, slots, slot, (dt, dq)) in enumerate(plan):
        copy = pltpu.make_async_remote_copy(
            src_ref=source,
            dst_ref=slots.at[slot],
            send_sem=send_sems.at[index],
            recv_sem=recv_sems.at[index],
            device_id=device(-dt, -dq),
            device_id_type=pl.DeviceIdType.MESH,
        )

        @pl.when(exists(-dt, -dq))
        def _():
            copy.start()

        copies.append(copy)
    for copy, (source, slots, slot, (dt, dq)) in zip(copies, plan):

        @pl.when(exists(-dt, -dq))
        def _():
            copy.wait_send()

        @pl.when(exists(dt, dq))
        def _():
            copy.wait_recv()

    for out, slots, offsets in ((mask_out, mask_slots, MASK_FROM), (q_out, q_slots, QUENCH_FROM)):
        for slot, (dt, dq) in enumerate(offsets):
            here = exists(dt, dq)

            @pl.when(here)
            def _():
                out[slot] = slots[slot]

            @pl.when(jnp.logical_not(here))
            def _():
                out[slot] = jnp.zeros(out.shape[1:], out.dtype)


def exchange(mask, quencher):
    mask_shape = (len(MASK_FROM),) + mask.shape
    q_shape = (len(QUENCH_FROM),) + quencher.shape
    vmem = pl.BlockSpec(memory_space=pltpu.VMEM)
    return pl.pallas_call(
        exchange_kernel,
        out_shape=(
            jax.ShapeDtypeStruct(mask_shape, mask.dtype),
            jax.ShapeDtypeStruct(q_shape, quencher.dtype),
        ),
        in_specs=[vmem, vmem],
        out_specs=(vmem, vmem),
        scratch_shapes=[
            pltpu.VMEM(mask_shape, mask.dtype),
            pltpu.VMEM(q_shape, quencher.dtype),
            pltpu.SemaphoreType.DMA((len(MASK_FROM) + len(QUENCH_FROM),)),
            pltpu.SemaphoreType.DMA((len(MASK_FROM) + len(QUENCH_FROM),)),
        ],
        compiler_params=pltpu.CompilerParams(collective_id=0, has_side_effects=True),
    )(mask, quencher)


def on_device(mask, kernels, socs_weights, quencher):
    ambit = kernels.shape[2]
    half_ambit = ambit // 2
    kern_count = lax.axis_size("kern")
    kern_index = lax.axis_index("kern")
    tile_index = lax.axis_index("tile")
    local_rows = mask.shape[0]
    local_cols = quencher.shape[1]
    halo = STEPS
    out_rows = local_rows + 2 * halo
    out_cols = local_cols + 2 * halo
    width = out_cols // BLOCKS
    window = 128

    mask_from, q_from = exchange(mask, quencher)
    top = jnp.concatenate(
        [q_from[0][-halo:, -halo:], q_from[1][-halo:], q_from[2][-halo:, :halo]], axis=1
    )
    middle = jnp.concatenate([q_from[3][:, -halo:], quencher, q_from[4][:, :halo]], axis=1)
    bottom = jnp.concatenate(
        [q_from[5][:halo, -halo:], q_from[6][:halo], q_from[7][:halo, :halo]], axis=1
    )
    base = jnp.concatenate([top, middle, bottom], axis=0)

    reach = halo + half_ambit - local_rows
    rows = jnp.concatenate(
        [mask_from[2][local_rows - reach :], mask_from[0], mask, mask_from[1], mask_from[3][:reach]],
        axis=0,
    ).astype(jnp.float32)
    lead = halo + half_ambit
    span = width * (BLOCKS - 1) + window
    total_cols = mask.shape[1]
    padded = jnp.pad(rows, ((0, 0), (lead, span + local_cols * kern_count - total_cols)))
    cols = lax.dynamic_slice_in_dim(padded, kern_index * local_cols, span, axis=1)
    windows = jnp.stack(
        [cols[:, width * block : width * block + window] for block in range(BLOCKS)], axis=1
    )
    windows = windows.reshape(-1, window)

    pairs = kernels.shape[0] * kernels.shape[1]
    kernel_rows = jnp.transpose(kernels, (2, 0, 1, 3)).reshape(ambit * pairs, ambit)
    selector = toeplitz_selector(ambit, window, width)
    lane_weights = jnp.broadcast_to(
        socs_weights[None, :, None], (width, kernels.shape[0], kernels.shape[1])
    ).reshape(1, width * pairs)
    lanes = 2 * window
    summer = (
        lax.iota(jnp.int32, width * pairs)[:, None] // pairs == lax.iota(jnp.int32, window)[None, :]
    ).astype(jnp.float32)

    rows_total = local_rows * lax.axis_size("tile")
    cols_total = local_cols * kern_count
    r = tile_index * local_rows - halo + lax.broadcasted_iota(jnp.int32, (out_rows, lanes), 0)
    c = kern_index * local_cols - halo + lax.broadcasted_iota(jnp.int32, (out_rows, lanes), 1)
    keep = (r >= 0) & (r < rows_total) & (c >= 0) & (c < cols_total)
    keep = (keep & (c < kern_index * local_cols - halo + out_cols)).astype(jnp.float32)
    base = jnp.pad(base, ((0, 0), (0, lanes - out_cols)))
    return resist_of(
        windows, kernel_rows, selector, lane_weights, summer, keep, base,
        out_rows, ambit, halo, (local_rows, local_cols),
    )


def solution(mesh):
    placed = (P("tile", None), P(), P(), P("tile", "kern"))
    return jax.shard_map(
        on_device,
        mesh=mesh,
        in_specs=placed,
        out_specs=(P("tile", "kern"), P("tile", "kern"), P("tile", "kern")),
        check_vma=False,
    )
```

```python
import functools

import jax
import jax.numpy as jnp
from jax import lax
from jax.experimental import pallas as pl
from jax.experimental.pallas import tpu as pltpu
from jax.sharding import PartitionSpec as P

STEPS = 8


DIFFUSE_ACID = 0.2
DIFFUSE_BASE = 0.1
QUENCH_RATE = 0.5
EXPOSURE = 0.35

BLOCKS = 8
HALO = STEPS
TAP_GROUP = 8


def shifted(value, axis, steps):
    count = lax.axis_size(axis)
    leading, last = (max(0, -steps), min(count, count - steps))
    return lax.ppermute(value, axis, [(source, source + steps) for source in range(leading, last)])


def padded_2(block, sides, width):
    for axis, dim in sides:
        count = lax.axis_size(axis)
        forward = [(i, i + 1) for i in range(count - 1)]
        backward = [(target, source) for source, target in forward]
        low = lax.ppermute(
            lax.slice_in_dim(block, block.shape[dim] - width, None, axis=dim), axis, forward
        )
        high = lax.ppermute(lax.slice_in_dim(block, 0, width, axis=dim), axis, backward)
        block = jnp.concatenate([low, block, high], axis=dim)
    return block


def react(padded):
    middle = padded[:, 1:-1, 1:-1]
    spread = (
        padded[:, :-2, 1:-1]
        + padded[:, 2:, 1:-1]
        + padded[:, 1:-1, :-2]
        + padded[:, 1:-1, 2:]
        - 4.0 * middle
    )
    quenched = QUENCH_RATE * middle[0] * middle[1]
    acid_next = middle[0] + DIFFUSE_ACID * spread[0] - quenched
    base_next = middle[1] + DIFFUSE_BASE * spread[1] - quenched
    return jnp.stack([acid_next, base_next], axis=0)


def toeplitz_selector(ambit, window, width):
    tap_ids = lax.iota(jnp.int32, ambit)
    input_ids = lax.iota(jnp.int32, window)
    output_ids = lax.iota(jnp.int32, width)
    offsets = input_ids[None, None, :] - output_ids[None, :, None]
    selector = (offsets == tap_ids[:, None, None]).astype(jnp.bfloat16)
    return selector.reshape(ambit, width * window)


def spread_of(value):
    rows, lanes = value.shape
    up = pltpu.roll(value, 1, 0)
    down = pltpu.roll(value, rows - 1, 0)
    left = pltpu.roll(value, 1, 1)
    right = pltpu.roll(value, lanes - 1, 1)
    return up + down + left + right - 4.0 * value


def field_kernel(
    x_ref, k_ref, sel_ref, w_ref, s_ref, keep_ref, base_ref,
    i_out, a_out, b_out, acc_ref, red_ref, *, out_rows, pairs, window, halo,
):
    step = pl.program_id(0)
    width = sel_ref.shape[1] // window

    @pl.when(step == 0)
    def _():
        acc_ref[...] = jnp.zeros_like(acc_ref)

    kernel_rows = k_ref[pl.ds(pl.multiple_of(step * TAP_GROUP * pairs, pairs), TAP_GROUP * pairs), :]
    taps = jnp.dot(kernel_rows, sel_ref[...], preferred_element_type=jnp.float32).astype(
        jnp.bfloat16
    )
    pieces = []
    columns = []
    for offset in range(TAP_GROUP):
        tap = step * TAP_GROUP + offset
        start = pl.multiple_of(tap * BLOCKS, BLOCKS)
        pieces.append(x_ref[pl.ds(start, out_rows * BLOCKS), :].astype(jnp.bfloat16))
        columns.append(
            jnp.concatenate(
                [
                    taps[offset * pairs : (offset + 1) * pairs, o * window : (o + 1) * window]
                    for o in range(width)
                ],
                axis=0,
            )
        )
    left = jnp.concatenate(pieces, axis=1)
    right = jnp.concatenate(columns, axis=1)
    acc_ref[...] += lax.dot_general(
        left, right, (((1,), (1,)), ((), ())), preferred_element_type=jnp.float32
    )

    @pl.when(step == pl.num_programs(0) - 1)
    def _():
        lanes = keep_ref.shape[1]
        field = acc_ref[...]
        weighted = field * field * w_ref[...]
        red_ref[...] = jnp.dot(
            weighted, s_ref[...], precision=lax.Precision.HIGHEST,
            preferred_element_type=jnp.float32,
        )
        intensity = jnp.zeros((out_rows, lanes), jnp.float32)
        for block in range(BLOCKS):
            part = red_ref[pl.ds(block, out_rows, stride=BLOCKS), :]
            part = jnp.concatenate([part, jnp.zeros_like(part)], axis=1)
            intensity = intensity + pltpu.roll(part, width * block, 1) if block else part
        keep = keep_ref[...] > 0.5
        acid = jnp.where(keep, 1.0 - jnp.exp(-EXPOSURE * intensity), 0.0)
        base = base_ref[...]
        for _ in range(STEPS):
            quenched = QUENCH_RATE * acid * base
            acid_next = acid + DIFFUSE_ACID * spread_of(acid) - quenched
            base_next = base + DIFFUSE_BASE * spread_of(base) - quenched
            acid = jnp.where(keep, acid_next, 0.0)
            base = jnp.where(keep, base_next, 0.0)
        rows, cols = i_out.shape
        for out, value in ((i_out, intensity), (a_out, acid), (b_out, base)):
            out[...] = pltpu.roll(value, lanes - halo, 1)[halo : halo + rows, :cols]


def resist_of(windows, kernel_rows, selector, lane_weights, summer, keep, base, out_rows, ambit, halo, local):
    window = windows.shape[1]
    width = selector.shape[1] // window
    pairs = kernel_rows.shape[0] // ambit
    width_n = pairs * width
    m_rows = out_rows * BLOCKS
    groups = ambit // TAP_GROUP
    whole = lambda g: (0, 0)
    out = jax.ShapeDtypeStruct(local, jnp.float32)

    return pl.pallas_call(
        functools.partial(field_kernel, out_rows=out_rows, pairs=pairs, window=window, halo=halo),
        out_shape=(out, out, out),
        grid=(groups,),
        in_specs=[
            pl.BlockSpec(windows.shape, whole),
            pl.BlockSpec(kernel_rows.shape, whole),
            pl.BlockSpec(selector.shape, whole),
            pl.BlockSpec(lane_weights.shape, whole),
            pl.BlockSpec(summer.shape, whole),
            pl.BlockSpec(keep.shape, whole),
            pl.BlockSpec(base.shape, whole),
        ],
        out_specs=(pl.BlockSpec(local, whole),) * 3,
        scratch_shapes=[
            pltpu.VMEM((m_rows, width_n), jnp.float32),
            pltpu.VMEM((m_rows, summer.shape[1]), jnp.float32),
        ],
        compiler_params=pltpu.CompilerParams(vmem_limit_bytes=48 * 1024 * 1024),
        cost_estimate=pl.CostEstimate(
            flops=2 * m_rows * ambit * window * width_n,
            transcendentals=0,
            bytes_accessed=windows.size * 4 + kernel_rows.size * 2,
        ),
    )(windows, kernel_rows, selector, lane_weights, summer, keep, base)


MASK_FROM = ((-1, 0), (1, 0), (-2, 0), (2, 0))
QUENCH_FROM = ((-1, -1), (-1, 0), (-1, 1), (0, -1), (0, 1), (1, -1), (1, 0), (1, 1))


def exchange_kernel(mask_ref, q_ref, mask_out, q_out, mask_slots, q_slots, send_sems, recv_sems):
    tile = lax.axis_index("tile")
    kern = lax.axis_index("kern")
    tiles = lax.axis_size("tile")
    kerns = lax.axis_size("kern")

    def exists(dt, dq):
        return (tile + dt >= 0) & (tile + dt < tiles) & (kern + dq >= 0) & (kern + dq < kerns)

    def device(dt, dq):
        return {"tile": tile + dt, "kern": kern + dq}

    barrier = pltpu.get_barrier_semaphore()
    partners = sorted(set(MASK_FROM) | set(QUENCH_FROM))
    count = jnp.int32(0)
    for dt, dq in partners:
        here = exists(dt, dq)

        @pl.when(here)
        def _():
            pl.semaphore_signal(
                barrier, 1, device_id=device(dt, dq), device_id_type=pl.DeviceIdType.MESH
            )

        count = count + here.astype(jnp.int32)
    pl.semaphore_wait(barrier, count)

    def rows_for(source, dt, whole):
        height = source.shape[0]
        if abs(dt) == 1 and whole:
            return 0, height
        return (height - HALO, HALO) if dt < 0 else (0, HALO)

    plan = [(mask_ref, mask_slots, slot, offset, True) for slot, offset in enumerate(MASK_FROM)]
    plan += [(q_ref, q_slots, slot, offset, False) for slot, offset in enumerate(QUENCH_FROM)]
    copies = []
    for index, (source, slots, slot, (dt, dq), whole) in enumerate(plan):
        if dt == 0:
            first, count = 0, source.shape[0]
        else:
            first, count = rows_for(source, dt, whole)
        copy = pltpu.make_async_remote_copy(
            src_ref=source.at[pl.ds(first, count)],
            dst_ref=slots.at[slot, pl.ds(first, count)],
            send_sem=send_sems.at[index],
            recv_sem=recv_sems.at[index],
            device_id=device(-dt, -dq),
            device_id_type=pl.DeviceIdType.MESH,
        )

        @pl.when(exists(-dt, -dq))
        def _():
            copy.start()

        copies.append((copy, first, count))
    for (copy, first, count), (source, slots, slot, (dt, dq), whole) in zip(copies, plan):

        @pl.when(exists(-dt, -dq))
        def _():
            copy.wait_send()

        out = mask_out if slots is mask_slots else q_out
        here = exists(dt, dq)

        @pl.when(here)
        def _():
            copy.wait_recv()
            out[slot, pl.ds(first, count)] = slots[slot, pl.ds(first, count)]

        @pl.when(jnp.logical_not(here))
        def _():
            out[slot] = jnp.zeros(out.shape[1:], out.dtype)


def exchange(mask, quencher):
    mask_shape = (len(MASK_FROM),) + mask.shape
    q_shape = (len(QUENCH_FROM),) + quencher.shape
    vmem = pl.BlockSpec(memory_space=pltpu.VMEM)
    return pl.pallas_call(
        exchange_kernel,
        out_shape=(
            jax.ShapeDtypeStruct(mask_shape, mask.dtype),
            jax.ShapeDtypeStruct(q_shape, quencher.dtype),
        ),
        in_specs=[vmem, vmem],
        out_specs=(vmem, vmem),
        scratch_shapes=[
            pltpu.VMEM(mask_shape, mask.dtype),
            pltpu.VMEM(q_shape, quencher.dtype),
            pltpu.SemaphoreType.DMA((len(MASK_FROM) + len(QUENCH_FROM),)),
            pltpu.SemaphoreType.DMA((len(MASK_FROM) + len(QUENCH_FROM),)),
        ],
        compiler_params=pltpu.CompilerParams(collective_id=0, has_side_effects=True),
    )(mask, quencher)


def on_device(mask, kernels, socs_weights, quencher):
    ambit = kernels.shape[2]
    half_ambit = ambit // 2
    kern_count = lax.axis_size("kern")
    kern_index = lax.axis_index("kern")
    tile_index = lax.axis_index("tile")
    local_rows = mask.shape[0]
    local_cols = quencher.shape[1]
    halo = STEPS
    out_rows = local_rows + 2 * halo
    out_cols = local_cols + 2 * halo
    width = out_cols // BLOCKS
    window = 128

    mask_from, q_from = exchange(mask, quencher)
    top = jnp.concatenate(
        [q_from[0][-halo:, -halo:], q_from[1][-halo:], q_from[2][-halo:, :halo]], axis=1
    )
    middle = jnp.concatenate([q_from[3][:, -halo:], quencher, q_from[4][:, :halo]], axis=1)
    bottom = jnp.concatenate(
        [q_from[5][:halo, -halo:], q_from[6][:halo], q_from[7][:halo, :halo]], axis=1
    )
    base = jnp.concatenate([top, middle, bottom], axis=0)

    reach = halo + half_ambit - local_rows
    rows = jnp.concatenate(
        [mask_from[2][local_rows - reach :], mask_from[0], mask, mask_from[1], mask_from[3][:reach]],
        axis=0,
    ).astype(jnp.float32)
    lead = halo + half_ambit
    span = width * (BLOCKS - 1) + window
    total_cols = mask.shape[1]
    padded = jnp.pad(rows, ((0, 0), (lead, span + local_cols * kern_count - total_cols)))
    cols = lax.dynamic_slice_in_dim(padded, kern_index * local_cols, span, axis=1)
    windows = jnp.stack(
        [cols[:, width * block : width * block + window] for block in range(BLOCKS)], axis=1
    )
    windows = windows.reshape(-1, window)

    pairs = kernels.shape[0] * kernels.shape[1]
    kernel_rows = jnp.transpose(kernels, (2, 0, 1, 3)).reshape(ambit * pairs, ambit)
    selector = toeplitz_selector(ambit, window, width)
    lane_weights = jnp.broadcast_to(
        socs_weights[None, :, None], (width, kernels.shape[0], kernels.shape[1])
    ).reshape(1, width * pairs)
    lanes = 2 * window
    summer = (
        lax.iota(jnp.int32, width * pairs)[:, None] // pairs == lax.iota(jnp.int32, window)[None, :]
    ).astype(jnp.float32)

    rows_total = local_rows * lax.axis_size("tile")
    cols_total = local_cols * kern_count
    r = tile_index * local_rows - halo + lax.broadcasted_iota(jnp.int32, (out_rows, lanes), 0)
    c = kern_index * local_cols - halo + lax.broadcasted_iota(jnp.int32, (out_rows, lanes), 1)
    keep = (r >= 0) & (r < rows_total) & (c >= 0) & (c < cols_total)
    keep = (keep & (c < kern_index * local_cols - halo + out_cols)).astype(jnp.float32)
    base = jnp.pad(base, ((0, 0), (0, lanes - out_cols)))
    return resist_of(
        windows, kernel_rows, selector, lane_weights, summer, keep, base,
        out_rows, ambit, halo, (local_rows, local_cols),
    )


def solution(mesh):
    placed = (P("tile", None), P(), P(), P("tile", "kern"))
    return jax.shard_map(
        on_device,
        mesh=mesh,
        in_specs=placed,
        out_specs=(P("tile", "kern"), P("tile", "kern"), P("tile", "kern")),
        check_vma=False,
    )
```

```python
import functools

import jax
import jax.numpy as jnp
from jax import lax
from jax.experimental import pallas as pl
from jax.experimental.pallas import tpu as pltpu
from jax.sharding import PartitionSpec as P

STEPS = 8


DIFFUSE_ACID = 0.2
DIFFUSE_BASE = 0.1
QUENCH_RATE = 0.5
EXPOSURE = 0.35

BLOCKS = 8
HALO = STEPS
TAP_GROUP = 8


def shifted(value, axis, steps):
    count = lax.axis_size(axis)
    leading, last = (max(0, -steps), min(count, count - steps))
    return lax.ppermute(value, axis, [(source, source + steps) for source in range(leading, last)])


def padded_2(block, sides, width):
    for axis, dim in sides:
        count = lax.axis_size(axis)
        forward = [(i, i + 1) for i in range(count - 1)]
        backward = [(target, source) for source, target in forward]
        low = lax.ppermute(
            lax.slice_in_dim(block, block.shape[dim] - width, None, axis=dim), axis, forward
        )
        high = lax.ppermute(lax.slice_in_dim(block, 0, width, axis=dim), axis, backward)
        block = jnp.concatenate([low, block, high], axis=dim)
    return block


def react(padded):
    middle = padded[:, 1:-1, 1:-1]
    spread = (
        padded[:, :-2, 1:-1]
        + padded[:, 2:, 1:-1]
        + padded[:, 1:-1, :-2]
        + padded[:, 1:-1, 2:]
        - 4.0 * middle
    )
    quenched = QUENCH_RATE * middle[0] * middle[1]
    acid_next = middle[0] + DIFFUSE_ACID * spread[0] - quenched
    base_next = middle[1] + DIFFUSE_BASE * spread[1] - quenched
    return jnp.stack([acid_next, base_next], axis=0)


def toeplitz_selector(ambit, window, width):
    tap_ids = lax.iota(jnp.int32, ambit)
    input_ids = lax.iota(jnp.int32, window)
    output_ids = lax.iota(jnp.int32, width)
    offsets = input_ids[None, None, :] - output_ids[None, :, None]
    selector = (offsets == tap_ids[:, None, None]).astype(jnp.bfloat16)
    return selector.reshape(ambit, width * window)


def spread_of(value):
    rows, lanes = value.shape
    up = pltpu.roll(value, 1, 0)
    down = pltpu.roll(value, rows - 1, 0)
    left = pltpu.roll(value, 1, 1)
    right = pltpu.roll(value, lanes - 1, 1)
    return up + down + left + right - 4.0 * value


def field_kernel(
    x_ref, k_ref, sel_ref, w_ref, s_ref, keep_ref, base_ref,
    i_out, a_out, b_out, acc_ref, red_ref, *, out_rows, pairs, window, halo,
):
    step = pl.program_id(0)
    width = sel_ref.shape[1] // window

    @pl.when(step == 0)
    def _():
        acc_ref[...] = jnp.zeros_like(acc_ref)

    kernel_rows = k_ref[pl.ds(pl.multiple_of(step * TAP_GROUP * pairs, pairs), TAP_GROUP * pairs), :]
    taps = jnp.dot(kernel_rows, sel_ref[...], preferred_element_type=jnp.float32).astype(
        jnp.bfloat16
    )
    pieces = []
    columns = []
    for offset in range(TAP_GROUP):
        tap = step * TAP_GROUP + offset
        start = pl.multiple_of(tap * BLOCKS, BLOCKS)
        pieces.append(x_ref[pl.ds(start, out_rows * BLOCKS), :].astype(jnp.bfloat16))
        columns.append(
            jnp.concatenate(
                [
                    taps[offset * pairs : (offset + 1) * pairs, o * window : (o + 1) * window]
                    for o in range(width)
                ],
                axis=0,
            )
        )
    left = jnp.concatenate(pieces, axis=1)
    right = jnp.concatenate(columns, axis=1)
    acc_ref[...] += lax.dot_general(
        left, right, (((1,), (1,)), ((), ())), preferred_element_type=jnp.float32
    )

    @pl.when(step == pl.num_programs(0) - 1)
    def _():
        lanes = keep_ref.shape[1]
        field = acc_ref[...]
        weighted = field * field * w_ref[...]
        red_ref[...] = jnp.dot(
            weighted, s_ref[...], precision=lax.Precision.HIGHEST,
            preferred_element_type=jnp.float32,
        )
        intensity = jnp.zeros((out_rows, lanes), jnp.float32)
        for block in range(BLOCKS):
            part = red_ref[pl.ds(block, out_rows, stride=BLOCKS), :]
            part = jnp.concatenate([part, jnp.zeros_like(part)], axis=1)
            intensity = intensity + pltpu.roll(part, width * block, 1) if block else part
        keep = keep_ref[...] > 0.5
        acid = jnp.where(keep, 1.0 - jnp.exp(-EXPOSURE * intensity), 0.0)
        base = base_ref[...]
        for _ in range(STEPS):
            quenched = QUENCH_RATE * acid * base
            acid_next = acid + DIFFUSE_ACID * spread_of(acid) - quenched
            base_next = base + DIFFUSE_BASE * spread_of(base) - quenched
            acid = jnp.where(keep, acid_next, 0.0)
            base = jnp.where(keep, base_next, 0.0)
        rows, cols = i_out.shape
        for out, value in ((i_out, intensity), (a_out, acid), (b_out, base)):
            out[...] = pltpu.roll(value, lanes - halo, 1)[halo : halo + rows, :cols]


def resist_of(windows, kernel_rows, selector, lane_weights, summer, keep, base, out_rows, ambit, halo, local):
    window = windows.shape[1]
    width = selector.shape[1] // window
    pairs = kernel_rows.shape[0] // ambit
    width_n = pairs * width
    m_rows = out_rows * BLOCKS
    groups = ambit // TAP_GROUP
    whole = lambda g: (0, 0)
    out = jax.ShapeDtypeStruct(local, jnp.float32)

    return pl.pallas_call(
        functools.partial(field_kernel, out_rows=out_rows, pairs=pairs, window=window, halo=halo),
        out_shape=(out, out, out),
        grid=(groups,),
        in_specs=[
            pl.BlockSpec(windows.shape, whole),
            pl.BlockSpec(kernel_rows.shape, whole),
            pl.BlockSpec(selector.shape, whole),
            pl.BlockSpec(lane_weights.shape, whole),
            pl.BlockSpec(summer.shape, whole),
            pl.BlockSpec(keep.shape, whole),
            pl.BlockSpec(base.shape, whole),
        ],
        out_specs=(pl.BlockSpec(local, whole),) * 3,
        scratch_shapes=[
            pltpu.VMEM((m_rows, width_n), jnp.float32),
            pltpu.VMEM((m_rows, summer.shape[1]), jnp.float32),
        ],
        compiler_params=pltpu.CompilerParams(vmem_limit_bytes=48 * 1024 * 1024),
        cost_estimate=pl.CostEstimate(
            flops=2 * m_rows * ambit * window * width_n,
            transcendentals=0,
            bytes_accessed=windows.size * 4 + kernel_rows.size * 2,
        ),
    )(windows, kernel_rows, selector, lane_weights, summer, keep, base)


MASK_FROM = ((-1, 0), (1, 0), (-2, 0), (2, 0))
QUENCH_FROM = ((-1, -1), (-1, 0), (-1, 1), (0, -1), (0, 1), (1, -1), (1, 0), (1, 1))


def exchange_kernel(mask_ref, q_ref, mask_out, q_out, mask_slots, q_slots, send_sems, recv_sems):
    tile = lax.axis_index("tile")
    kern = lax.axis_index("kern")
    tiles = lax.axis_size("tile")
    kerns = lax.axis_size("kern")

    def exists(dt, dq):
        return (tile + dt >= 0) & (tile + dt < tiles) & (kern + dq >= 0) & (kern + dq < kerns)

    def device(dt, dq):
        return {"tile": tile + dt, "kern": kern + dq}

    barrier = pltpu.get_barrier_semaphore()
    partners = sorted(set(MASK_FROM) | set(QUENCH_FROM))
    count = jnp.int32(0)
    for dt, dq in partners:
        here = exists(dt, dq)

        @pl.when(here)
        def _():
            pl.semaphore_signal(
                barrier, 1, device_id=device(dt, dq), device_id_type=pl.DeviceIdType.MESH
            )

        count = count + here.astype(jnp.int32)
    pl.semaphore_wait(barrier, count)

    def rows_for(source, dt, whole):
        height = source.shape[0]
        if abs(dt) == 1 and whole:
            return 0, height
        return (height - HALO, HALO) if dt < 0 else (0, HALO)

    plan = [(mask_ref, mask_slots, slot, offset, True) for slot, offset in enumerate(MASK_FROM)]
    plan += [(q_ref, q_slots, slot, offset, False) for slot, offset in enumerate(QUENCH_FROM)]
    copies = []
    for index, (source, slots, slot, (dt, dq), whole) in enumerate(plan):
        if dt == 0:
            first, count = 0, source.shape[0]
        else:
            first, count = rows_for(source, dt, whole)
        copy = pltpu.make_async_remote_copy(
            src_ref=source.at[pl.ds(first, count)],
            dst_ref=slots.at[slot, pl.ds(first, count)],
            send_sem=send_sems.at[index],
            recv_sem=recv_sems.at[index],
            device_id=device(-dt, -dq),
            device_id_type=pl.DeviceIdType.MESH,
        )

        @pl.when(exists(-dt, -dq))
        def _():
            copy.start()

        copies.append((copy, first, count))
    for (copy, first, count), (source, slots, slot, (dt, dq), whole) in zip(copies, plan):

        @pl.when(exists(-dt, -dq))
        def _():
            copy.wait_send()

        out = mask_out if slots is mask_slots else q_out
        here = exists(dt, dq)

        @pl.when(here)
        def _():
            copy.wait_recv()
            out[slot, pl.ds(first, count)] = slots[slot, pl.ds(first, count)]

        @pl.when(jnp.logical_not(here))
        def _():
            out[slot] = jnp.zeros(out.shape[1:], out.dtype)


def exchange(mask, quencher):
    mask_shape = (len(MASK_FROM),) + mask.shape
    q_shape = (len(QUENCH_FROM),) + quencher.shape
    vmem = pl.BlockSpec(memory_space=pltpu.VMEM)
    return pl.pallas_call(
        exchange_kernel,
        out_shape=(
            jax.ShapeDtypeStruct(mask_shape, mask.dtype),
            jax.ShapeDtypeStruct(q_shape, quencher.dtype),
        ),
        in_specs=[vmem, vmem],
        out_specs=(vmem, vmem),
        scratch_shapes=[
            pltpu.VMEM(mask_shape, mask.dtype),
            pltpu.VMEM(q_shape, quencher.dtype),
            pltpu.SemaphoreType.DMA((len(MASK_FROM) + len(QUENCH_FROM),)),
            pltpu.SemaphoreType.DMA((len(MASK_FROM) + len(QUENCH_FROM),)),
        ],
        compiler_params=pltpu.CompilerParams(collective_id=0, has_side_effects=True),
    )(mask, quencher)


def fused_kernel(
    mask_ref, q_ref, k_ref, sel_ref, w_ref, s_ref, keep_ref,
    i_out, a_out, b_out,
    mask_slots, q_slots, send_sems, recv_sems, taps_ref, win_ref, acc_ref, red_ref,
    *, pairs, window, halo,
):
    tile = lax.axis_index("tile")
    kern = lax.axis_index("kern")
    tiles = lax.axis_size("tile")
    kerns = lax.axis_size("kern")
    local_rows, local_cols = q_ref.shape
    out_rows = local_rows + 2 * halo
    out_cols = local_cols + 2 * halo
    width = sel_ref.shape[1] // window
    lanes = keep_ref.shape[1]
    groups = k_ref.shape[0] // (TAP_GROUP * pairs)
    span = TAP_GROUP * window

    def exists(dt, dq):
        return (tile + dt >= 0) & (tile + dt < tiles) & (kern + dq >= 0) & (kern + dq < kerns)

    def device(dt, dq):
        return {"tile": tile + dt, "kern": kern + dq}

    barrier = pltpu.get_barrier_semaphore()
    partners = sorted(set(MASK_FROM) | set(QUENCH_FROM))
    count = jnp.int32(0)
    for dt, dq in partners:
        here = exists(dt, dq)

        @pl.when(here)
        def _():
            pl.semaphore_signal(
                barrier, 1, device_id=device(dt, dq), device_id_type=pl.DeviceIdType.MESH
            )

        count = count + here.astype(jnp.int32)
    pl.semaphore_wait(barrier, count)

    def rows_for(source, dt, whole):
        height = source.shape[0]
        if dt == 0 or (abs(dt) == 1 and whole):
            return 0, height
        return (height - HALO, HALO) if dt < 0 else (0, HALO)

    plan = [(mask_ref, mask_slots, slot, offset, True) for slot, offset in enumerate(MASK_FROM)]
    plan += [(q_ref, q_slots, slot, offset, False) for slot, offset in enumerate(QUENCH_FROM)]
    copies = []
    for index, (source, slots, slot, (dt, dq), whole) in enumerate(plan):
        first, rows = rows_for(source, dt, whole)
        copy = pltpu.make_async_remote_copy(
            src_ref=source.at[pl.ds(first, rows)],
            dst_ref=slots.at[slot, pl.ds(first, rows)],
            send_sem=send_sems.at[index],
            recv_sem=recv_sems.at[index],
            device_id=device(-dt, -dq),
            device_id_type=pl.DeviceIdType.MESH,
        )

        @pl.when(exists(-dt, -dq))
        def _():
            copy.start()

        copies.append(copy)

    def build(group, carry):
        first = pl.multiple_of(group * TAP_GROUP * pairs, TAP_GROUP * pairs)
        product = jnp.dot(
            k_ref[pl.ds(first, TAP_GROUP * pairs), :], sel_ref[...],
            preferred_element_type=jnp.float32,
        ).astype(jnp.bfloat16)
        columns = [
            jnp.concatenate(
                [
                    product[j * pairs : (j + 1) * pairs, o * window : (o + 1) * window]
                    for o in range(width)
                ],
                axis=0,
            )
            for j in range(TAP_GROUP)
        ]
        taps_ref[:, pl.ds(pl.multiple_of(group * span, span), span)] = jnp.concatenate(
            columns, axis=1
        )
        return carry

    lax.fori_loop(0, groups, build, 0)

    for copy, (source, slots, slot, (dt, dq), whole) in zip(copies, plan):

        @pl.when(exists(-dt, -dq))
        def _():
            copy.wait_send()

        @pl.when(exists(dt, dq))
        def _():
            copy.wait_recv()

    def slot_rows(slots, slot, first, rows):
        dt, dq = (MASK_FROM if slots is mask_slots else QUENCH_FROM)[slot]
        value = slots[slot, pl.ds(first, rows), :]
        return jnp.where(exists(dt, dq), value, jnp.zeros_like(value))

    reach = HALO
    rows = jnp.concatenate(
        [
            slot_rows(mask_slots, 2, local_rows - reach, reach),
            slot_rows(mask_slots, 0, 0, local_rows),
            mask_ref[...],
            slot_rows(mask_slots, 1, 0, local_rows),
            slot_rows(mask_slots, 3, 0, reach),
        ],
        axis=0,
    ).astype(jnp.float32)
    total = rows.shape[1] + 128
    rows = jnp.concatenate([rows, jnp.zeros((rows.shape[0], 128), jnp.float32)], axis=1)
    lead = (win_ref.shape[0] // BLOCKS - out_rows) // 2 + halo
    for block in range(BLOCKS):
        start = kern * local_cols - lead + width * block
        part = pltpu.roll(rows, lax.rem(total - start, total), 1)[:, :window]
        win_ref[pl.ds(block, rows.shape[0], stride=BLOCKS), :] = part

    def band(left, middle, right):
        lane = lax.broadcasted_iota(jnp.int32, (middle.shape[0], lanes), 1)

        def widen(value):
            return jnp.concatenate(
                [value, jnp.zeros((value.shape[0], lanes - value.shape[1]), value.dtype)], axis=1
            )

        outer = lanes - (local_cols - halo)
        return jnp.where(
            lane < halo,
            pltpu.roll(widen(left), outer, 1),
            jnp.where(
                lane < halo + local_cols,
                pltpu.roll(widen(middle), halo, 1),
                jnp.where(lane < out_cols, pltpu.roll(widen(right), outer, 1), 0.0),
            ),
        )

    low = local_rows - halo
    base = jnp.concatenate(
        [
            band(*(slot_rows(q_slots, s, low, halo) for s in (0, 1, 2))),
            band(slot_rows(q_slots, 3, 0, local_rows), q_ref[...], slot_rows(q_slots, 4, 0, local_rows)),
            band(*(slot_rows(q_slots, s, 0, halo) for s in (5, 6, 7))),
        ],
        axis=0,
    )

    acc_ref[...] = jnp.zeros_like(acc_ref)

    def accumulate(group, carry):
        pieces = []
        for offset in range(TAP_GROUP):
            start = pl.multiple_of((group * TAP_GROUP + offset) * BLOCKS, BLOCKS)
            pieces.append(win_ref[pl.ds(start, out_rows * BLOCKS), :].astype(jnp.bfloat16))
        left = jnp.concatenate(pieces, axis=1)
        right = taps_ref[:, pl.ds(pl.multiple_of(group * span, span), span)]
        acc_ref[...] += lax.dot_general(
            left, right, (((1,), (1,)), ((), ())), preferred_element_type=jnp.float32
        )
        return carry

    lax.fori_loop(0, groups, accumulate, 0)

    field = acc_ref[...]
    weighted = field * field * w_ref[...]
    red_ref[...] = jnp.dot(
        weighted, s_ref[...], precision=lax.Precision.HIGHEST,
        preferred_element_type=jnp.float32,
    )
    intensity = jnp.zeros((out_rows, lanes), jnp.float32)
    for block in range(BLOCKS):
        part = red_ref[pl.ds(block, out_rows, stride=BLOCKS), :]
        part = jnp.concatenate([part, jnp.zeros_like(part)], axis=1)
        intensity = intensity + pltpu.roll(part, width * block, 1) if block else part
    keep = keep_ref[...] > 0.5
    acid = jnp.where(keep, 1.0 - jnp.exp(-EXPOSURE * intensity), 0.0)
    for _ in range(STEPS):
        quenched = QUENCH_RATE * acid * base
        acid_next = acid + DIFFUSE_ACID * spread_of(acid) - quenched
        base_next = base + DIFFUSE_BASE * spread_of(base) - quenched
        acid = jnp.where(keep, acid_next, 0.0)
        base = jnp.where(keep, base_next, 0.0)
    for out, value in ((i_out, intensity), (a_out, acid), (b_out, base)):
        out[...] = pltpu.roll(value, lanes - halo, 1)[halo : halo + local_rows, :local_cols]


def on_device(mask, kernels, socs_weights, quencher):
    ambit = kernels.shape[2]
    half_ambit = ambit // 2
    kern_count = lax.axis_size("kern")
    kern_index = lax.axis_index("kern")
    tile_index = lax.axis_index("tile")
    local_rows = mask.shape[0]
    local_cols = quencher.shape[1]
    halo = HALO
    out_rows = local_rows + 2 * halo
    out_cols = local_cols + 2 * halo
    width = out_cols // BLOCKS
    window = 128
    lanes = 2 * window
    window_rows = out_rows + ambit

    pairs = kernels.shape[0] * kernels.shape[1]
    kernel_rows = jnp.transpose(kernels, (2, 0, 1, 3)).reshape(ambit * pairs, ambit)
    selector = toeplitz_selector(ambit, window, width)
    lane_weights = jnp.broadcast_to(
        socs_weights[None, :, None], (width, kernels.shape[0], kernels.shape[1])
    ).reshape(1, width * pairs)
    summer = (
        lax.iota(jnp.int32, width * pairs)[:, None] // pairs == lax.iota(jnp.int32, window)[None, :]
    ).astype(jnp.float32)
    rows_total = local_rows * lax.axis_size("tile")
    cols_total = local_cols * kern_count
    r = tile_index * local_rows - halo + lax.broadcasted_iota(jnp.int32, (out_rows, lanes), 0)
    c = kern_index * local_cols - halo + lax.broadcasted_iota(jnp.int32, (out_rows, lanes), 1)
    keep = (r >= 0) & (r < rows_total) & (c >= 0) & (c < cols_total)
    keep = (keep & (c < kern_index * local_cols - halo + out_cols)).astype(jnp.float32)

    vmem = pl.BlockSpec(memory_space=pltpu.VMEM)
    out = jax.ShapeDtypeStruct((local_rows, local_cols), jnp.float32)
    copies = len(MASK_FROM) + len(QUENCH_FROM)
    m_rows = out_rows * BLOCKS
    return pl.pallas_call(
        functools.partial(fused_kernel, pairs=pairs, window=window, halo=halo),
        out_shape=(out, out, out),
        in_specs=[vmem] * 7,
        out_specs=(vmem, vmem, vmem),
        scratch_shapes=[
            pltpu.VMEM((len(MASK_FROM),) + mask.shape, mask.dtype),
            pltpu.VMEM((len(QUENCH_FROM),) + quencher.shape, quencher.dtype),
            pltpu.SemaphoreType.DMA((copies,)),
            pltpu.SemaphoreType.DMA((copies,)),
            pltpu.VMEM((width * pairs, ambit * window), jnp.bfloat16),
            pltpu.VMEM((window_rows * BLOCKS, window), jnp.float32),
            pltpu.VMEM((m_rows, width * pairs), jnp.float32),
            pltpu.VMEM((m_rows, window), jnp.float32),
        ],
        compiler_params=pltpu.CompilerParams(
            collective_id=0, has_side_effects=True, vmem_limit_bytes=56 * 1024 * 1024
        ),
        cost_estimate=pl.CostEstimate(
            flops=2 * m_rows * ambit * window * width * pairs,
            transcendentals=0,
            bytes_accessed=kernel_rows.size * 2 + mask.size * 4 * 5,
        ),
    )(mask, quencher, kernel_rows, selector, lane_weights, summer, keep)


def solution(mesh):
    placed = (P("tile", None), P(), P(), P("tile", "kern"))
    return jax.shard_map(
        on_device,
        mesh=mesh,
        in_specs=placed,
        out_specs=(P("tile", "kern"), P("tile", "kern"), P("tile", "kern")),
        check_vma=False,
    )
```

```python
import functools

import jax
import jax.numpy as jnp
from jax import lax
from jax.experimental import pallas as pl
from jax.experimental.pallas import tpu as pltpu
from jax.sharding import PartitionSpec as P

STEPS = 8


DIFFUSE_ACID = 0.2
DIFFUSE_BASE = 0.1
QUENCH_RATE = 0.5
EXPOSURE = 0.35

BLOCKS = 8
HALO = STEPS
TAP_GROUP = 8


def shifted(value, axis, steps):
    count = lax.axis_size(axis)
    leading, last = (max(0, -steps), min(count, count - steps))
    return lax.ppermute(value, axis, [(source, source + steps) for source in range(leading, last)])


def padded_2(block, sides, width):
    for axis, dim in sides:
        count = lax.axis_size(axis)
        forward = [(i, i + 1) for i in range(count - 1)]
        backward = [(target, source) for source, target in forward]
        low = lax.ppermute(
            lax.slice_in_dim(block, block.shape[dim] - width, None, axis=dim), axis, forward
        )
        high = lax.ppermute(lax.slice_in_dim(block, 0, width, axis=dim), axis, backward)
        block = jnp.concatenate([low, block, high], axis=dim)
    return block


def react(padded):
    middle = padded[:, 1:-1, 1:-1]
    spread = (
        padded[:, :-2, 1:-1]
        + padded[:, 2:, 1:-1]
        + padded[:, 1:-1, :-2]
        + padded[:, 1:-1, 2:]
        - 4.0 * middle
    )
    quenched = QUENCH_RATE * middle[0] * middle[1]
    acid_next = middle[0] + DIFFUSE_ACID * spread[0] - quenched
    base_next = middle[1] + DIFFUSE_BASE * spread[1] - quenched
    return jnp.stack([acid_next, base_next], axis=0)


def toeplitz_selector(ambit, window, width):
    tap_ids = lax.iota(jnp.int32, ambit)
    input_ids = lax.iota(jnp.int32, window)
    output_ids = lax.iota(jnp.int32, width)
    offsets = input_ids[None, None, :] - output_ids[None, :, None]
    selector = (offsets == tap_ids[:, None, None]).astype(jnp.bfloat16)
    return selector.reshape(ambit, width * window)


def spread_of(value):
    rows, lanes = value.shape
    up = pltpu.roll(value, 1, 0)
    down = pltpu.roll(value, rows - 1, 0)
    left = pltpu.roll(value, 1, 1)
    right = pltpu.roll(value, lanes - 1, 1)
    return up + down + left + right - 4.0 * value


def field_kernel(
    x_ref, k_ref, sel_ref, w_ref, s_ref, keep_ref, base_ref,
    i_out, a_out, b_out, acc_ref, red_ref, *, out_rows, pairs, window, halo,
):
    step = pl.program_id(0)
    width = sel_ref.shape[1] // window

    @pl.when(step == 0)
    def _():
        acc_ref[...] = jnp.zeros_like(acc_ref)

    kernel_rows = k_ref[pl.ds(pl.multiple_of(step * TAP_GROUP * pairs, pairs), TAP_GROUP * pairs), :]
    taps = jnp.dot(kernel_rows, sel_ref[...], preferred_element_type=jnp.float32).astype(
        jnp.bfloat16
    )
    pieces = []
    columns = []
    for offset in range(TAP_GROUP):
        tap = step * TAP_GROUP + offset
        start = pl.multiple_of(tap * BLOCKS, BLOCKS)
        pieces.append(x_ref[pl.ds(start, out_rows * BLOCKS), :].astype(jnp.bfloat16))
        columns.append(
            jnp.concatenate(
                [
                    taps[offset * pairs : (offset + 1) * pairs, o * window : (o + 1) * window]
                    for o in range(width)
                ],
                axis=0,
            )
        )
    left = jnp.concatenate(pieces, axis=1)
    right = jnp.concatenate(columns, axis=1)
    acc_ref[...] += lax.dot_general(
        left, right, (((1,), (1,)), ((), ())), preferred_element_type=jnp.float32
    )

    @pl.when(step == pl.num_programs(0) - 1)
    def _():
        lanes = keep_ref.shape[1]
        field = acc_ref[...]
        weighted = field * field * w_ref[...]
        red_ref[...] = jnp.dot(
            weighted, s_ref[...], precision=lax.Precision.HIGHEST,
            preferred_element_type=jnp.float32,
        )
        intensity = jnp.zeros((out_rows, lanes), jnp.float32)
        for block in range(BLOCKS):
            part = red_ref[pl.ds(block, out_rows, stride=BLOCKS), :]
            part = jnp.concatenate([part, jnp.zeros_like(part)], axis=1)
            intensity = intensity + pltpu.roll(part, width * block, 1) if block else part
        keep = keep_ref[...] > 0.5
        acid = jnp.where(keep, 1.0 - jnp.exp(-EXPOSURE * intensity), 0.0)
        base = base_ref[...]
        for _ in range(STEPS):
            quenched = QUENCH_RATE * acid * base
            acid_next = acid + DIFFUSE_ACID * spread_of(acid) - quenched
            base_next = base + DIFFUSE_BASE * spread_of(base) - quenched
            acid = jnp.where(keep, acid_next, 0.0)
            base = jnp.where(keep, base_next, 0.0)
        rows, cols = i_out.shape
        for out, value in ((i_out, intensity), (a_out, acid), (b_out, base)):
            out[...] = pltpu.roll(value, lanes - halo, 1)[halo : halo + rows, :cols]


def resist_of(windows, kernel_rows, selector, lane_weights, summer, keep, base, out_rows, ambit, halo, local):
    window = windows.shape[1]
    width = selector.shape[1] // window
    pairs = kernel_rows.shape[0] // ambit
    width_n = pairs * width
    m_rows = out_rows * BLOCKS
    groups = ambit // TAP_GROUP
    whole = lambda g: (0, 0)
    out = jax.ShapeDtypeStruct(local, jnp.float32)

    return pl.pallas_call(
        functools.partial(field_kernel, out_rows=out_rows, pairs=pairs, window=window, halo=halo),
        out_shape=(out, out, out),
        grid=(groups,),
        in_specs=[
            pl.BlockSpec(windows.shape, whole),
            pl.BlockSpec(kernel_rows.shape, whole),
            pl.BlockSpec(selector.shape, whole),
            pl.BlockSpec(lane_weights.shape, whole),
            pl.BlockSpec(summer.shape, whole),
            pl.BlockSpec(keep.shape, whole),
            pl.BlockSpec(base.shape, whole),
        ],
        out_specs=(pl.BlockSpec(local, whole),) * 3,
        scratch_shapes=[
            pltpu.VMEM((m_rows, width_n), jnp.float32),
            pltpu.VMEM((m_rows, summer.shape[1]), jnp.float32),
        ],
        compiler_params=pltpu.CompilerParams(vmem_limit_bytes=48 * 1024 * 1024),
        cost_estimate=pl.CostEstimate(
            flops=2 * m_rows * ambit * window * width_n,
            transcendentals=0,
            bytes_accessed=windows.size * 4 + kernel_rows.size * 2,
        ),
    )(windows, kernel_rows, selector, lane_weights, summer, keep, base)


MASK_FROM = ((-1, 0), (1, 0), (-2, 0), (2, 0))
QUENCH_FROM = ((-1, -1), (-1, 0), (-1, 1), (0, -1), (0, 1), (1, -1), (1, 0), (1, 1))


def exchange_kernel(mask_ref, q_ref, mask_out, q_out, mask_slots, q_slots, send_sems, recv_sems):
    tile = lax.axis_index("tile")
    kern = lax.axis_index("kern")
    tiles = lax.axis_size("tile")
    kerns = lax.axis_size("kern")

    def exists(dt, dq):
        return (tile + dt >= 0) & (tile + dt < tiles) & (kern + dq >= 0) & (kern + dq < kerns)

    def device(dt, dq):
        return {"tile": tile + dt, "kern": kern + dq}

    barrier = pltpu.get_barrier_semaphore()
    partners = sorted(set(MASK_FROM) | set(QUENCH_FROM))
    count = jnp.int32(0)
    for dt, dq in partners:
        here = exists(dt, dq)

        @pl.when(here)
        def _():
            pl.semaphore_signal(
                barrier, 1, device_id=device(dt, dq), device_id_type=pl.DeviceIdType.MESH
            )

        count = count + here.astype(jnp.int32)
    pl.semaphore_wait(barrier, count)

    def rows_for(source, dt, whole):
        height = source.shape[0]
        if abs(dt) == 1 and whole:
            return 0, height
        return (height - HALO, HALO) if dt < 0 else (0, HALO)

    plan = [(mask_ref, mask_slots, slot, offset, True) for slot, offset in enumerate(MASK_FROM)]
    plan += [(q_ref, q_slots, slot, offset, False) for slot, offset in enumerate(QUENCH_FROM)]
    copies = []
    for index, (source, slots, slot, (dt, dq), whole) in enumerate(plan):
        if dt == 0:
            first, count = 0, source.shape[0]
        else:
            first, count = rows_for(source, dt, whole)
        copy = pltpu.make_async_remote_copy(
            src_ref=source.at[pl.ds(first, count)],
            dst_ref=slots.at[slot, pl.ds(first, count)],
            send_sem=send_sems.at[index],
            recv_sem=recv_sems.at[index],
            device_id=device(-dt, -dq),
            device_id_type=pl.DeviceIdType.MESH,
        )

        @pl.when(exists(-dt, -dq))
        def _():
            copy.start()

        copies.append((copy, first, count))
    for (copy, first, count), (source, slots, slot, (dt, dq), whole) in zip(copies, plan):

        @pl.when(exists(-dt, -dq))
        def _():
            copy.wait_send()

        out = mask_out if slots is mask_slots else q_out
        here = exists(dt, dq)

        @pl.when(here)
        def _():
            copy.wait_recv()
            out[slot, pl.ds(first, count)] = slots[slot, pl.ds(first, count)]

        @pl.when(jnp.logical_not(here))
        def _():
            out[slot] = jnp.zeros(out.shape[1:], out.dtype)


def exchange(mask, quencher):
    mask_shape = (len(MASK_FROM),) + mask.shape
    q_shape = (len(QUENCH_FROM),) + quencher.shape
    vmem = pl.BlockSpec(memory_space=pltpu.VMEM)
    return pl.pallas_call(
        exchange_kernel,
        out_shape=(
            jax.ShapeDtypeStruct(mask_shape, mask.dtype),
            jax.ShapeDtypeStruct(q_shape, quencher.dtype),
        ),
        in_specs=[vmem, vmem],
        out_specs=(vmem, vmem),
        scratch_shapes=[
            pltpu.VMEM(mask_shape, mask.dtype),
            pltpu.VMEM(q_shape, quencher.dtype),
            pltpu.SemaphoreType.DMA((len(MASK_FROM) + len(QUENCH_FROM),)),
            pltpu.SemaphoreType.DMA((len(MASK_FROM) + len(QUENCH_FROM),)),
        ],
        compiler_params=pltpu.CompilerParams(collective_id=0, has_side_effects=True),
    )(mask, quencher)


def fused_kernel(
    mask_ref, q_ref, k_ref, w_smem,
    i_out, a_out, b_out,
    mask_slots, q_slots, send_sems, recv_sems, taps_ref, win_ref, acc_ref, red_ref,
    *, pairs, window, halo, width,
):
    tile = lax.axis_index("tile")
    kern = lax.axis_index("kern")
    tiles = lax.axis_size("tile")
    kerns = lax.axis_size("kern")
    local_rows, local_cols = q_ref.shape
    out_rows = local_rows + 2 * halo
    out_cols = local_cols + 2 * halo
    lanes = 2 * window
    ambit = k_ref.shape[1]
    groups = k_ref.shape[0] // (TAP_GROUP * pairs)
    span = TAP_GROUP * window
    width_n = width * pairs

    def exists(dt, dq):
        return (tile + dt >= 0) & (tile + dt < tiles) & (kern + dq >= 0) & (kern + dq < kerns)

    def device(dt, dq):
        return {"tile": tile + dt, "kern": kern + dq}

    barrier = pltpu.get_barrier_semaphore()
    partners = sorted(set(MASK_FROM) | set(QUENCH_FROM))
    count = jnp.int32(0)
    for dt, dq in partners:
        here = exists(dt, dq)

        @pl.when(here)
        def _():
            pl.semaphore_signal(
                barrier, 1, device_id=device(dt, dq), device_id_type=pl.DeviceIdType.MESH
            )

        count = count + here.astype(jnp.int32)
    pl.semaphore_wait(barrier, count)

    def rows_for(source, dt, whole):
        height = source.shape[0]
        if dt == 0 or (abs(dt) == 1 and whole):
            return 0, height
        return (height - HALO, HALO) if dt < 0 else (0, HALO)

    plan = [(mask_ref, mask_slots, slot, offset, True) for slot, offset in enumerate(MASK_FROM)]
    plan += [(q_ref, q_slots, slot, offset, False) for slot, offset in enumerate(QUENCH_FROM)]
    copies = []
    for index, (source, slots, slot, (dt, dq), whole) in enumerate(plan):
        first, rows = rows_for(source, dt, whole)
        copy = pltpu.make_async_remote_copy(
            src_ref=source.at[pl.ds(first, rows)],
            dst_ref=slots.at[slot, pl.ds(first, rows)],
            send_sem=send_sems.at[index],
            recv_sem=recv_sems.at[index],
            device_id=device(-dt, -dq),
            device_id_type=pl.DeviceIdType.MESH,
        )

        @pl.when(exists(-dt, -dq))
        def _():
            copy.start()

        copies.append(copy)

    sel_lane = lax.broadcasted_iota(jnp.int32, (ambit, width * window), 1)
    sel_row = lax.broadcasted_iota(jnp.int32, (ambit, width * window), 0)
    selector = (sel_lane % window - sel_lane // window == sel_row).astype(jnp.bfloat16)

    def build(group, carry):
        first = pl.multiple_of(group * TAP_GROUP * pairs, TAP_GROUP * pairs)
        product = jnp.dot(
            k_ref[pl.ds(first, TAP_GROUP * pairs), :], selector,
            preferred_element_type=jnp.float32,
        ).astype(jnp.bfloat16)
        columns = [
            jnp.concatenate(
                [
                    product[j * pairs : (j + 1) * pairs, o * window : (o + 1) * window]
                    for o in range(width)
                ],
                axis=0,
            )
            for j in range(TAP_GROUP)
        ]
        taps_ref[:, pl.ds(pl.multiple_of(group * span, span), span)] = jnp.concatenate(
            columns, axis=1
        )
        return carry

    lax.fori_loop(0, groups, build, 0)

    for copy, (source, slots, slot, (dt, dq), whole) in zip(copies, plan):

        @pl.when(exists(-dt, -dq))
        def _():
            copy.wait_send()

        @pl.when(exists(dt, dq))
        def _():
            copy.wait_recv()

    def slot_rows(slots, slot, first, rows):
        dt, dq = (MASK_FROM if slots is mask_slots else QUENCH_FROM)[slot]
        value = slots[slot, pl.ds(first, rows), :]
        return jnp.where(exists(dt, dq), value, jnp.zeros_like(value))

    reach = HALO
    rows = jnp.concatenate(
        [
            slot_rows(mask_slots, 2, local_rows - reach, reach),
            slot_rows(mask_slots, 0, 0, local_rows),
            mask_ref[...],
            slot_rows(mask_slots, 1, 0, local_rows),
            slot_rows(mask_slots, 3, 0, reach),
        ],
        axis=0,
    ).astype(jnp.float32)
    total = rows.shape[1] + 128
    rows = jnp.concatenate([rows, jnp.zeros((rows.shape[0], 128), jnp.float32)], axis=1)
    lead = (win_ref.shape[0] // BLOCKS - out_rows) // 2 + halo
    for block in range(BLOCKS):
        start = kern * local_cols - lead + width * block
        part = pltpu.roll(rows, lax.rem(total - start, total), 1)[:, :window]
        win_ref[pl.ds(block, rows.shape[0], stride=BLOCKS), :] = part

    def band(left, middle, right):
        lane = lax.broadcasted_iota(jnp.int32, (middle.shape[0], lanes), 1)

        def widen(value):
            return jnp.concatenate(
                [value, jnp.zeros((value.shape[0], lanes - value.shape[1]), value.dtype)], axis=1
            )

        outer = lanes - (local_cols - halo)
        return jnp.where(
            lane < halo,
            pltpu.roll(widen(left), outer, 1),
            jnp.where(
                lane < halo + local_cols,
                pltpu.roll(widen(middle), halo, 1),
                jnp.where(lane < out_cols, pltpu.roll(widen(right), outer, 1), 0.0),
            ),
        )

    low = local_rows - halo
    base = jnp.concatenate(
        [
            band(*(slot_rows(q_slots, s, low, halo) for s in (0, 1, 2))),
            band(slot_rows(q_slots, 3, 0, local_rows), q_ref[...], slot_rows(q_slots, 4, 0, local_rows)),
            band(*(slot_rows(q_slots, s, 0, halo) for s in (5, 6, 7))),
        ],
        axis=0,
    )

    acc_ref[...] = jnp.zeros_like(acc_ref)

    def accumulate(group, carry):
        pieces = []
        for offset in range(TAP_GROUP):
            start = pl.multiple_of((group * TAP_GROUP + offset) * BLOCKS, BLOCKS)
            pieces.append(win_ref[pl.ds(start, out_rows * BLOCKS), :].astype(jnp.bfloat16))
        left = jnp.concatenate(pieces, axis=1)
        right = taps_ref[:, pl.ds(pl.multiple_of(group * span, span), span)]
        acc_ref[...] += lax.dot_general(
            left, right, (((1,), (1,)), ((), ())), preferred_element_type=jnp.float32
        )
        return carry

    lax.fori_loop(0, groups, accumulate, 0)

    kernel_of_lane = lax.broadcasted_iota(jnp.int32, (1, width_n), 1) % pairs // 2
    lane_weights = jnp.zeros((1, width_n), jnp.float32)
    for k in range(pairs // 2):
        lane_weights = jnp.where(kernel_of_lane == k, w_smem[k], lane_weights)
    summer = (
        lax.broadcasted_iota(jnp.int32, (width_n, window), 0) // pairs
        == lax.broadcasted_iota(jnp.int32, (width_n, window), 1)
    ).astype(jnp.float32)
    field = acc_ref[...]
    weighted = field * field * lane_weights
    red_ref[...] = jnp.dot(
        weighted, summer, precision=lax.Precision.HIGHEST,
        preferred_element_type=jnp.float32,
    )
    intensity = jnp.zeros((out_rows, lanes), jnp.float32)
    for block in range(BLOCKS):
        part = red_ref[pl.ds(block, out_rows, stride=BLOCKS), :]
        part = jnp.concatenate([part, jnp.zeros_like(part)], axis=1)
        intensity = intensity + pltpu.roll(part, width * block, 1) if block else part
    r = tile * local_rows - halo + lax.broadcasted_iota(jnp.int32, (out_rows, lanes), 0)
    c = kern * local_cols - halo + lax.broadcasted_iota(jnp.int32, (out_rows, lanes), 1)
    keep = (r >= 0) & (r < tiles * local_rows) & (c >= 0) & (c < kerns * local_cols)
    keep = keep & (c < kern * local_cols - halo + out_cols)
    acid = jnp.where(keep, 1.0 - jnp.exp(-EXPOSURE * intensity), 0.0)
    for _ in range(STEPS):
        quenched = QUENCH_RATE * acid * base
        acid_next = acid + DIFFUSE_ACID * spread_of(acid) - quenched
        base_next = base + DIFFUSE_BASE * spread_of(base) - quenched
        acid = jnp.where(keep, acid_next, 0.0)
        base = jnp.where(keep, base_next, 0.0)
    for out, value in ((i_out, intensity), (a_out, acid), (b_out, base)):
        out[...] = pltpu.roll(value, lanes - halo, 1)[halo : halo + local_rows, :local_cols]


def on_device(mask, kernels, socs_weights, quencher):
    ambit = kernels.shape[2]
    half_ambit = ambit // 2
    kern_count = lax.axis_size("kern")
    kern_index = lax.axis_index("kern")
    tile_index = lax.axis_index("tile")
    local_rows = mask.shape[0]
    local_cols = quencher.shape[1]
    halo = HALO
    out_rows = local_rows + 2 * halo
    out_cols = local_cols + 2 * halo
    width = out_cols // BLOCKS
    window = 128
    lanes = 2 * window
    window_rows = out_rows + ambit

    pairs = kernels.shape[0] * kernels.shape[1]
    kernel_rows = jnp.transpose(kernels, (2, 0, 1, 3)).reshape(ambit * pairs, ambit)

    vmem = pl.BlockSpec(memory_space=pltpu.VMEM)
    out = jax.ShapeDtypeStruct((local_rows, local_cols), jnp.float32)
    copies = len(MASK_FROM) + len(QUENCH_FROM)
    m_rows = out_rows * BLOCKS
    return pl.pallas_call(
        functools.partial(fused_kernel, pairs=pairs, window=window, halo=halo, width=width),
        out_shape=(out, out, out),
        in_specs=[vmem] * 3 + [pl.BlockSpec(memory_space=pltpu.SMEM)],
        out_specs=(vmem, vmem, vmem),
        scratch_shapes=[
            pltpu.VMEM((len(MASK_FROM),) + mask.shape, mask.dtype),
            pltpu.VMEM((len(QUENCH_FROM),) + quencher.shape, quencher.dtype),
            pltpu.SemaphoreType.DMA((copies,)),
            pltpu.SemaphoreType.DMA((copies,)),
            pltpu.VMEM((width * pairs, ambit * window), jnp.bfloat16),
            pltpu.VMEM((window_rows * BLOCKS, window), jnp.float32),
            pltpu.VMEM((m_rows, width * pairs), jnp.float32),
            pltpu.VMEM((m_rows, window), jnp.float32),
        ],
        compiler_params=pltpu.CompilerParams(
            collective_id=0, has_side_effects=True, vmem_limit_bytes=56 * 1024 * 1024
        ),
        cost_estimate=pl.CostEstimate(
            flops=2 * m_rows * ambit * window * width * pairs,
            transcendentals=0,
            bytes_accessed=kernel_rows.size * 2 + mask.size * 4 * 5,
        ),
    )(mask, quencher, kernel_rows, socs_weights)


def solution(mesh):
    placed = (P("tile", None), P(), P(), P("tile", "kern"))
    return jax.shard_map(
        on_device,
        mesh=mesh,
        in_specs=placed,
        out_specs=(P("tile", "kern"), P("tile", "kern"), P("tile", "kern")),
        check_vma=False,
    )
```

```python
import functools

import jax
import jax.numpy as jnp
from jax import lax
from jax.experimental import pallas as pl
from jax.experimental.pallas import tpu as pltpu
from jax.sharding import PartitionSpec as P

STEPS = 8


DIFFUSE_ACID = 0.2
DIFFUSE_BASE = 0.1
QUENCH_RATE = 0.5
EXPOSURE = 0.35

BLOCKS = 8
HALO = STEPS
TAP_GROUP = 8


def shifted(value, axis, steps):
    count = lax.axis_size(axis)
    leading, last = (max(0, -steps), min(count, count - steps))
    return lax.ppermute(value, axis, [(source, source + steps) for source in range(leading, last)])


def padded_2(block, sides, width):
    for axis, dim in sides:
        count = lax.axis_size(axis)
        forward = [(i, i + 1) for i in range(count - 1)]
        backward = [(target, source) for source, target in forward]
        low = lax.ppermute(
            lax.slice_in_dim(block, block.shape[dim] - width, None, axis=dim), axis, forward
        )
        high = lax.ppermute(lax.slice_in_dim(block, 0, width, axis=dim), axis, backward)
        block = jnp.concatenate([low, block, high], axis=dim)
    return block


def react(padded):
    middle = padded[:, 1:-1, 1:-1]
    spread = (
        padded[:, :-2, 1:-1]
        + padded[:, 2:, 1:-1]
        + padded[:, 1:-1, :-2]
        + padded[:, 1:-1, 2:]
        - 4.0 * middle
    )
    quenched = QUENCH_RATE * middle[0] * middle[1]
    acid_next = middle[0] + DIFFUSE_ACID * spread[0] - quenched
    base_next = middle[1] + DIFFUSE_BASE * spread[1] - quenched
    return jnp.stack([acid_next, base_next], axis=0)


def toeplitz_selector(ambit, window, width):
    tap_ids = lax.iota(jnp.int32, ambit)
    input_ids = lax.iota(jnp.int32, window)
    output_ids = lax.iota(jnp.int32, width)
    offsets = input_ids[None, None, :] - output_ids[None, :, None]
    selector = (offsets == tap_ids[:, None, None]).astype(jnp.bfloat16)
    return selector.reshape(ambit, width * window)


def spread_of(value):
    rows, lanes = value.shape
    up = pltpu.roll(value, 1, 0)
    down = pltpu.roll(value, rows - 1, 0)
    left = pltpu.roll(value, 1, 1)
    right = pltpu.roll(value, lanes - 1, 1)
    return up + down + left + right - 4.0 * value


def field_kernel(
    x_ref, k_ref, sel_ref, w_ref, s_ref, keep_ref, base_ref,
    i_out, a_out, b_out, acc_ref, red_ref, *, out_rows, pairs, window, halo,
):
    step = pl.program_id(0)
    width = sel_ref.shape[1] // window

    @pl.when(step == 0)
    def _():
        acc_ref[...] = jnp.zeros_like(acc_ref)

    kernel_rows = k_ref[pl.ds(pl.multiple_of(step * TAP_GROUP * pairs, pairs), TAP_GROUP * pairs), :]
    taps = jnp.dot(kernel_rows, sel_ref[...], preferred_element_type=jnp.float32).astype(
        jnp.bfloat16
    )
    pieces = []
    columns = []
    for offset in range(TAP_GROUP):
        tap = step * TAP_GROUP + offset
        start = pl.multiple_of(tap * BLOCKS, BLOCKS)
        pieces.append(x_ref[pl.ds(start, out_rows * BLOCKS), :].astype(jnp.bfloat16))
        columns.append(
            jnp.concatenate(
                [
                    taps[offset * pairs : (offset + 1) * pairs, o * window : (o + 1) * window]
                    for o in range(width)
                ],
                axis=0,
            )
        )
    left = jnp.concatenate(pieces, axis=1)
    right = jnp.concatenate(columns, axis=1)
    acc_ref[...] += lax.dot_general(
        left, right, (((1,), (1,)), ((), ())), preferred_element_type=jnp.float32
    )

    @pl.when(step == pl.num_programs(0) - 1)
    def _():
        lanes = keep_ref.shape[1]
        field = acc_ref[...]
        weighted = field * field * w_ref[...]
        red_ref[...] = jnp.dot(
            weighted, s_ref[...], precision=lax.Precision.HIGHEST,
            preferred_element_type=jnp.float32,
        )
        intensity = jnp.zeros((out_rows, lanes), jnp.float32)
        for block in range(BLOCKS):
            part = red_ref[pl.ds(block, out_rows, stride=BLOCKS), :]
            part = jnp.concatenate([part, jnp.zeros_like(part)], axis=1)
            intensity = intensity + pltpu.roll(part, width * block, 1) if block else part
        keep = keep_ref[...] > 0.5
        acid = jnp.where(keep, 1.0 - jnp.exp(-EXPOSURE * intensity), 0.0)
        base = base_ref[...]
        for _ in range(STEPS):
            quenched = QUENCH_RATE * acid * base
            acid_next = acid + DIFFUSE_ACID * spread_of(acid) - quenched
            base_next = base + DIFFUSE_BASE * spread_of(base) - quenched
            acid = jnp.where(keep, acid_next, 0.0)
            base = jnp.where(keep, base_next, 0.0)
        rows, cols = i_out.shape
        for out, value in ((i_out, intensity), (a_out, acid), (b_out, base)):
            out[...] = pltpu.roll(value, lanes - halo, 1)[halo : halo + rows, :cols]


def resist_of(windows, kernel_rows, selector, lane_weights, summer, keep, base, out_rows, ambit, halo, local):
    window = windows.shape[1]
    width = selector.shape[1] // window
    pairs = kernel_rows.shape[0] // ambit
    width_n = pairs * width
    m_rows = out_rows * BLOCKS
    groups = ambit // TAP_GROUP
    whole = lambda g: (0, 0)
    out = jax.ShapeDtypeStruct(local, jnp.float32)

    return pl.pallas_call(
        functools.partial(field_kernel, out_rows=out_rows, pairs=pairs, window=window, halo=halo),
        out_shape=(out, out, out),
        grid=(groups,),
        in_specs=[
            pl.BlockSpec(windows.shape, whole),
            pl.BlockSpec(kernel_rows.shape, whole),
            pl.BlockSpec(selector.shape, whole),
            pl.BlockSpec(lane_weights.shape, whole),
            pl.BlockSpec(summer.shape, whole),
            pl.BlockSpec(keep.shape, whole),
            pl.BlockSpec(base.shape, whole),
        ],
        out_specs=(pl.BlockSpec(local, whole),) * 3,
        scratch_shapes=[
            pltpu.VMEM((m_rows, width_n), jnp.float32),
            pltpu.VMEM((m_rows, summer.shape[1]), jnp.float32),
        ],
        compiler_params=pltpu.CompilerParams(vmem_limit_bytes=48 * 1024 * 1024),
        cost_estimate=pl.CostEstimate(
            flops=2 * m_rows * ambit * window * width_n,
            transcendentals=0,
            bytes_accessed=windows.size * 4 + kernel_rows.size * 2,
        ),
    )(windows, kernel_rows, selector, lane_weights, summer, keep, base)


MASK_FROM = ((-1, 0), (1, 0), (-2, 0), (2, 0))
QUENCH_FROM = ((-1, -1), (-1, 0), (-1, 1), (0, -1), (0, 1), (1, -1), (1, 0), (1, 1))


def exchange_kernel(mask_ref, q_ref, mask_out, q_out, mask_slots, q_slots, send_sems, recv_sems):
    tile = lax.axis_index("tile")
    kern = lax.axis_index("kern")
    tiles = lax.axis_size("tile")
    kerns = lax.axis_size("kern")

    def exists(dt, dq):
        return (tile + dt >= 0) & (tile + dt < tiles) & (kern + dq >= 0) & (kern + dq < kerns)

    def device(dt, dq):
        return {"tile": tile + dt, "kern": kern + dq}

    barrier = pltpu.get_barrier_semaphore()
    partners = sorted(set(MASK_FROM) | set(QUENCH_FROM))
    count = jnp.int32(0)
    for dt, dq in partners:
        here = exists(dt, dq)

        @pl.when(here)
        def _():
            pl.semaphore_signal(
                barrier, 1, device_id=device(dt, dq), device_id_type=pl.DeviceIdType.MESH
            )

        count = count + here.astype(jnp.int32)
    pl.semaphore_wait(barrier, count)

    def rows_for(source, dt, whole):
        height = source.shape[0]
        if abs(dt) == 1 and whole:
            return 0, height
        return (height - HALO, HALO) if dt < 0 else (0, HALO)

    plan = [(mask_ref, mask_slots, slot, offset, True) for slot, offset in enumerate(MASK_FROM)]
    plan += [(q_ref, q_slots, slot, offset, False) for slot, offset in enumerate(QUENCH_FROM)]
    copies = []
    for index, (source, slots, slot, (dt, dq), whole) in enumerate(plan):
        if dt == 0:
            first, count = 0, source.shape[0]
        else:
            first, count = rows_for(source, dt, whole)
        copy = pltpu.make_async_remote_copy(
            src_ref=source.at[pl.ds(first, count)],
            dst_ref=slots.at[slot, pl.ds(first, count)],
            send_sem=send_sems.at[index],
            recv_sem=recv_sems.at[index],
            device_id=device(-dt, -dq),
            device_id_type=pl.DeviceIdType.MESH,
        )

        @pl.when(exists(-dt, -dq))
        def _():
            copy.start()

        copies.append((copy, first, count))
    for (copy, first, count), (source, slots, slot, (dt, dq), whole) in zip(copies, plan):

        @pl.when(exists(-dt, -dq))
        def _():
            copy.wait_send()

        out = mask_out if slots is mask_slots else q_out
        here = exists(dt, dq)

        @pl.when(here)
        def _():
            copy.wait_recv()
            out[slot, pl.ds(first, count)] = slots[slot, pl.ds(first, count)]

        @pl.when(jnp.logical_not(here))
        def _():
            out[slot] = jnp.zeros(out.shape[1:], out.dtype)


def exchange(mask, quencher):
    mask_shape = (len(MASK_FROM),) + mask.shape
    q_shape = (len(QUENCH_FROM),) + quencher.shape
    vmem = pl.BlockSpec(memory_space=pltpu.VMEM)
    return pl.pallas_call(
        exchange_kernel,
        out_shape=(
            jax.ShapeDtypeStruct(mask_shape, mask.dtype),
            jax.ShapeDtypeStruct(q_shape, quencher.dtype),
        ),
        in_specs=[vmem, vmem],
        out_specs=(vmem, vmem),
        scratch_shapes=[
            pltpu.VMEM(mask_shape, mask.dtype),
            pltpu.VMEM(q_shape, quencher.dtype),
            pltpu.SemaphoreType.DMA((len(MASK_FROM) + len(QUENCH_FROM),)),
            pltpu.SemaphoreType.DMA((len(MASK_FROM) + len(QUENCH_FROM),)),
        ],
        compiler_params=pltpu.CompilerParams(collective_id=0, has_side_effects=True),
    )(mask, quencher)


def fused_kernel(
    mask_ref, q_ref, k_ref, w_smem,
    i_out, a_out, b_out,
    mask_slots, q_slots, send_sems, recv_sems, taps_ref, win_ref, acc_ref, red_ref, rows_ref,
    *, pairs, window, halo, width,
):
    tile = lax.axis_index("tile")
    kern = lax.axis_index("kern")
    tiles = lax.axis_size("tile")
    kerns = lax.axis_size("kern")
    local_rows, local_cols = q_ref.shape
    out_rows = local_rows + 2 * halo
    out_cols = local_cols + 2 * halo
    lanes = 2 * window
    ambit = k_ref.shape[1]
    groups = ambit // TAP_GROUP
    span = TAP_GROUP * window
    width_n = width * pairs

    def exists(dt, dq):
        return (tile + dt >= 0) & (tile + dt < tiles) & (kern + dq >= 0) & (kern + dq < kerns)

    def device(dt, dq):
        return {"tile": tile + dt, "kern": kern + dq}

    barrier = pltpu.get_barrier_semaphore()
    partners = sorted(set(MASK_FROM) | set(QUENCH_FROM))
    count = jnp.int32(0)
    for dt, dq in partners:
        here = exists(dt, dq)

        @pl.when(here)
        def _():
            pl.semaphore_signal(
                barrier, 1, device_id=device(dt, dq), device_id_type=pl.DeviceIdType.MESH
            )

        count = count + here.astype(jnp.int32)
    pl.semaphore_wait(barrier, count)

    def rows_for(source, dt, whole):
        height = source.shape[0]
        if dt == 0 or (abs(dt) == 1 and whole):
            return 0, height
        return (height - HALO, HALO) if dt < 0 else (0, HALO)

    plan = [(mask_ref, mask_slots, slot, offset, True) for slot, offset in enumerate(MASK_FROM)]
    plan += [(q_ref, q_slots, slot, offset, False) for slot, offset in enumerate(QUENCH_FROM)]
    copies = []
    for index, (source, slots, slot, (dt, dq), whole) in enumerate(plan):
        first, rows = rows_for(source, dt, whole)
        copy = pltpu.make_async_remote_copy(
            src_ref=source.at[pl.ds(first, rows)],
            dst_ref=slots.at[slot, pl.ds(first, rows)],
            send_sem=send_sems.at[index],
            recv_sem=recv_sems.at[index],
            device_id=device(-dt, -dq),
            device_id_type=pl.DeviceIdType.MESH,
        )

        @pl.when(exists(-dt, -dq))
        def _():
            copy.start()

        copies.append(copy)

    sel_lane = lax.broadcasted_iota(jnp.int32, (ambit, width * window), 1)
    sel_row = lax.broadcasted_iota(jnp.int32, (ambit, width * window), 0)
    selector = (sel_lane % window - sel_lane // window == sel_row).astype(jnp.bfloat16)

    rows_ref[...] = k_ref[...].astype(jnp.float32)

    def build(group, carry):
        kernel_rows = jnp.concatenate(
            [
                rows_ref[pl.ds(group * TAP_GROUP + j, pairs, stride=ambit), :]
                for j in range(TAP_GROUP)
            ],
            axis=0,
        ).astype(jnp.bfloat16)
        product = jnp.dot(
            kernel_rows, selector, preferred_element_type=jnp.float32
        ).astype(jnp.bfloat16)
        columns = [
            jnp.concatenate(
                [
                    product[j * pairs : (j + 1) * pairs, o * window : (o + 1) * window]
                    for o in range(width)
                ],
                axis=0,
            )
            for j in range(TAP_GROUP)
        ]
        taps_ref[:, pl.ds(pl.multiple_of(group * span, span), span)] = jnp.concatenate(
            columns, axis=1
        )
        return carry

    lax.fori_loop(0, groups, build, 0)

    for copy, (source, slots, slot, (dt, dq), whole) in zip(copies, plan):

        @pl.when(exists(-dt, -dq))
        def _():
            copy.wait_send()

        @pl.when(exists(dt, dq))
        def _():
            copy.wait_recv()

    def slot_rows(slots, slot, first, rows):
        dt, dq = (MASK_FROM if slots is mask_slots else QUENCH_FROM)[slot]
        value = slots[slot, pl.ds(first, rows), :]
        return jnp.where(exists(dt, dq), value, jnp.zeros_like(value))

    reach = HALO
    rows = jnp.concatenate(
        [
            slot_rows(mask_slots, 2, local_rows - reach, reach),
            slot_rows(mask_slots, 0, 0, local_rows),
            mask_ref[...],
            slot_rows(mask_slots, 1, 0, local_rows),
            slot_rows(mask_slots, 3, 0, reach),
        ],
        axis=0,
    ).astype(jnp.float32)
    total = rows.shape[1] + 128
    rows = jnp.concatenate([rows, jnp.zeros((rows.shape[0], 128), jnp.float32)], axis=1)
    lead = (win_ref.shape[0] // BLOCKS - out_rows) // 2 + halo
    for block in range(BLOCKS):
        start = kern * local_cols - lead + width * block
        part = pltpu.roll(rows, lax.rem(total - start, total), 1)[:, :window]
        win_ref[pl.ds(block, rows.shape[0], stride=BLOCKS), :] = part

    def band(left, middle, right):
        lane = lax.broadcasted_iota(jnp.int32, (middle.shape[0], lanes), 1)

        def widen(value):
            return jnp.concatenate(
                [value, jnp.zeros((value.shape[0], lanes - value.shape[1]), value.dtype)], axis=1
            )

        outer = lanes - (local_cols - halo)
        return jnp.where(
            lane < halo,
            pltpu.roll(widen(left), outer, 1),
            jnp.where(
                lane < halo + local_cols,
                pltpu.roll(widen(middle), halo, 1),
                jnp.where(lane < out_cols, pltpu.roll(widen(right), outer, 1), 0.0),
            ),
        )

    low = local_rows - halo
    base = jnp.concatenate(
        [
            band(*(slot_rows(q_slots, s, low, halo) for s in (0, 1, 2))),
            band(slot_rows(q_slots, 3, 0, local_rows), q_ref[...], slot_rows(q_slots, 4, 0, local_rows)),
            band(*(slot_rows(q_slots, s, 0, halo) for s in (5, 6, 7))),
        ],
        axis=0,
    )

    acc_ref[...] = jnp.zeros_like(acc_ref)

    def accumulate(group, carry):
        pieces = []
        for offset in range(TAP_GROUP):
            start = pl.multiple_of((group * TAP_GROUP + offset) * BLOCKS, BLOCKS)
            pieces.append(win_ref[pl.ds(start, out_rows * BLOCKS), :].astype(jnp.bfloat16))
        left = jnp.concatenate(pieces, axis=1)
        right = taps_ref[:, pl.ds(pl.multiple_of(group * span, span), span)]
        acc_ref[...] += lax.dot_general(
            left, right, (((1,), (1,)), ((), ())), preferred_element_type=jnp.float32
        )
        return carry

    lax.fori_loop(0, groups, accumulate, 0)

    kernel_of_lane = lax.broadcasted_iota(jnp.int32, (1, width_n), 1) % pairs // 2
    lane_weights = jnp.zeros((1, width_n), jnp.float32)
    for k in range(pairs // 2):
        lane_weights = jnp.where(kernel_of_lane == k, w_smem[k], lane_weights)
    summer = (
        lax.broadcasted_iota(jnp.int32, (width_n, window), 0) // pairs
        == lax.broadcasted_iota(jnp.int32, (width_n, window), 1)
    ).astype(jnp.float32)
    field = acc_ref[...]
    weighted = field * field * lane_weights
    red_ref[...] = jnp.dot(
        weighted, summer, precision=lax.Precision.HIGHEST,
        preferred_element_type=jnp.float32,
    )
    intensity = jnp.zeros((out_rows, lanes), jnp.float32)
    for block in range(BLOCKS):
        part = red_ref[pl.ds(block, out_rows, stride=BLOCKS), :]
        part = jnp.concatenate([part, jnp.zeros_like(part)], axis=1)
        intensity = intensity + pltpu.roll(part, width * block, 1) if block else part
    r = tile * local_rows - halo + lax.broadcasted_iota(jnp.int32, (out_rows, lanes), 0)
    c = kern * local_cols - halo + lax.broadcasted_iota(jnp.int32, (out_rows, lanes), 1)
    keep = (r >= 0) & (r < tiles * local_rows) & (c >= 0) & (c < kerns * local_cols)
    keep = keep & (c < kern * local_cols - halo + out_cols)
    acid = jnp.where(keep, 1.0 - jnp.exp(-EXPOSURE * intensity), 0.0)
    for _ in range(STEPS):
        quenched = QUENCH_RATE * acid * base
        acid_next = acid + DIFFUSE_ACID * spread_of(acid) - quenched
        base_next = base + DIFFUSE_BASE * spread_of(base) - quenched
        acid = jnp.where(keep, acid_next, 0.0)
        base = jnp.where(keep, base_next, 0.0)
    for out, value in ((i_out, intensity), (a_out, acid), (b_out, base)):
        out[...] = pltpu.roll(value, lanes - halo, 1)[halo : halo + local_rows, :local_cols]


def on_device(mask, kernels, socs_weights, quencher):
    ambit = kernels.shape[2]
    half_ambit = ambit // 2
    kern_count = lax.axis_size("kern")
    kern_index = lax.axis_index("kern")
    tile_index = lax.axis_index("tile")
    local_rows = mask.shape[0]
    local_cols = quencher.shape[1]
    halo = HALO
    out_rows = local_rows + 2 * halo
    out_cols = local_cols + 2 * halo
    width = out_cols // BLOCKS
    window = 128
    lanes = 2 * window
    window_rows = out_rows + ambit

    pairs = kernels.shape[0] * kernels.shape[1]
    kernel_rows = kernels.reshape(pairs * ambit, ambit)

    vmem = pl.BlockSpec(memory_space=pltpu.VMEM)
    out = jax.ShapeDtypeStruct((local_rows, local_cols), jnp.float32)
    copies = len(MASK_FROM) + len(QUENCH_FROM)
    m_rows = out_rows * BLOCKS
    return pl.pallas_call(
        functools.partial(fused_kernel, pairs=pairs, window=window, halo=halo, width=width),
        out_shape=(out, out, out),
        in_specs=[vmem] * 3 + [pl.BlockSpec(memory_space=pltpu.SMEM)],
        out_specs=(vmem, vmem, vmem),
        scratch_shapes=[
            pltpu.VMEM((len(MASK_FROM),) + mask.shape, mask.dtype),
            pltpu.VMEM((len(QUENCH_FROM),) + quencher.shape, quencher.dtype),
            pltpu.SemaphoreType.DMA((copies,)),
            pltpu.SemaphoreType.DMA((copies,)),
            pltpu.VMEM((width * pairs, ambit * window), jnp.bfloat16),
            pltpu.VMEM((window_rows * BLOCKS, window), jnp.float32),
            pltpu.VMEM((m_rows, width * pairs), jnp.float32),
            pltpu.VMEM((m_rows, window), jnp.float32),
            pltpu.VMEM((pairs * ambit, ambit), jnp.float32),
        ],
        compiler_params=pltpu.CompilerParams(
            collective_id=0, has_side_effects=True, vmem_limit_bytes=56 * 1024 * 1024
        ),
        cost_estimate=pl.CostEstimate(
            flops=2 * m_rows * ambit * window * width * pairs,
            transcendentals=0,
            bytes_accessed=kernel_rows.size * 2 + mask.size * 4 * 5,
        ),
    )(mask, quencher, kernel_rows, socs_weights)


def solution(mesh):
    placed = (P("tile", None), P(), P(), P("tile", "kern"))
    return jax.shard_map(
        on_device,
        mesh=mesh,
        in_specs=placed,
        out_specs=(P("tile", "kern"), P("tile", "kern"), P("tile", "kern")),
        check_vma=False,
    )
```

```python
import functools

import jax
import jax.numpy as jnp
from jax import lax
from jax.experimental import pallas as pl
from jax.experimental.pallas import tpu as pltpu
from jax.sharding import PartitionSpec as P

STEPS = 8


DIFFUSE_ACID = 0.2
DIFFUSE_BASE = 0.1
QUENCH_RATE = 0.5
EXPOSURE = 0.35

BLOCKS = 8
HALO = STEPS
TAP_GROUP = 8


def toeplitz_selector(ambit, window, width):
    tap_ids = lax.iota(jnp.int32, ambit)
    input_ids = lax.iota(jnp.int32, window)
    output_ids = lax.iota(jnp.int32, width)
    offsets = input_ids[None, None, :] - output_ids[None, :, None]
    selector = (offsets == tap_ids[:, None, None]).astype(jnp.bfloat16)
    return selector.reshape(ambit, width * window)


def spread_of(value):
    rows, lanes = value.shape
    up = pltpu.roll(value, 1, 0)
    down = pltpu.roll(value, rows - 1, 0)
    left = pltpu.roll(value, 1, 1)
    right = pltpu.roll(value, lanes - 1, 1)
    return up + down + left + right - 4.0 * value


MASK_FROM = ((-1, 0), (1, 0), (-2, 0), (2, 0))
QUENCH_FROM = ((-1, -1), (-1, 0), (-1, 1), (0, -1), (0, 1), (1, -1), (1, 0), (1, 1))


def fused_kernel(
    mask_ref, q_ref, k_ref, w_smem,
    o_ref,
    mask_slots, q_slots, send_sems, recv_sems, taps_ref, win_ref, acc_ref, red_ref, rows_ref,
    *, pairs, window, halo, width,
):
    tile = lax.axis_index("tile")
    kern = lax.axis_index("kern")
    tiles = lax.axis_size("tile")
    kerns = lax.axis_size("kern")
    local_rows, local_cols = q_ref.shape
    out_rows = local_rows + 2 * halo
    out_cols = local_cols + 2 * halo
    lanes = 2 * window
    ambit = k_ref.shape[1]
    groups = ambit // TAP_GROUP
    span = TAP_GROUP * window
    width_n = width * pairs

    def exists(dt, dq):
        return (tile + dt >= 0) & (tile + dt < tiles) & (kern + dq >= 0) & (kern + dq < kerns)

    def device(dt, dq):
        return {"tile": tile + dt, "kern": kern + dq}

    barrier = pltpu.get_barrier_semaphore()
    partners = sorted(set(MASK_FROM) | set(QUENCH_FROM))
    count = jnp.int32(0)
    for dt, dq in partners:
        here = exists(dt, dq)

        @pl.when(here)
        def _():
            pl.semaphore_signal(
                barrier, 1, device_id=device(dt, dq), device_id_type=pl.DeviceIdType.MESH
            )

        count = count + here.astype(jnp.int32)
    pl.semaphore_wait(barrier, count)

    def rows_for(source, dt, whole):
        height = source.shape[0]
        if dt == 0 or (abs(dt) == 1 and whole):
            return 0, height
        return (height - HALO, HALO) if dt < 0 else (0, HALO)

    plan = [(mask_ref, mask_slots, slot, offset, True) for slot, offset in enumerate(MASK_FROM)]
    plan += [(q_ref, q_slots, slot, offset, False) for slot, offset in enumerate(QUENCH_FROM)]
    copies = []
    for index, (source, slots, slot, (dt, dq), whole) in enumerate(plan):
        first, rows = rows_for(source, dt, whole)
        copy = pltpu.make_async_remote_copy(
            src_ref=source.at[pl.ds(first, rows)],
            dst_ref=slots.at[slot, pl.ds(first, rows)],
            send_sem=send_sems.at[index],
            recv_sem=recv_sems.at[index],
            device_id=device(-dt, -dq),
            device_id_type=pl.DeviceIdType.MESH,
        )

        @pl.when(exists(-dt, -dq))
        def _():
            copy.start()

        copies.append(copy)

    sel_lane = lax.broadcasted_iota(jnp.int32, (ambit, width * window), 1)
    sel_row = lax.broadcasted_iota(jnp.int32, (ambit, width * window), 0)
    selector = (sel_lane % window - sel_lane // window == sel_row).astype(jnp.bfloat16)

    rows_ref[...] = k_ref[...].astype(jnp.float32)

    def build(group, carry):
        kernel_rows = jnp.concatenate(
            [
                rows_ref[pl.ds(group * TAP_GROUP + j, pairs, stride=ambit), :]
                for j in range(TAP_GROUP)
            ],
            axis=0,
        ).astype(jnp.bfloat16)
        product = jnp.dot(
            kernel_rows, selector, preferred_element_type=jnp.float32
        ).astype(jnp.bfloat16)
        columns = [
            jnp.concatenate(
                [
                    product[j * pairs : (j + 1) * pairs, o * window : (o + 1) * window]
                    for o in range(width)
                ],
                axis=0,
            )
            for j in range(TAP_GROUP)
        ]
        taps_ref[:, pl.ds(pl.multiple_of(group * span, span), span)] = jnp.concatenate(
            columns, axis=1
        )
        return carry

    lax.fori_loop(0, groups, build, 0)

    def wait_for(kind):
        for copy, (source, slots, slot, (dt, dq), whole) in zip(copies, plan):
            if kind == "send":

                @pl.when(exists(-dt, -dq))
                def _():
                    copy.wait_send()

            elif (slots is mask_slots) == (kind == "mask"):

                @pl.when(exists(dt, dq))
                def _():
                    copy.wait_recv()

    wait_for("mask")

    def slot_rows(slots, slot, first, rows):
        dt, dq = (MASK_FROM if slots is mask_slots else QUENCH_FROM)[slot]
        value = slots[slot, pl.ds(first, rows), :]
        return jnp.where(exists(dt, dq), value, jnp.zeros_like(value))

    reach = HALO
    rows = jnp.concatenate(
        [
            slot_rows(mask_slots, 2, local_rows - reach, reach),
            slot_rows(mask_slots, 0, 0, local_rows),
            mask_ref[...],
            slot_rows(mask_slots, 1, 0, local_rows),
            slot_rows(mask_slots, 3, 0, reach),
        ],
        axis=0,
    ).astype(jnp.float32)
    total = rows.shape[1] + 128
    rows = jnp.concatenate([rows, jnp.zeros((rows.shape[0], 128), jnp.float32)], axis=1)
    lead = (win_ref.shape[0] // BLOCKS - out_rows) // 2 + halo
    for block in range(BLOCKS):
        start = kern * local_cols - lead + width * block
        part = pltpu.roll(rows, lax.rem(total - start, total), 1)[:, :window]
        win_ref[pl.ds(block, rows.shape[0], stride=BLOCKS), :] = part

    def band(left, middle, right):
        lane = lax.broadcasted_iota(jnp.int32, (middle.shape[0], lanes), 1)

        def widen(value):
            return jnp.concatenate(
                [value, jnp.zeros((value.shape[0], lanes - value.shape[1]), value.dtype)], axis=1
            )

        outer = lanes - (local_cols - halo)
        return jnp.where(
            lane < halo,
            pltpu.roll(widen(left), outer, 1),
            jnp.where(
                lane < halo + local_cols,
                pltpu.roll(widen(middle), halo, 1),
                jnp.where(lane < out_cols, pltpu.roll(widen(right), outer, 1), 0.0),
            ),
        )

    acc_ref[...] = jnp.zeros_like(acc_ref)

    def accumulate(group, carry):
        pieces = []
        for offset in range(TAP_GROUP):
            start = pl.multiple_of((group * TAP_GROUP + offset) * BLOCKS, BLOCKS)
            pieces.append(win_ref[pl.ds(start, out_rows * BLOCKS), :].astype(jnp.bfloat16))
        left = jnp.concatenate(pieces, axis=1)
        right = taps_ref[:, pl.ds(pl.multiple_of(group * span, span), span)]
        acc_ref[...] += lax.dot_general(
            left, right, (((1,), (1,)), ((), ())), preferred_element_type=jnp.float32
        )
        return carry

    lax.fori_loop(0, groups, accumulate, 0)

    wait_for("quench")
    wait_for("send")
    low = local_rows - halo
    base = jnp.concatenate(
        [
            band(*(slot_rows(q_slots, s, low, halo) for s in (0, 1, 2))),
            band(slot_rows(q_slots, 3, 0, local_rows), q_ref[...], slot_rows(q_slots, 4, 0, local_rows)),
            band(*(slot_rows(q_slots, s, 0, halo) for s in (5, 6, 7))),
        ],
        axis=0,
    )


    kernel_of_lane = lax.broadcasted_iota(jnp.int32, (1, width_n), 1) % pairs // 2
    lane_weights = jnp.zeros((1, width_n), jnp.float32)
    for k in range(pairs // 2):
        lane_weights = jnp.where(kernel_of_lane == k, w_smem[k], lane_weights)
    summer = (
        lax.broadcasted_iota(jnp.int32, (width_n, window), 0) // pairs
        == lax.broadcasted_iota(jnp.int32, (width_n, window), 1)
    ).astype(jnp.float32)
    field = acc_ref[...]
    weighted = field * field * lane_weights
    red_ref[...] = jnp.dot(
        weighted, summer, precision=lax.Precision.HIGHEST,
        preferred_element_type=jnp.float32,
    )
    intensity = jnp.zeros((out_rows, lanes), jnp.float32)
    for block in range(BLOCKS):
        part = red_ref[pl.ds(block, out_rows, stride=BLOCKS), :]
        part = jnp.concatenate([part, jnp.zeros_like(part)], axis=1)
        intensity = intensity + pltpu.roll(part, width * block, 1) if block else part
    r = tile * local_rows - halo + lax.broadcasted_iota(jnp.int32, (out_rows, lanes), 0)
    c = kern * local_cols - halo + lax.broadcasted_iota(jnp.int32, (out_rows, lanes), 1)
    keep = (r >= 0) & (r < tiles * local_rows) & (c >= 0) & (c < kerns * local_cols)
    keep = keep & (c < kern * local_cols - halo + out_cols)
    acid = jnp.where(keep, 1.0 - jnp.exp(-EXPOSURE * intensity), 0.0)
    for _ in range(STEPS):
        quenched = QUENCH_RATE * acid * base
        acid_next = acid + DIFFUSE_ACID * spread_of(acid) - quenched
        base_next = base + DIFFUSE_BASE * spread_of(base) - quenched
        acid = jnp.where(keep, acid_next, 0.0)
        base = jnp.where(keep, base_next, 0.0)
    for index, value in enumerate((intensity, acid, base)):
        o_ref[index] = pltpu.roll(value, lanes - halo, 1)[halo : halo + local_rows, :local_cols]


def on_device(mask, kernels, socs_weights, quencher):
    ambit = kernels.shape[2]
    half_ambit = ambit // 2
    kern_count = lax.axis_size("kern")
    kern_index = lax.axis_index("kern")
    tile_index = lax.axis_index("tile")
    local_rows = mask.shape[0]
    local_cols = quencher.shape[1]
    halo = HALO
    out_rows = local_rows + 2 * halo
    out_cols = local_cols + 2 * halo
    width = out_cols // BLOCKS
    window = 128
    lanes = 2 * window
    window_rows = out_rows + ambit

    pairs = kernels.shape[0] * kernels.shape[1]
    kernel_rows = kernels.reshape(pairs * ambit, ambit)

    vmem = pl.BlockSpec(memory_space=pltpu.VMEM)
    out = jax.ShapeDtypeStruct((3, local_rows, local_cols), jnp.float32)
    copies = len(MASK_FROM) + len(QUENCH_FROM)
    m_rows = out_rows * BLOCKS
    result = pl.pallas_call(
        functools.partial(fused_kernel, pairs=pairs, window=window, halo=halo, width=width),
        out_shape=out,
        in_specs=[vmem] * 3 + [pl.BlockSpec(memory_space=pltpu.SMEM)],
        out_specs=vmem,
        scratch_shapes=[
            pltpu.VMEM((len(MASK_FROM),) + mask.shape, mask.dtype),
            pltpu.VMEM((len(QUENCH_FROM),) + quencher.shape, quencher.dtype),
            pltpu.SemaphoreType.DMA((copies,)),
            pltpu.SemaphoreType.DMA((copies,)),
            pltpu.VMEM((width * pairs, ambit * window), jnp.bfloat16),
            pltpu.VMEM((window_rows * BLOCKS, window), jnp.float32),
            pltpu.VMEM((m_rows, width * pairs), jnp.float32),
            pltpu.VMEM((m_rows, window), jnp.float32),
            pltpu.VMEM((pairs * ambit, ambit), jnp.float32),
        ],
        compiler_params=pltpu.CompilerParams(
            collective_id=0, has_side_effects=True, vmem_limit_bytes=56 * 1024 * 1024
        ),
        cost_estimate=pl.CostEstimate(
            flops=2 * m_rows * ambit * window * width * pairs,
            transcendentals=0,
            bytes_accessed=kernel_rows.size * 2 + mask.size * 4 * 5,
        ),
    )(mask, quencher, kernel_rows, socs_weights)
    return result[0], result[1], result[2]


def solution(mesh):
    placed = (P("tile", None), P(), P(), P("tile", "kern"))
    return jax.shard_map(
        on_device,
        mesh=mesh,
        in_specs=placed,
        out_specs=(P("tile", "kern"), P("tile", "kern"), P("tile", "kern")),
        check_vma=False,
    )
```

```python
import functools

import jax
import jax.numpy as jnp
from jax import lax
from jax.experimental import pallas as pl
from jax.experimental.pallas import tpu as pltpu
from jax.sharding import PartitionSpec as P

STEPS = 8


DIFFUSE_ACID = 0.2
DIFFUSE_BASE = 0.1
QUENCH_RATE = 0.5
EXPOSURE = 0.35

BLOCKS = 8
HALO = STEPS
TAP_GROUP = 8


def toeplitz_selector(ambit, window, width):
    tap_ids = lax.iota(jnp.int32, ambit)
    input_ids = lax.iota(jnp.int32, window)
    output_ids = lax.iota(jnp.int32, width)
    offsets = input_ids[None, None, :] - output_ids[None, :, None]
    selector = (offsets == tap_ids[:, None, None]).astype(jnp.bfloat16)
    return selector.reshape(ambit, width * window)


def spread_of(value):
    rows, lanes = value.shape
    up = pltpu.roll(value, 1, 0)
    down = pltpu.roll(value, rows - 1, 0)
    left = pltpu.roll(value, 1, 1)
    right = pltpu.roll(value, lanes - 1, 1)
    return up + down + left + right - 4.0 * value


MASK_FROM = ((-1, 0), (1, 0), (-2, 0), (2, 0))
QUENCH_FROM = ((-1, -1), (-1, 0), (-1, 1), (0, -1), (0, 1), (1, -1), (1, 0), (1, 1))


def fused_kernel(
    mask_ref, q_ref, k_ref, w_smem,
    o_ref,
    mask_slots, q_slots, send_sems, recv_sems, taps_ref, win_ref, acc_ref, red_ref, rows_ref,
    *, pairs, window, halo, width,
):
    tile = lax.axis_index("tile")
    kern = lax.axis_index("kern")
    tiles = lax.axis_size("tile")
    kerns = lax.axis_size("kern")
    local_rows, local_cols = q_ref.shape
    out_rows = local_rows + 2 * halo
    out_cols = local_cols + 2 * halo
    lanes = 2 * window
    ambit = k_ref.shape[1]
    groups = ambit // TAP_GROUP
    span = TAP_GROUP * window
    width_n = width * pairs

    def exists(dt, dq):
        return (tile + dt >= 0) & (tile + dt < tiles) & (kern + dq >= 0) & (kern + dq < kerns)

    def device(dt, dq):
        return {"tile": tile + dt, "kern": kern + dq}

    barrier = pltpu.get_barrier_semaphore()
    partners = sorted(set(MASK_FROM) | set(QUENCH_FROM))
    count = jnp.int32(0)
    for dt, dq in partners:
        here = exists(dt, dq)

        @pl.when(here)
        def _():
            pl.semaphore_signal(
                barrier, 1, device_id=device(dt, dq), device_id_type=pl.DeviceIdType.MESH
            )

        count = count + here.astype(jnp.int32)
    sel_lane = lax.broadcasted_iota(jnp.int32, (ambit, width * window), 1)
    sel_row = lax.broadcasted_iota(jnp.int32, (ambit, width * window), 0)
    selector = (sel_lane % window - sel_lane // window == sel_row).astype(jnp.bfloat16)

    rows_ref[...] = k_ref[...].astype(jnp.float32)

    def build(group, carry):
        kernel_rows = jnp.concatenate(
            [
                rows_ref[pl.ds(group * TAP_GROUP + j, pairs, stride=ambit), :]
                for j in range(TAP_GROUP)
            ],
            axis=0,
        ).astype(jnp.bfloat16)
        product = jnp.dot(
            kernel_rows, selector, preferred_element_type=jnp.float32
        ).astype(jnp.bfloat16)
        columns = [
            jnp.concatenate(
                [
                    product[j * pairs : (j + 1) * pairs, o * window : (o + 1) * window]
                    for o in range(width)
                ],
                axis=0,
            )
            for j in range(TAP_GROUP)
        ]
        taps_ref[:, pl.ds(pl.multiple_of(group * span, span), span)] = jnp.concatenate(
            columns, axis=1
        )
        return carry

    lax.fori_loop(0, groups // 2, build, 0)
    pl.semaphore_wait(barrier, count)

    def rows_for(source, dt, whole):
        height = source.shape[0]
        if dt == 0 or (abs(dt) == 1 and whole):
            return 0, height
        return (height - HALO, HALO) if dt < 0 else (0, HALO)

    plan = [(mask_ref, mask_slots, slot, offset, True) for slot, offset in enumerate(MASK_FROM)]
    plan += [(q_ref, q_slots, slot, offset, False) for slot, offset in enumerate(QUENCH_FROM)]
    copies = []
    for index, (source, slots, slot, (dt, dq), whole) in enumerate(plan):
        first, rows = rows_for(source, dt, whole)
        copy = pltpu.make_async_remote_copy(
            src_ref=source.at[pl.ds(first, rows)],
            dst_ref=slots.at[slot, pl.ds(first, rows)],
            send_sem=send_sems.at[index],
            recv_sem=recv_sems.at[index],
            device_id=device(-dt, -dq),
            device_id_type=pl.DeviceIdType.MESH,
        )

        @pl.when(exists(-dt, -dq))
        def _():
            copy.start()

        copies.append(copy)

    lax.fori_loop(groups // 2, groups, build, 0)

    def wait_for(kind):
        for copy, (source, slots, slot, (dt, dq), whole) in zip(copies, plan):
            if kind == "send":

                @pl.when(exists(-dt, -dq))
                def _():
                    copy.wait_send()

            elif (slots is mask_slots) == (kind == "mask"):

                @pl.when(exists(dt, dq))
                def _():
                    copy.wait_recv()

    wait_for("mask")

    def slot_rows(slots, slot, first, rows):
        dt, dq = (MASK_FROM if slots is mask_slots else QUENCH_FROM)[slot]
        value = slots[slot, pl.ds(first, rows), :]
        return jnp.where(exists(dt, dq), value, jnp.zeros_like(value))

    reach = HALO
    rows = jnp.concatenate(
        [
            slot_rows(mask_slots, 2, local_rows - reach, reach),
            slot_rows(mask_slots, 0, 0, local_rows),
            mask_ref[...],
            slot_rows(mask_slots, 1, 0, local_rows),
            slot_rows(mask_slots, 3, 0, reach),
        ],
        axis=0,
    ).astype(jnp.float32)
    total = rows.shape[1] + 128
    rows = jnp.concatenate([rows, jnp.zeros((rows.shape[0], 128), jnp.float32)], axis=1)
    lead = (win_ref.shape[0] // BLOCKS - out_rows) // 2 + halo
    for block in range(BLOCKS):
        start = kern * local_cols - lead + width * block
        part = pltpu.roll(rows, lax.rem(total - start, total), 1)[:, :window]
        win_ref[pl.ds(block, rows.shape[0], stride=BLOCKS), :] = part

    def band(left, middle, right):
        lane = lax.broadcasted_iota(jnp.int32, (middle.shape[0], lanes), 1)

        def widen(value):
            return jnp.concatenate(
                [value, jnp.zeros((value.shape[0], lanes - value.shape[1]), value.dtype)], axis=1
            )

        outer = lanes - (local_cols - halo)
        return jnp.where(
            lane < halo,
            pltpu.roll(widen(left), outer, 1),
            jnp.where(
                lane < halo + local_cols,
                pltpu.roll(widen(middle), halo, 1),
                jnp.where(lane < out_cols, pltpu.roll(widen(right), outer, 1), 0.0),
            ),
        )

    acc_ref[...] = jnp.zeros_like(acc_ref)

    def accumulate(group, carry):
        pieces = []
        for offset in range(32):
            start = pl.multiple_of((group * 32 + offset) * BLOCKS, BLOCKS)
            pieces.append(win_ref[pl.ds(start, out_rows * BLOCKS), :].astype(jnp.bfloat16))
        left = jnp.concatenate(pieces, axis=1)
        right = taps_ref[:, pl.ds(pl.multiple_of(group * 32 * window, 32 * window), 32 * window)]
        acc_ref[...] += lax.dot_general(
            left, right, (((1,), (1,)), ((), ())), preferred_element_type=jnp.float32
        )
        return carry

    lax.fori_loop(0, ambit // 32, accumulate, 0)

    wait_for("quench")
    wait_for("send")
    low = local_rows - halo
    base = jnp.concatenate(
        [
            band(*(slot_rows(q_slots, s, low, halo) for s in (0, 1, 2))),
            band(slot_rows(q_slots, 3, 0, local_rows), q_ref[...], slot_rows(q_slots, 4, 0, local_rows)),
            band(*(slot_rows(q_slots, s, 0, halo) for s in (5, 6, 7))),
        ],
        axis=0,
    )


    kernel_of_lane = lax.broadcasted_iota(jnp.int32, (1, width_n), 1) % pairs // 2
    lane_weights = jnp.zeros((1, width_n), jnp.float32)
    for k in range(pairs // 2):
        lane_weights = jnp.where(kernel_of_lane == k, w_smem[k], lane_weights)
    summer = (
        lax.broadcasted_iota(jnp.int32, (width_n, window), 0) // pairs
        == lax.broadcasted_iota(jnp.int32, (width_n, window), 1)
    ).astype(jnp.float32)
    field = acc_ref[...]
    weighted = field * field * lane_weights
    red_ref[...] = jnp.dot(
        weighted, summer, precision=lax.Precision.HIGHEST,
        preferred_element_type=jnp.float32,
    )
    intensity = jnp.zeros((out_rows, lanes), jnp.float32)
    for block in range(BLOCKS):
        part = red_ref[pl.ds(block, out_rows, stride=BLOCKS), :]
        part = jnp.concatenate([part, jnp.zeros_like(part)], axis=1)
        intensity = intensity + pltpu.roll(part, width * block, 1) if block else part
    r = tile * local_rows - halo + lax.broadcasted_iota(jnp.int32, (out_rows, lanes), 0)
    c = kern * local_cols - halo + lax.broadcasted_iota(jnp.int32, (out_rows, lanes), 1)
    keep = (r >= 0) & (r < tiles * local_rows) & (c >= 0) & (c < kerns * local_cols)
    keep = keep & (c < kern * local_cols - halo + out_cols)
    acid = jnp.where(keep, 1.0 - jnp.exp(-EXPOSURE * intensity), 0.0)
    for _ in range(STEPS):
        quenched = QUENCH_RATE * acid * base
        acid_next = acid + DIFFUSE_ACID * spread_of(acid) - quenched
        base_next = base + DIFFUSE_BASE * spread_of(base) - quenched
        acid = jnp.where(keep, acid_next, 0.0)
        base = jnp.where(keep, base_next, 0.0)
    for index, value in enumerate((intensity, acid, base)):
        o_ref[index] = pltpu.roll(value, lanes - halo, 1)[halo : halo + local_rows, :local_cols]


def on_device(mask, kernels, socs_weights, quencher):
    ambit = kernels.shape[2]
    half_ambit = ambit // 2
    kern_count = lax.axis_size("kern")
    kern_index = lax.axis_index("kern")
    tile_index = lax.axis_index("tile")
    local_rows = mask.shape[0]
    local_cols = quencher.shape[1]
    halo = HALO
    out_rows = local_rows + 2 * halo
    out_cols = local_cols + 2 * halo
    width = out_cols // BLOCKS
    window = 128
    lanes = 2 * window
    window_rows = out_rows + ambit

    pairs = kernels.shape[0] * kernels.shape[1]
    kernel_rows = kernels.reshape(pairs * ambit, ambit)

    vmem = pl.BlockSpec(memory_space=pltpu.VMEM)
    out = jax.ShapeDtypeStruct((3, local_rows, local_cols), jnp.float32)
    copies = len(MASK_FROM) + len(QUENCH_FROM)
    m_rows = out_rows * BLOCKS
    result = pl.pallas_call(
        functools.partial(fused_kernel, pairs=pairs, window=window, halo=halo, width=width),
        out_shape=out,
        in_specs=[vmem] * 3 + [pl.BlockSpec(memory_space=pltpu.SMEM)],
        out_specs=vmem,
        scratch_shapes=[
            pltpu.VMEM((len(MASK_FROM),) + mask.shape, mask.dtype),
            pltpu.VMEM((len(QUENCH_FROM),) + quencher.shape, quencher.dtype),
            pltpu.SemaphoreType.DMA((copies,)),
            pltpu.SemaphoreType.DMA((copies,)),
            pltpu.VMEM((width * pairs, ambit * window), jnp.bfloat16),
            pltpu.VMEM((window_rows * BLOCKS, window), jnp.float32),
            pltpu.VMEM((m_rows, width * pairs), jnp.float32),
            pltpu.VMEM((m_rows, window), jnp.float32),
            pltpu.VMEM((pairs * ambit, ambit), jnp.float32),
        ],
        compiler_params=pltpu.CompilerParams(
            collective_id=0, has_side_effects=True, vmem_limit_bytes=56 * 1024 * 1024
        ),
        cost_estimate=pl.CostEstimate(
            flops=2 * m_rows * ambit * window * width * pairs,
            transcendentals=0,
            bytes_accessed=kernel_rows.size * 2 + mask.size * 4 * 5,
        ),
    )(mask, quencher, kernel_rows, socs_weights)
    return result[0], result[1], result[2]


def solution(mesh):
    placed = (P("tile", None), P(), P(), P("tile", "kern"))
    return jax.shard_map(
        on_device,
        mesh=mesh,
        in_specs=placed,
        out_specs=(P("tile", "kern"), P("tile", "kern"), P("tile", "kern")),
        check_vma=False,
    )
```

```python
import functools

import jax
import jax.numpy as jnp
from jax import lax
from jax.experimental import pallas as pl
from jax.experimental.pallas import tpu as pltpu
from jax.sharding import PartitionSpec as P

STEPS = 8


DIFFUSE_ACID = 0.2
DIFFUSE_BASE = 0.1
QUENCH_RATE = 0.5
EXPOSURE = 0.35

BLOCKS = 8
HALO = STEPS
TAP_GROUP = 8


def toeplitz_selector(ambit, window, width):
    tap_ids = lax.iota(jnp.int32, ambit)
    input_ids = lax.iota(jnp.int32, window)
    output_ids = lax.iota(jnp.int32, width)
    offsets = input_ids[None, None, :] - output_ids[None, :, None]
    selector = (offsets == tap_ids[:, None, None]).astype(jnp.bfloat16)
    return selector.reshape(ambit, width * window)


def spread_of(value):
    rows, lanes = value.shape
    up = pltpu.roll(value, 1, 0)
    down = pltpu.roll(value, rows - 1, 0)
    left = pltpu.roll(value, 1, 1)
    right = pltpu.roll(value, lanes - 1, 1)
    return up + down + left + right - 4.0 * value


MASK_FROM = ((-1, 0), (1, 0), (-2, 0), (2, 0))
QUENCH_FROM = ((-1, -1), (-1, 0), (-1, 1), (0, -1), (0, 1), (1, -1), (1, 0), (1, 1))


def fused_kernel(
    mask_ref, q_ref, k_ref, w_smem,
    o_ref,
    mask_slots, q_slots, send_sems, recv_sems, taps_ref, win_ref, acc_ref, red_ref, rows_ref,
    *, pairs, window, halo, width,
):
    tile = lax.axis_index("tile")
    kern = lax.axis_index("kern")
    tiles = lax.axis_size("tile")
    kerns = lax.axis_size("kern")
    local_rows, local_cols = q_ref.shape
    out_rows = local_rows + 2 * halo
    out_cols = local_cols + 2 * halo
    lanes = 2 * window
    ambit = k_ref.shape[1]
    groups = ambit // TAP_GROUP
    span = TAP_GROUP * window
    width_n = width * pairs

    def exists(dt, dq):
        return (tile + dt >= 0) & (tile + dt < tiles) & (kern + dq >= 0) & (kern + dq < kerns)

    def device(dt, dq):
        return {"tile": tile + dt, "kern": kern + dq}

    barrier = pltpu.get_barrier_semaphore()
    partners = sorted(set(MASK_FROM) | set(QUENCH_FROM))
    count = jnp.int32(0)
    for dt, dq in partners:
        here = exists(dt, dq)

        @pl.when(here)
        def _():
            pl.semaphore_signal(
                barrier, 1, device_id=device(dt, dq), device_id_type=pl.DeviceIdType.MESH
            )

        count = count + here.astype(jnp.int32)
    sel_lane = lax.broadcasted_iota(jnp.int32, (ambit, width * window), 1)
    sel_row = lax.broadcasted_iota(jnp.int32, (ambit, width * window), 0)
    selector = (sel_lane % window - sel_lane // window == sel_row).astype(jnp.bfloat16)

    rows_ref[...] = k_ref[...].astype(jnp.float32)

    def build(group, carry):
        kernel_rows = jnp.concatenate(
            [
                rows_ref[pl.ds(group * TAP_GROUP + j, pairs, stride=ambit), :]
                for j in range(TAP_GROUP)
            ],
            axis=0,
        ).astype(jnp.bfloat16)
        product = jnp.dot(
            kernel_rows, selector, preferred_element_type=jnp.float32
        ).astype(jnp.bfloat16)
        columns = [
            jnp.concatenate(
                [
                    product[j * pairs : (j + 1) * pairs, o * window : (o + 1) * window]
                    for o in range(width)
                ],
                axis=0,
            )
            for j in range(TAP_GROUP)
        ]
        taps_ref[:, pl.ds(pl.multiple_of(group * span, span), span)] = jnp.concatenate(
            columns, axis=1
        )
        return carry

    lax.fori_loop(0, groups // 4, build, 0)
    pl.semaphore_wait(barrier, count)

    def rows_for(source, dt, whole):
        height = source.shape[0]
        if dt == 0 or (abs(dt) == 1 and whole):
            return 0, height
        return (height - HALO, HALO) if dt < 0 else (0, HALO)

    plan = [(mask_ref, mask_slots, slot, offset, True) for slot, offset in enumerate(MASK_FROM)]
    plan += [(q_ref, q_slots, slot, offset, False) for slot, offset in enumerate(QUENCH_FROM)]
    copies = []
    for index, (source, slots, slot, (dt, dq), whole) in enumerate(plan):
        first, rows = rows_for(source, dt, whole)
        copy = pltpu.make_async_remote_copy(
            src_ref=source.at[pl.ds(first, rows)],
            dst_ref=slots.at[slot, pl.ds(first, rows)],
            send_sem=send_sems.at[index],
            recv_sem=recv_sems.at[index],
            device_id=device(-dt, -dq),
            device_id_type=pl.DeviceIdType.MESH,
        )

        @pl.when(exists(-dt, -dq))
        def _():
            copy.start()

        copies.append(copy)

    lax.fori_loop(groups // 4, groups, build, 0)

    def wait_for(kind):
        for copy, (source, slots, slot, (dt, dq), whole) in zip(copies, plan):
            if kind == "send":

                @pl.when(exists(-dt, -dq))
                def _():
                    copy.wait_send()

            elif (slots is mask_slots) == (kind == "mask"):

                @pl.when(exists(dt, dq))
                def _():
                    copy.wait_recv()

    wait_for("mask")

    def slot_rows(slots, slot, first, rows):
        dt, dq = (MASK_FROM if slots is mask_slots else QUENCH_FROM)[slot]
        value = slots[slot, pl.ds(first, rows), :]
        return jnp.where(exists(dt, dq), value, jnp.zeros_like(value))

    reach = HALO
    rows = jnp.concatenate(
        [
            slot_rows(mask_slots, 2, local_rows - reach, reach),
            slot_rows(mask_slots, 0, 0, local_rows),
            mask_ref[...],
            slot_rows(mask_slots, 1, 0, local_rows),
            slot_rows(mask_slots, 3, 0, reach),
        ],
        axis=0,
    ).astype(jnp.float32)
    total = rows.shape[1] + 128
    rows = jnp.concatenate([rows, jnp.zeros((rows.shape[0], 128), jnp.float32)], axis=1)
    lead = (win_ref.shape[0] // BLOCKS - out_rows) // 2 + halo
    for block in range(BLOCKS):
        start = kern * local_cols - lead + width * block
        part = pltpu.roll(rows, lax.rem(total - start, total), 1)[:, :window]
        win_ref[pl.ds(block, rows.shape[0], stride=BLOCKS), :] = part

    def band(left, middle, right):
        lane = lax.broadcasted_iota(jnp.int32, (middle.shape[0], lanes), 1)

        def widen(value):
            return jnp.concatenate(
                [value, jnp.zeros((value.shape[0], lanes - value.shape[1]), value.dtype)], axis=1
            )

        outer = lanes - (local_cols - halo)
        return jnp.where(
            lane < halo,
            pltpu.roll(widen(left), outer, 1),
            jnp.where(
                lane < halo + local_cols,
                pltpu.roll(widen(middle), halo, 1),
                jnp.where(lane < out_cols, pltpu.roll(widen(right), outer, 1), 0.0),
            ),
        )

    acc_ref[...] = jnp.zeros_like(acc_ref)

    def accumulate(group, carry):
        pieces = []
        for offset in range(32):
            start = pl.multiple_of((group * 32 + offset) * BLOCKS, BLOCKS)
            pieces.append(win_ref[pl.ds(start, out_rows * BLOCKS), :].astype(jnp.bfloat16))
        left = jnp.concatenate(pieces, axis=1)
        right = taps_ref[:, pl.ds(pl.multiple_of(group * 32 * window, 32 * window), 32 * window)]
        acc_ref[...] += lax.dot_general(
            left, right, (((1,), (1,)), ((), ())), preferred_element_type=jnp.float32
        )
        return carry

    lax.fori_loop(0, ambit // 32, accumulate, 0)

    wait_for("quench")
    wait_for("send")
    low = local_rows - halo
    base = jnp.concatenate(
        [
            band(*(slot_rows(q_slots, s, low, halo) for s in (0, 1, 2))),
            band(slot_rows(q_slots, 3, 0, local_rows), q_ref[...], slot_rows(q_slots, 4, 0, local_rows)),
            band(*(slot_rows(q_slots, s, 0, halo) for s in (5, 6, 7))),
        ],
        axis=0,
    )


    kernel_of_lane = lax.broadcasted_iota(jnp.int32, (1, width_n), 1) % pairs // 2
    lane_weights = jnp.zeros((1, width_n), jnp.float32)
    for k in range(pairs // 2):
        lane_weights = jnp.where(kernel_of_lane == k, w_smem[k], lane_weights)
    summer = (
        lax.broadcasted_iota(jnp.int32, (width_n, window), 0) // pairs
        == lax.broadcasted_iota(jnp.int32, (width_n, window), 1)
    ).astype(jnp.float32)
    field = acc_ref[...]
    weighted = field * field * lane_weights
    red_ref[...] = jnp.dot(
        weighted, summer, precision=lax.Precision.HIGHEST,
        preferred_element_type=jnp.float32,
    )
    intensity = jnp.zeros((out_rows, lanes), jnp.float32)
    for block in range(BLOCKS):
        part = red_ref[pl.ds(block, out_rows, stride=BLOCKS), :]
        part = jnp.concatenate([part, jnp.zeros_like(part)], axis=1)
        intensity = intensity + pltpu.roll(part, width * block, 1) if block else part
    r = tile * local_rows - halo + lax.broadcasted_iota(jnp.int32, (out_rows, lanes), 0)
    c = kern * local_cols - halo + lax.broadcasted_iota(jnp.int32, (out_rows, lanes), 1)
    keep = (r >= 0) & (r < tiles * local_rows) & (c >= 0) & (c < kerns * local_cols)
    keep = keep & (c < kern * local_cols - halo + out_cols)
    acid = jnp.where(keep, 1.0 - jnp.exp(-EXPOSURE * intensity), 0.0)
    for _ in range(STEPS):
        quenched = QUENCH_RATE * acid * base
        acid_next = acid + DIFFUSE_ACID * spread_of(acid) - quenched
        base_next = base + DIFFUSE_BASE * spread_of(base) - quenched
        acid = jnp.where(keep, acid_next, 0.0)
        base = jnp.where(keep, base_next, 0.0)
    for index, value in enumerate((intensity, acid, base)):
        o_ref[index] = pltpu.roll(value, lanes - halo, 1)[halo : halo + local_rows, :local_cols]


def on_device(mask, kernels, socs_weights, quencher):
    ambit = kernels.shape[2]
    half_ambit = ambit // 2
    kern_count = lax.axis_size("kern")
    kern_index = lax.axis_index("kern")
    tile_index = lax.axis_index("tile")
    local_rows = mask.shape[0]
    local_cols = quencher.shape[1]
    halo = HALO
    out_rows = local_rows + 2 * halo
    out_cols = local_cols + 2 * halo
    width = out_cols // BLOCKS
    window = 128
    lanes = 2 * window
    window_rows = out_rows + ambit

    pairs = kernels.shape[0] * kernels.shape[1]
    kernel_rows = kernels.reshape(pairs * ambit, ambit)

    vmem = pl.BlockSpec(memory_space=pltpu.VMEM)
    out = jax.ShapeDtypeStruct((3, local_rows, local_cols), jnp.float32)
    copies = len(MASK_FROM) + len(QUENCH_FROM)
    m_rows = out_rows * BLOCKS
    result = pl.pallas_call(
        functools.partial(fused_kernel, pairs=pairs, window=window, halo=halo, width=width),
        out_shape=out,
        in_specs=[vmem] * 3 + [pl.BlockSpec(memory_space=pltpu.SMEM)],
        out_specs=vmem,
        scratch_shapes=[
            pltpu.VMEM((len(MASK_FROM),) + mask.shape, mask.dtype),
            pltpu.VMEM((len(QUENCH_FROM),) + quencher.shape, quencher.dtype),
            pltpu.SemaphoreType.DMA((copies,)),
            pltpu.SemaphoreType.DMA((copies,)),
            pltpu.VMEM((width * pairs, ambit * window), jnp.bfloat16),
            pltpu.VMEM((window_rows * BLOCKS, window), jnp.float32),
            pltpu.VMEM((m_rows, width * pairs), jnp.float32),
            pltpu.VMEM((m_rows, window), jnp.float32),
            pltpu.VMEM((pairs * ambit, ambit), jnp.float32),
        ],
        compiler_params=pltpu.CompilerParams(
            collective_id=0, has_side_effects=True, vmem_limit_bytes=56 * 1024 * 1024
        ),
        cost_estimate=pl.CostEstimate(
            flops=2 * m_rows * ambit * window * width * pairs,
            transcendentals=0,
            bytes_accessed=kernel_rows.size * 2 + mask.size * 4 * 5,
        ),
    )(mask, quencher, kernel_rows, socs_weights)
    return result[0], result[1], result[2]


def solution(mesh):
    placed = (P("tile", None), P(), P(), P("tile", "kern"))
    return jax.shard_map(
        on_device,
        mesh=mesh,
        in_specs=placed,
        out_specs=(P("tile", "kern"), P("tile", "kern"), P("tile", "kern")),
        check_vma=False,
    )
```

```python
import functools

import jax
import jax.numpy as jnp
from jax import lax
from jax.experimental import pallas as pl
from jax.experimental.pallas import tpu as pltpu
from jax.sharding import PartitionSpec as P

STEPS = 8


DIFFUSE_ACID = 0.2
DIFFUSE_BASE = 0.1
QUENCH_RATE = 0.5
EXPOSURE = 0.35

BLOCKS = 9
SHIFTS = 8
HALO = STEPS
TAP_GROUP = 8


def toeplitz_selector(ambit, window, width):
    tap_ids = lax.iota(jnp.int32, ambit)
    input_ids = lax.iota(jnp.int32, window)
    output_ids = lax.iota(jnp.int32, width)
    offsets = input_ids[None, None, :] - output_ids[None, :, None]
    selector = (offsets == tap_ids[:, None, None]).astype(jnp.bfloat16)
    return selector.reshape(ambit, width * window)


def spread_of(value):
    rows, lanes = value.shape
    up = pltpu.roll(value, 1, 0)
    down = pltpu.roll(value, rows - 1, 0)
    left = pltpu.roll(value, 1, 1)
    right = pltpu.roll(value, lanes - 1, 1)
    return up + down + left + right - 4.0 * value


MASK_FROM = ((-1, 0), (1, 0), (-2, 0), (2, 0))
QUENCH_FROM = ((-1, -1), (-1, 0), (-1, 1), (0, -1), (0, 1), (1, -1), (1, 0), (1, 1))


def fused_kernel(
    mask_ref, q_ref, k_ref, w_smem,
    o_ref,
    mask_slots, q_slots, send_sems, recv_sems, taps_ref, win_ref, acc_ref, red_ref, rows_ref,
    shifted_ref,
    *, pairs, window, halo, width,
):
    tile = lax.axis_index("tile")
    kern = lax.axis_index("kern")
    tiles = lax.axis_size("tile")
    kerns = lax.axis_size("kern")
    local_rows, local_cols = q_ref.shape
    out_rows = local_rows + 2 * halo
    out_cols = local_cols + 2 * halo
    lanes = 2 * window
    ambit = k_ref.shape[1]
    groups = ambit // TAP_GROUP
    span = TAP_GROUP * window
    width_n = width * pairs

    def exists(dt, dq):
        return (tile + dt >= 0) & (tile + dt < tiles) & (kern + dq >= 0) & (kern + dq < kerns)

    def device(dt, dq):
        return {"tile": tile + dt, "kern": kern + dq}

    barrier = pltpu.get_barrier_semaphore()
    partners = sorted(set(MASK_FROM) | set(QUENCH_FROM))
    count = jnp.int32(0)
    for dt, dq in partners:
        here = exists(dt, dq)

        @pl.when(here)
        def _():
            pl.semaphore_signal(
                barrier, 1, device_id=device(dt, dq), device_id_type=pl.DeviceIdType.MESH
            )

        count = count + here.astype(jnp.int32)
    sel_lane = lax.broadcasted_iota(jnp.int32, (ambit, width * window), 1)
    sel_row = lax.broadcasted_iota(jnp.int32, (ambit, width * window), 0)
    selector = (sel_lane % window - sel_lane // window == sel_row).astype(jnp.bfloat16)

    rows_ref[...] = k_ref[...].astype(jnp.float32)

    def build(group, carry):
        kernel_rows = jnp.concatenate(
            [
                rows_ref[pl.ds(group * TAP_GROUP + j, pairs, stride=ambit), :]
                for j in range(TAP_GROUP)
            ],
            axis=0,
        ).astype(jnp.bfloat16)
        product = jnp.dot(
            kernel_rows, selector, preferred_element_type=jnp.float32
        ).astype(jnp.bfloat16)
        columns = [
            jnp.concatenate(
                [
                    product[j * pairs : (j + 1) * pairs, o * window : (o + 1) * window]
                    for o in range(width)
                ],
                axis=0,
            )
            for j in range(TAP_GROUP)
        ]
        taps_ref[:, pl.ds(pl.multiple_of(group * span, span), span)] = jnp.concatenate(
            columns, axis=1
        )
        return carry

    lax.fori_loop(0, groups // 4, build, 0)
    pl.semaphore_wait(barrier, count)

    def rows_for(source, dt, whole):
        height = source.shape[0]
        if dt == 0 or (abs(dt) == 1 and whole):
            return 0, height
        return (height - HALO, HALO) if dt < 0 else (0, HALO)

    plan = [(mask_ref, mask_slots, slot, offset, True) for slot, offset in enumerate(MASK_FROM)]
    plan += [(q_ref, q_slots, slot, offset, False) for slot, offset in enumerate(QUENCH_FROM)]
    copies = []
    for index, (source, slots, slot, (dt, dq), whole) in enumerate(plan):
        first, rows = rows_for(source, dt, whole)
        copy = pltpu.make_async_remote_copy(
            src_ref=source.at[pl.ds(first, rows)],
            dst_ref=slots.at[slot, pl.ds(first, rows)],
            send_sem=send_sems.at[index],
            recv_sem=recv_sems.at[index],
            device_id=device(-dt, -dq),
            device_id_type=pl.DeviceIdType.MESH,
        )

        @pl.when(exists(-dt, -dq))
        def _():
            copy.start()

        copies.append(copy)

    lax.fori_loop(groups // 4, groups, build, 0)

    def wait_for(kind):
        for copy, (source, slots, slot, (dt, dq), whole) in zip(copies, plan):
            if kind == "send":

                @pl.when(exists(-dt, -dq))
                def _():
                    copy.wait_send()

            elif (slots is mask_slots) == (kind == "mask"):

                @pl.when(exists(dt, dq))
                def _():
                    copy.wait_recv()

    wait_for("mask")

    def slot_rows(slots, slot, first, rows):
        dt, dq = (MASK_FROM if slots is mask_slots else QUENCH_FROM)[slot]
        value = slots[slot, pl.ds(first, rows), :]
        return jnp.where(exists(dt, dq), value, jnp.zeros_like(value))

    reach = HALO
    rows = jnp.concatenate(
        [
            slot_rows(mask_slots, 2, local_rows - reach, reach),
            slot_rows(mask_slots, 0, 0, local_rows),
            mask_ref[...],
            slot_rows(mask_slots, 1, 0, local_rows),
            slot_rows(mask_slots, 3, 0, reach),
        ],
        axis=0,
    ).astype(jnp.float32)
    total = rows.shape[1] + 128
    rows = jnp.concatenate([rows, jnp.zeros((rows.shape[0], 128), jnp.float32)], axis=1)
    lead = (win_ref.shape[0] // BLOCKS - out_rows) // 2 + halo
    for block in range(BLOCKS):
        start = kern * local_cols - lead + width * block
        part = pltpu.roll(rows, lax.rem(total - start, total), 1)[:, :window]
        win_ref[pl.ds(block, rows.shape[0], stride=BLOCKS), :] = part

    def band(left, middle, right):
        lane = lax.broadcasted_iota(jnp.int32, (middle.shape[0], lanes), 1)

        def widen(value):
            return jnp.concatenate(
                [value, jnp.zeros((value.shape[0], lanes - value.shape[1]), value.dtype)], axis=1
            )

        outer = lanes - (local_cols - halo)
        return jnp.where(
            lane < halo,
            pltpu.roll(widen(left), outer, 1),
            jnp.where(
                lane < halo + local_cols,
                pltpu.roll(widen(middle), halo, 1),
                jnp.where(lane < out_cols, pltpu.roll(widen(right), outer, 1), 0.0),
            ),
        )

    acc_ref[...] = jnp.zeros_like(acc_ref)

    height = win_ref.shape[0]
    for shift in range(SHIFTS):
        shifted_ref[shift, pl.ds(0, height - shift), :] = win_ref[pl.ds(shift, height - shift), :]

    def accumulate(group, carry):
        pieces = []
        for offset in range(32):
            start = pl.multiple_of(
                (group * 32 + offset) * SHIFTS + (group * 32 + offset) // SHIFTS * SHIFTS, SHIFTS
            )
            pieces.append(
                shifted_ref[offset % SHIFTS, pl.ds(start, out_rows * BLOCKS), :].astype(jnp.bfloat16)
            )
        left = jnp.concatenate(pieces, axis=1)
        right = taps_ref[:, pl.ds(pl.multiple_of(group * 32 * window, 32 * window), 32 * window)]
        acc_ref[...] += lax.dot_general(
            left, right, (((1,), (1,)), ((), ())), preferred_element_type=jnp.float32
        )
        return carry

    lax.fori_loop(0, ambit // 32, accumulate, 0)

    wait_for("quench")
    wait_for("send")
    low = local_rows - halo
    base = jnp.concatenate(
        [
            band(*(slot_rows(q_slots, s, low, halo) for s in (0, 1, 2))),
            band(slot_rows(q_slots, 3, 0, local_rows), q_ref[...], slot_rows(q_slots, 4, 0, local_rows)),
            band(*(slot_rows(q_slots, s, 0, halo) for s in (5, 6, 7))),
        ],
        axis=0,
    )


    kernel_of_lane = lax.broadcasted_iota(jnp.int32, (1, width_n), 1) % pairs // 2
    lane_weights = jnp.zeros((1, width_n), jnp.float32)
    for k in range(pairs // 2):
        lane_weights = jnp.where(kernel_of_lane == k, w_smem[k], lane_weights)
    summer = (
        lax.broadcasted_iota(jnp.int32, (width_n, window), 0) // pairs
        == lax.broadcasted_iota(jnp.int32, (width_n, window), 1)
    ).astype(jnp.float32)
    field = acc_ref[...]
    weighted = field * field * lane_weights
    red_ref[...] = jnp.dot(
        weighted, summer, precision=lax.Precision.HIGHEST,
        preferred_element_type=jnp.float32,
    )
    intensity = jnp.zeros((out_rows, lanes), jnp.float32)
    for block in range(BLOCKS):
        part = red_ref[pl.ds(block, out_rows, stride=BLOCKS), :]
        part = jnp.concatenate([part, jnp.zeros_like(part)], axis=1)
        intensity = intensity + pltpu.roll(part, width * block, 1) if block else part
    r = tile * local_rows - halo + lax.broadcasted_iota(jnp.int32, (out_rows, lanes), 0)
    c = kern * local_cols - halo + lax.broadcasted_iota(jnp.int32, (out_rows, lanes), 1)
    keep = (r >= 0) & (r < tiles * local_rows) & (c >= 0) & (c < kerns * local_cols)
    keep = keep & (c < kern * local_cols - halo + out_cols)
    acid = jnp.where(keep, 1.0 - jnp.exp(-EXPOSURE * intensity), 0.0)
    for _ in range(STEPS):
        quenched = QUENCH_RATE * acid * base
        acid_next = acid + DIFFUSE_ACID * spread_of(acid) - quenched
        base_next = base + DIFFUSE_BASE * spread_of(base) - quenched
        acid = jnp.where(keep, acid_next, 0.0)
        base = jnp.where(keep, base_next, 0.0)
    for index, value in enumerate((intensity, acid, base)):
        o_ref[index] = pltpu.roll(value, lanes - halo, 1)[halo : halo + local_rows, :local_cols]


def on_device(mask, kernels, socs_weights, quencher):
    ambit = kernels.shape[2]
    half_ambit = ambit // 2
    kern_count = lax.axis_size("kern")
    kern_index = lax.axis_index("kern")
    tile_index = lax.axis_index("tile")
    local_rows = mask.shape[0]
    local_cols = quencher.shape[1]
    halo = HALO
    out_rows = local_rows + 2 * halo
    out_cols = local_cols + 2 * halo
    width = out_cols // BLOCKS
    window = 128
    lanes = 2 * window
    window_rows = out_rows + ambit

    pairs = kernels.shape[0] * kernels.shape[1]
    kernel_rows = kernels.reshape(pairs * ambit, ambit)

    vmem = pl.BlockSpec(memory_space=pltpu.VMEM)
    out = jax.ShapeDtypeStruct((3, local_rows, local_cols), jnp.float32)
    copies = len(MASK_FROM) + len(QUENCH_FROM)
    m_rows = out_rows * BLOCKS
    result = pl.pallas_call(
        functools.partial(fused_kernel, pairs=pairs, window=window, halo=halo, width=width),
        out_shape=out,
        in_specs=[vmem] * 3 + [pl.BlockSpec(memory_space=pltpu.SMEM)],
        out_specs=vmem,
        scratch_shapes=[
            pltpu.VMEM((len(MASK_FROM),) + mask.shape, mask.dtype),
            pltpu.VMEM((len(QUENCH_FROM),) + quencher.shape, quencher.dtype),
            pltpu.SemaphoreType.DMA((copies,)),
            pltpu.SemaphoreType.DMA((copies,)),
            pltpu.VMEM((width * pairs, ambit * window), jnp.bfloat16),
            pltpu.VMEM((window_rows * BLOCKS, window), jnp.float32),
            pltpu.VMEM((m_rows, width * pairs), jnp.float32),
            pltpu.VMEM((m_rows, window), jnp.float32),
            pltpu.VMEM((pairs * ambit, ambit), jnp.float32),
            pltpu.VMEM((SHIFTS, window_rows * BLOCKS, window), jnp.float32),
        ],
        compiler_params=pltpu.CompilerParams(
            collective_id=0, has_side_effects=True, vmem_limit_bytes=56 * 1024 * 1024
        ),
        cost_estimate=pl.CostEstimate(
            flops=2 * m_rows * ambit * window * width * pairs,
            transcendentals=0,
            bytes_accessed=kernel_rows.size * 2 + mask.size * 4 * 5,
        ),
    )(mask, quencher, kernel_rows, socs_weights)
    return result[0], result[1], result[2]


def solution(mesh):
    placed = (P("tile", None), P(), P(), P("tile", "kern"))
    return jax.shard_map(
        on_device,
        mesh=mesh,
        in_specs=placed,
        out_specs=(P("tile", "kern"), P("tile", "kern"), P("tile", "kern")),
        check_vma=False,
    )
```

```python
import functools

import jax
import jax.numpy as jnp
from jax import lax
from jax.experimental import pallas as pl
from jax.experimental.pallas import tpu as pltpu
from jax.sharding import PartitionSpec as P

STEPS = 8


DIFFUSE_ACID = 0.2
DIFFUSE_BASE = 0.1
QUENCH_RATE = 0.5
EXPOSURE = 0.35

BLOCKS = 9
SHIFTS = 8
HALO = STEPS
TAP_GROUP = 8


def toeplitz_selector(ambit, window, width):
    tap_ids = lax.iota(jnp.int32, ambit)
    input_ids = lax.iota(jnp.int32, window)
    output_ids = lax.iota(jnp.int32, width)
    offsets = input_ids[None, None, :] - output_ids[None, :, None]
    selector = (offsets == tap_ids[:, None, None]).astype(jnp.bfloat16)
    return selector.reshape(ambit, width * window)


def spread_of(value):
    rows, lanes = value.shape
    up = pltpu.roll(value, 1, 0)
    down = pltpu.roll(value, rows - 1, 0)
    left = pltpu.roll(value, 1, 1)
    right = pltpu.roll(value, lanes - 1, 1)
    return up + down + left + right - 4.0 * value


MASK_FROM = ((-1, 0), (1, 0), (-2, 0), (2, 0))
QUENCH_FROM = ((-1, -1), (-1, 0), (-1, 1), (0, -1), (0, 1), (1, -1), (1, 0), (1, 1))


def fused_kernel(
    mask_ref, q_ref, k_ref, w_smem,
    o_ref,
    mask_slots, q_slots, send_sems, recv_sems, taps_ref, win_ref, acc_ref, red_ref, rows_ref,
    shifted_ref,
    *, pairs, window, halo, width,
):
    tile = lax.axis_index("tile")
    kern = lax.axis_index("kern")
    tiles = lax.axis_size("tile")
    kerns = lax.axis_size("kern")
    local_rows, local_cols = q_ref.shape
    out_rows = local_rows + 2 * halo
    out_cols = local_cols + 2 * halo
    lanes = 2 * window
    ambit = k_ref.shape[1]
    groups = ambit // TAP_GROUP
    span = TAP_GROUP * window
    width_n = width * pairs

    def exists(dt, dq):
        return (tile + dt >= 0) & (tile + dt < tiles) & (kern + dq >= 0) & (kern + dq < kerns)

    def device(dt, dq):
        return {"tile": tile + dt, "kern": kern + dq}

    barrier = pltpu.get_barrier_semaphore()
    partners = sorted(set(MASK_FROM) | set(QUENCH_FROM))
    count = jnp.int32(0)
    for dt, dq in partners:
        here = exists(dt, dq)

        @pl.when(here)
        def _():
            pl.semaphore_signal(
                barrier, 1, device_id=device(dt, dq), device_id_type=pl.DeviceIdType.MESH
            )

        count = count + here.astype(jnp.int32)
    sel_lane = lax.broadcasted_iota(jnp.int32, (ambit, width * window), 1)
    sel_row = lax.broadcasted_iota(jnp.int32, (ambit, width * window), 0)
    selector = (sel_lane % window - sel_lane // window == sel_row).astype(jnp.bfloat16)

    rows_ref[...] = k_ref[...].astype(jnp.float32)

    def build(group, carry):
        kernel_rows = jnp.concatenate(
            [
                rows_ref[pl.ds(group * TAP_GROUP + j, pairs, stride=ambit), :]
                for j in range(TAP_GROUP)
            ],
            axis=0,
        ).astype(jnp.bfloat16)
        product = jnp.dot(
            kernel_rows, selector, preferred_element_type=jnp.float32
        ).astype(jnp.bfloat16)
        columns = [
            jnp.concatenate(
                [
                    product[j * pairs : (j + 1) * pairs, o * window : (o + 1) * window]
                    for o in range(width)
                ],
                axis=0,
            )
            for j in range(TAP_GROUP)
        ]
        taps_ref[:, pl.ds(pl.multiple_of(group * span, span), span)] = jnp.concatenate(
            columns, axis=1
        )
        return carry

    lax.fori_loop(0, groups // 4, build, 0)
    pl.semaphore_wait(barrier, count)

    def rows_for(source, dt, whole):
        height = source.shape[0]
        if dt == 0 or (abs(dt) == 1 and whole):
            return 0, height
        return (height - HALO, HALO) if dt < 0 else (0, HALO)

    plan = [(mask_ref, mask_slots, slot, offset, True) for slot, offset in enumerate(MASK_FROM)]
    plan += [(q_ref, q_slots, slot, offset, False) for slot, offset in enumerate(QUENCH_FROM)]
    copies = []
    for index, (source, slots, slot, (dt, dq), whole) in enumerate(plan):
        first, rows = rows_for(source, dt, whole)
        copy = pltpu.make_async_remote_copy(
            src_ref=source.at[pl.ds(first, rows)],
            dst_ref=slots.at[slot, pl.ds(first, rows)],
            send_sem=send_sems.at[index],
            recv_sem=recv_sems.at[index],
            device_id=device(-dt, -dq),
            device_id_type=pl.DeviceIdType.MESH,
        )

        @pl.when(exists(-dt, -dq))
        def _():
            copy.start()

        copies.append(copy)

    lax.fori_loop(groups // 4, groups, build, 0)

    def wait_for(kind):
        for copy, (source, slots, slot, (dt, dq), whole) in zip(copies, plan):
            if kind == "send":

                @pl.when(exists(-dt, -dq))
                def _():
                    copy.wait_send()

            elif (slots is mask_slots) == (kind == "mask"):

                @pl.when(exists(dt, dq))
                def _():
                    copy.wait_recv()

    wait_for("mask")

    def slot_rows(slots, slot, first, rows):
        dt, dq = (MASK_FROM if slots is mask_slots else QUENCH_FROM)[slot]
        value = slots[slot, pl.ds(first, rows), :]
        return jnp.where(exists(dt, dq), value, jnp.zeros_like(value))

    reach = HALO
    rows = jnp.concatenate(
        [
            slot_rows(mask_slots, 2, local_rows - reach, reach),
            slot_rows(mask_slots, 0, 0, local_rows),
            mask_ref[...],
            slot_rows(mask_slots, 1, 0, local_rows),
            slot_rows(mask_slots, 3, 0, reach),
        ],
        axis=0,
    ).astype(jnp.float32)
    total = rows.shape[1] + 128
    rows = jnp.concatenate([rows, jnp.zeros((rows.shape[0], 128), jnp.float32)], axis=1)
    lead = (win_ref.shape[0] // BLOCKS - out_rows) // 2 + halo
    for block in range(BLOCKS):
        start = kern * local_cols - lead + width * block
        part = pltpu.roll(rows, lax.rem(total - start, total), 1)[:, :window]
        win_ref[pl.ds(block, rows.shape[0], stride=BLOCKS), :] = part

    def band(left, middle, right):
        lane = lax.broadcasted_iota(jnp.int32, (middle.shape[0], lanes), 1)

        def widen(value):
            return jnp.concatenate(
                [value, jnp.zeros((value.shape[0], lanes - value.shape[1]), value.dtype)], axis=1
            )

        outer = lanes - (local_cols - halo)
        return jnp.where(
            lane < halo,
            pltpu.roll(widen(left), outer, 1),
            jnp.where(
                lane < halo + local_cols,
                pltpu.roll(widen(middle), halo, 1),
                jnp.where(lane < out_cols, pltpu.roll(widen(right), outer, 1), 0.0),
            ),
        )

    acc_ref[...] = jnp.zeros_like(acc_ref)

    height = win_ref.shape[0]
    for shift in range(SHIFTS):
        shifted_ref[shift, pl.ds(0, height - shift), :] = win_ref[pl.ds(shift, height - shift), :]

    def accumulate(group, carry):
        pieces = []
        for offset in range(32):
            start = pl.multiple_of(
                (group * 32 + offset) * SHIFTS + (group * 32 + offset) // SHIFTS * SHIFTS, SHIFTS
            )
            pieces.append(
                shifted_ref[offset % SHIFTS, pl.ds(start, out_rows * BLOCKS), :].astype(jnp.bfloat16)
            )
        left = jnp.concatenate(pieces, axis=1)
        right = taps_ref[:, pl.ds(pl.multiple_of(group * 32 * window, 32 * window), 32 * window)]
        acc_ref[...] += lax.dot_general(
            left, right, (((1,), (1,)), ((), ())), preferred_element_type=jnp.float32
        )
        return carry

    lax.fori_loop(0, ambit // 32, accumulate, 0)

    wait_for("quench")
    wait_for("send")
    low = local_rows - halo
    base = jnp.concatenate(
        [
            band(*(slot_rows(q_slots, s, low, halo) for s in (0, 1, 2))),
            band(slot_rows(q_slots, 3, 0, local_rows), q_ref[...], slot_rows(q_slots, 4, 0, local_rows)),
            band(*(slot_rows(q_slots, s, 0, halo) for s in (5, 6, 7))),
        ],
        axis=0,
    )


    kernel_of_lane = lax.broadcasted_iota(jnp.int32, (1, width_n), 1) % pairs // 2
    lane_weights = jnp.zeros((1, width_n), jnp.float32)
    for k in range(pairs // 2):
        lane_weights = jnp.where(kernel_of_lane == k, w_smem[k], lane_weights)
    summer = (
        lax.broadcasted_iota(jnp.int32, (width_n, window), 0) // pairs
        == lax.broadcasted_iota(jnp.int32, (width_n, window), 1)
    ).astype(jnp.float32)
    field = acc_ref[...]
    weighted = field * field * lane_weights
    red_ref[...] = jnp.dot(
        weighted, summer, precision=lax.Precision.HIGH,
        preferred_element_type=jnp.float32,
    )
    intensity = jnp.zeros((out_rows, lanes), jnp.float32)
    for block in range(BLOCKS):
        part = red_ref[pl.ds(block, out_rows, stride=BLOCKS), :]
        part = jnp.concatenate([part, jnp.zeros_like(part)], axis=1)
        intensity = intensity + pltpu.roll(part, width * block, 1) if block else part
    r = tile * local_rows - halo + lax.broadcasted_iota(jnp.int32, (out_rows, lanes), 0)
    c = kern * local_cols - halo + lax.broadcasted_iota(jnp.int32, (out_rows, lanes), 1)
    keep = (r >= 0) & (r < tiles * local_rows) & (c >= 0) & (c < kerns * local_cols)
    keep = keep & (c < kern * local_cols - halo + out_cols)
    acid = jnp.where(keep, 1.0 - jnp.exp(-EXPOSURE * intensity), 0.0)
    for _ in range(STEPS):
        quenched = QUENCH_RATE * acid * base
        acid_next = acid + DIFFUSE_ACID * spread_of(acid) - quenched
        base_next = base + DIFFUSE_BASE * spread_of(base) - quenched
        acid = jnp.where(keep, acid_next, 0.0)
        base = jnp.where(keep, base_next, 0.0)
    for index, value in enumerate((intensity, acid, base)):
        o_ref[index] = pltpu.roll(value, lanes - halo, 1)[halo : halo + local_rows, :local_cols]


def on_device(mask, kernels, socs_weights, quencher):
    ambit = kernels.shape[2]
    half_ambit = ambit // 2
    kern_count = lax.axis_size("kern")
    kern_index = lax.axis_index("kern")
    tile_index = lax.axis_index("tile")
    local_rows = mask.shape[0]
    local_cols = quencher.shape[1]
    halo = HALO
    out_rows = local_rows + 2 * halo
    out_cols = local_cols + 2 * halo
    width = out_cols // BLOCKS
    window = 128
    lanes = 2 * window
    window_rows = out_rows + ambit

    pairs = kernels.shape[0] * kernels.shape[1]
    kernel_rows = kernels.reshape(pairs * ambit, ambit)

    vmem = pl.BlockSpec(memory_space=pltpu.VMEM)
    out = jax.ShapeDtypeStruct((3, local_rows, local_cols), jnp.float32)
    copies = len(MASK_FROM) + len(QUENCH_FROM)
    m_rows = out_rows * BLOCKS
    result = pl.pallas_call(
        functools.partial(fused_kernel, pairs=pairs, window=window, halo=halo, width=width),
        out_shape=out,
        in_specs=[vmem] * 3 + [pl.BlockSpec(memory_space=pltpu.SMEM)],
        out_specs=vmem,
        scratch_shapes=[
            pltpu.VMEM((len(MASK_FROM),) + mask.shape, mask.dtype),
            pltpu.VMEM((len(QUENCH_FROM),) + quencher.shape, quencher.dtype),
            pltpu.SemaphoreType.DMA((copies,)),
            pltpu.SemaphoreType.DMA((copies,)),
            pltpu.VMEM((width * pairs, ambit * window), jnp.bfloat16),
            pltpu.VMEM((window_rows * BLOCKS, window), jnp.float32),
            pltpu.VMEM((m_rows, width * pairs), jnp.float32),
            pltpu.VMEM((m_rows, window), jnp.float32),
            pltpu.VMEM((pairs * ambit, ambit), jnp.float32),
            pltpu.VMEM((SHIFTS, window_rows * BLOCKS, window), jnp.float32),
        ],
        compiler_params=pltpu.CompilerParams(
            collective_id=0, has_side_effects=True, vmem_limit_bytes=56 * 1024 * 1024
        ),
        cost_estimate=pl.CostEstimate(
            flops=2 * m_rows * ambit * window * width * pairs,
            transcendentals=0,
            bytes_accessed=kernel_rows.size * 2 + mask.size * 4 * 5,
        ),
    )(mask, quencher, kernel_rows, socs_weights)
    return result[0], result[1], result[2]


def solution(mesh):
    placed = (P("tile", None), P(), P(), P("tile", "kern"))
    return jax.shard_map(
        on_device,
        mesh=mesh,
        in_specs=placed,
        out_specs=(P("tile", "kern"), P("tile", "kern"), P("tile", "kern")),
        check_vma=False,
    )
```

```python
import functools

import jax
import jax.numpy as jnp
from jax import lax
from jax.experimental import pallas as pl
from jax.experimental.pallas import tpu as pltpu
from jax.sharding import PartitionSpec as P

STEPS = 8


DIFFUSE_ACID = 0.2
DIFFUSE_BASE = 0.1
QUENCH_RATE = 0.5
EXPOSURE = 0.35

BLOCKS = 9
SHIFTS = 8
HALO = STEPS
TAP_GROUP = 8


def toeplitz_selector(ambit, window, width):
    tap_ids = lax.iota(jnp.int32, ambit)
    input_ids = lax.iota(jnp.int32, window)
    output_ids = lax.iota(jnp.int32, width)
    offsets = input_ids[None, None, :] - output_ids[None, :, None]
    selector = (offsets == tap_ids[:, None, None]).astype(jnp.bfloat16)
    return selector.reshape(ambit, width * window)


def spread_of(value):
    rows, lanes = value.shape
    up = pltpu.roll(value, 1, 0)
    down = pltpu.roll(value, rows - 1, 0)
    left = pltpu.roll(value, 1, 1)
    right = pltpu.roll(value, lanes - 1, 1)
    return up + down + left + right - 4.0 * value


MASK_FROM = ((-1, 0), (1, 0), (-2, 0), (2, 0))
QUENCH_FROM = ((-1, -1), (-1, 0), (-1, 1), (0, -1), (0, 1), (1, -1), (1, 0), (1, 1))


def fused_kernel(
    mask_ref, q_ref, k_ref, w_smem,
    o_ref,
    mask_slots, q_slots, send_sems, recv_sems, taps_ref, win_ref, acc_ref, red_ref, rows_ref,
    shifted_ref,
    *, pairs, window, halo, width,
):
    tile = lax.axis_index("tile")
    kern = lax.axis_index("kern")
    tiles = lax.axis_size("tile")
    kerns = lax.axis_size("kern")
    local_rows, local_cols = q_ref.shape
    out_rows = local_rows + 2 * halo
    out_cols = local_cols + 2 * halo
    lanes = 2 * window
    ambit = k_ref.shape[1]
    groups = ambit // TAP_GROUP
    span = TAP_GROUP * window
    width_n = width * pairs

    def exists(dt, dq):
        return (tile + dt >= 0) & (tile + dt < tiles) & (kern + dq >= 0) & (kern + dq < kerns)

    def device(dt, dq):
        return {"tile": tile + dt, "kern": kern + dq}

    barrier = pltpu.get_barrier_semaphore()
    partners = sorted(set(MASK_FROM) | set(QUENCH_FROM))
    count = jnp.int32(0)
    for dt, dq in partners:
        here = exists(dt, dq)

        @pl.when(here)
        def _():
            pl.semaphore_signal(
                barrier, 1, device_id=device(dt, dq), device_id_type=pl.DeviceIdType.MESH
            )

        count = count + here.astype(jnp.int32)
    sel_lane = lax.broadcasted_iota(jnp.int32, (ambit, width * window), 1)
    sel_row = lax.broadcasted_iota(jnp.int32, (ambit, width * window), 0)
    selector = (sel_lane % window - sel_lane // window == sel_row).astype(jnp.bfloat16)

    rows_ref[...] = k_ref[...].astype(jnp.float32)

    def build(group, carry):
        kernel_rows = jnp.concatenate(
            [
                rows_ref[pl.ds(group * TAP_GROUP + j, pairs, stride=ambit), :]
                for j in range(TAP_GROUP)
            ],
            axis=0,
        ).astype(jnp.bfloat16)
        product = jnp.dot(
            kernel_rows, selector, preferred_element_type=jnp.float32
        ).astype(jnp.bfloat16)
        columns = [
            jnp.concatenate(
                [
                    product[j * pairs : (j + 1) * pairs, o * window : (o + 1) * window]
                    for o in range(width)
                ],
                axis=0,
            )
            for j in range(TAP_GROUP)
        ]
        taps_ref[:, pl.ds(pl.multiple_of(group * span, span), span)] = jnp.concatenate(
            columns, axis=1
        )
        return carry

    lax.fori_loop(0, groups // 4, build, 0)
    pl.semaphore_wait(barrier, count)

    def rows_for(source, dt, whole):
        height = source.shape[0]
        if dt == 0 or (abs(dt) == 1 and whole):
            return 0, height
        return (height - HALO, HALO) if dt < 0 else (0, HALO)

    plan = [(mask_ref, mask_slots, slot, offset, True) for slot, offset in enumerate(MASK_FROM)]
    plan += [(q_ref, q_slots, slot, offset, False) for slot, offset in enumerate(QUENCH_FROM)]
    copies = []
    for index, (source, slots, slot, (dt, dq), whole) in enumerate(plan):
        first, rows = rows_for(source, dt, whole)
        copy = pltpu.make_async_remote_copy(
            src_ref=source.at[pl.ds(first, rows)],
            dst_ref=slots.at[slot, pl.ds(first, rows)],
            send_sem=send_sems.at[index],
            recv_sem=recv_sems.at[index],
            device_id=device(-dt, -dq),
            device_id_type=pl.DeviceIdType.MESH,
        )

        @pl.when(exists(-dt, -dq))
        def _():
            copy.start()

        copies.append(copy)

    lax.fori_loop(groups // 4, groups, build, 0)

    def wait_for(kind):
        for copy, (source, slots, slot, (dt, dq), whole) in zip(copies, plan):
            if kind == "send":

                @pl.when(exists(-dt, -dq))
                def _():
                    copy.wait_send()

            elif (slots is mask_slots) == (kind == "mask"):

                @pl.when(exists(dt, dq))
                def _():
                    copy.wait_recv()

    wait_for("mask")

    def slot_rows(slots, slot, first, rows):
        dt, dq = (MASK_FROM if slots is mask_slots else QUENCH_FROM)[slot]
        value = slots[slot, pl.ds(first, rows), :]
        return jnp.where(exists(dt, dq), value, jnp.zeros_like(value))

    reach = HALO
    rows = jnp.concatenate(
        [
            slot_rows(mask_slots, 2, local_rows - reach, reach),
            slot_rows(mask_slots, 0, 0, local_rows),
            mask_ref[...],
            slot_rows(mask_slots, 1, 0, local_rows),
            slot_rows(mask_slots, 3, 0, reach),
        ],
        axis=0,
    ).astype(jnp.float32)
    total = rows.shape[1] + 128
    rows = jnp.concatenate([rows, jnp.zeros((rows.shape[0], 128), jnp.float32)], axis=1)
    lead = (win_ref.shape[0] // BLOCKS - out_rows) // 2 + halo
    for block in range(BLOCKS):
        start = kern * local_cols - lead + width * block
        part = pltpu.roll(rows, lax.rem(total - start, total), 1)[:, :window]
        win_ref[pl.ds(block, rows.shape[0], stride=BLOCKS), :] = part

    def band(left, middle, right):
        lane = lax.broadcasted_iota(jnp.int32, (middle.shape[0], lanes), 1)

        def widen(value):
            return jnp.concatenate(
                [value, jnp.zeros((value.shape[0], lanes - value.shape[1]), value.dtype)], axis=1
            )

        outer = lanes - (local_cols - halo)
        return jnp.where(
            lane < halo,
            pltpu.roll(widen(left), outer, 1),
            jnp.where(
                lane < halo + local_cols,
                pltpu.roll(widen(middle), halo, 1),
                jnp.where(lane < out_cols, pltpu.roll(widen(right), outer, 1), 0.0),
            ),
        )

    acc_ref[...] = jnp.zeros_like(acc_ref)

    height = win_ref.shape[0]
    for shift in range(SHIFTS):
        shifted_ref[shift, pl.ds(0, height - shift), :] = win_ref[pl.ds(shift, height - shift), :]

    def accumulate(group, carry):
        pieces = []
        for offset in range(32):
            start = pl.multiple_of(
                (group * 32 + offset) * SHIFTS + (group * 32 + offset) // SHIFTS * SHIFTS, SHIFTS
            )
            pieces.append(
                shifted_ref[offset % SHIFTS, pl.ds(start, out_rows * BLOCKS), :].astype(jnp.bfloat16)
            )
        left = jnp.concatenate(pieces, axis=1)
        right = taps_ref[:, pl.ds(pl.multiple_of(group * 32 * window, 32 * window), 32 * window)]
        acc_ref[...] += lax.dot_general(
            left, right, (((1,), (1,)), ((), ())), preferred_element_type=jnp.float32
        )
        return carry

    lax.fori_loop(0, ambit // 32, accumulate, 0)

    wait_for("quench")
    wait_for("send")
    low = local_rows - halo
    base = jnp.concatenate(
        [
            band(*(slot_rows(q_slots, s, low, halo) for s in (0, 1, 2))),
            band(slot_rows(q_slots, 3, 0, local_rows), q_ref[...], slot_rows(q_slots, 4, 0, local_rows)),
            band(*(slot_rows(q_slots, s, 0, halo) for s in (5, 6, 7))),
        ],
        axis=0,
    )


    kernel_of_lane = lax.broadcasted_iota(jnp.int32, (1, width_n), 1) % pairs // 2
    lane_weights = jnp.zeros((1, width_n), jnp.float32)
    for k in range(pairs // 2):
        lane_weights = jnp.where(kernel_of_lane == k, w_smem[k], lane_weights)
    summer = (
        lax.broadcasted_iota(jnp.int32, (width_n, window), 0) // pairs
        == lax.broadcasted_iota(jnp.int32, (width_n, window), 1)
    ).astype(jnp.float32)
    field = acc_ref[...]
    weighted = field * field * lane_weights
    high = weighted.astype(jnp.bfloat16)
    low = (weighted - high.astype(jnp.float32)).astype(jnp.bfloat16)
    summer = summer.astype(jnp.bfloat16)
    red_ref[...] = jnp.dot(high, summer, preferred_element_type=jnp.float32) + jnp.dot(
        low, summer, preferred_element_type=jnp.float32
    )
    intensity = jnp.zeros((out_rows, lanes), jnp.float32)
    for block in range(BLOCKS):
        part = red_ref[pl.ds(block, out_rows, stride=BLOCKS), :]
        part = jnp.concatenate([part, jnp.zeros_like(part)], axis=1)
        intensity = intensity + pltpu.roll(part, width * block, 1) if block else part
    r = tile * local_rows - halo + lax.broadcasted_iota(jnp.int32, (out_rows, lanes), 0)
    c = kern * local_cols - halo + lax.broadcasted_iota(jnp.int32, (out_rows, lanes), 1)
    keep = (r >= 0) & (r < tiles * local_rows) & (c >= 0) & (c < kerns * local_cols)
    keep = keep & (c < kern * local_cols - halo + out_cols)
    acid = jnp.where(keep, 1.0 - jnp.exp(-EXPOSURE * intensity), 0.0)
    for _ in range(STEPS):
        quenched = QUENCH_RATE * acid * base
        acid_next = acid + DIFFUSE_ACID * spread_of(acid) - quenched
        base_next = base + DIFFUSE_BASE * spread_of(base) - quenched
        acid = jnp.where(keep, acid_next, 0.0)
        base = jnp.where(keep, base_next, 0.0)
    for index, value in enumerate((intensity, acid, base)):
        o_ref[index] = pltpu.roll(value, lanes - halo, 1)[halo : halo + local_rows, :local_cols]


def on_device(mask, kernels, socs_weights, quencher):
    ambit = kernels.shape[2]
    half_ambit = ambit // 2
    kern_count = lax.axis_size("kern")
    kern_index = lax.axis_index("kern")
    tile_index = lax.axis_index("tile")
    local_rows = mask.shape[0]
    local_cols = quencher.shape[1]
    halo = HALO
    out_rows = local_rows + 2 * halo
    out_cols = local_cols + 2 * halo
    width = out_cols // BLOCKS
    window = 128
    lanes = 2 * window
    window_rows = out_rows + ambit

    pairs = kernels.shape[0] * kernels.shape[1]
    kernel_rows = kernels.reshape(pairs * ambit, ambit)

    vmem = pl.BlockSpec(memory_space=pltpu.VMEM)
    out = jax.ShapeDtypeStruct((3, local_rows, local_cols), jnp.float32)
    copies = len(MASK_FROM) + len(QUENCH_FROM)
    m_rows = out_rows * BLOCKS
    result = pl.pallas_call(
        functools.partial(fused_kernel, pairs=pairs, window=window, halo=halo, width=width),
        out_shape=out,
        in_specs=[vmem] * 3 + [pl.BlockSpec(memory_space=pltpu.SMEM)],
        out_specs=vmem,
        scratch_shapes=[
            pltpu.VMEM((len(MASK_FROM),) + mask.shape, mask.dtype),
            pltpu.VMEM((len(QUENCH_FROM),) + quencher.shape, quencher.dtype),
            pltpu.SemaphoreType.DMA((copies,)),
            pltpu.SemaphoreType.DMA((copies,)),
            pltpu.VMEM((width * pairs, ambit * window), jnp.bfloat16),
            pltpu.VMEM((window_rows * BLOCKS, window), jnp.float32),
            pltpu.VMEM((m_rows, width * pairs), jnp.float32),
            pltpu.VMEM((m_rows, window), jnp.float32),
            pltpu.VMEM((pairs * ambit, ambit), jnp.float32),
            pltpu.VMEM((SHIFTS, window_rows * BLOCKS, window), jnp.float32),
        ],
        compiler_params=pltpu.CompilerParams(
            collective_id=0, has_side_effects=True, vmem_limit_bytes=56 * 1024 * 1024
        ),
        cost_estimate=pl.CostEstimate(
            flops=2 * m_rows * ambit * window * width * pairs,
            transcendentals=0,
            bytes_accessed=kernel_rows.size * 2 + mask.size * 4 * 5,
        ),
    )(mask, quencher, kernel_rows, socs_weights)
    return result[0], result[1], result[2]


def solution(mesh):
    placed = (P("tile", None), P(), P(), P("tile", "kern"))
    return jax.shard_map(
        on_device,
        mesh=mesh,
        in_specs=placed,
        out_specs=(P("tile", "kern"), P("tile", "kern"), P("tile", "kern")),
        check_vma=False,
    )
```

```python
import functools

import jax
import jax.numpy as jnp
from jax import lax
from jax.experimental import pallas as pl
from jax.experimental.pallas import tpu as pltpu
from jax.sharding import PartitionSpec as P

STEPS = 8


DIFFUSE_ACID = 0.2
DIFFUSE_BASE = 0.1
QUENCH_RATE = 0.5
EXPOSURE = 0.35

BLOCKS = 9
SHIFTS = 8
HALO = STEPS
TAP_GROUP = 8


def toeplitz_selector(ambit, window, width):
    tap_ids = lax.iota(jnp.int32, ambit)
    input_ids = lax.iota(jnp.int32, window)
    output_ids = lax.iota(jnp.int32, width)
    offsets = input_ids[None, None, :] - output_ids[None, :, None]
    selector = (offsets == tap_ids[:, None, None]).astype(jnp.bfloat16)
    return selector.reshape(ambit, width * window)


def spread_of(value):
    rows, lanes = value.shape
    up = pltpu.roll(value, 1, 0)
    down = pltpu.roll(value, rows - 1, 0)
    left = pltpu.roll(value, 1, 1)
    right = pltpu.roll(value, lanes - 1, 1)
    return up + down + left + right - 4.0 * value


MASK_FROM = ((-1, 0), (1, 0), (-2, 0), (2, 0))
QUENCH_FROM = ((-1, -1), (-1, 0), (-1, 1), (0, -1), (0, 1), (1, -1), (1, 0), (1, 1))


def fused_kernel(
    mask_ref, q_ref, k_ref, w_smem,
    o_ref,
    mask_slots, q_slots, send_sems, recv_sems, taps_ref, win_ref, acc_ref, red_ref, rows_ref,
    shifted_ref,
    *, pairs, window, halo, width,
):
    tile = lax.axis_index("tile")
    kern = lax.axis_index("kern")
    tiles = lax.axis_size("tile")
    kerns = lax.axis_size("kern")
    local_rows, local_cols = q_ref.shape
    out_rows = local_rows + 2 * halo
    out_cols = local_cols + 2 * halo
    lanes = 2 * window
    ambit = k_ref.shape[1]
    groups = ambit // TAP_GROUP
    span = TAP_GROUP * window
    width_n = width * pairs

    def exists(dt, dq):
        return (tile + dt >= 0) & (tile + dt < tiles) & (kern + dq >= 0) & (kern + dq < kerns)

    def device(dt, dq):
        return {"tile": tile + dt, "kern": kern + dq}

    barrier = pltpu.get_barrier_semaphore()
    partners = sorted(set(MASK_FROM) | set(QUENCH_FROM))
    count = jnp.int32(0)
    for dt, dq in partners:
        here = exists(dt, dq)

        @pl.when(here)
        def _():
            pl.semaphore_signal(
                barrier, 1, device_id=device(dt, dq), device_id_type=pl.DeviceIdType.MESH
            )

        count = count + here.astype(jnp.int32)
    sel_lane = lax.broadcasted_iota(jnp.int32, (ambit, width * window), 1)
    sel_row = lax.broadcasted_iota(jnp.int32, (ambit, width * window), 0)
    selector = (sel_lane % window - sel_lane // window == sel_row).astype(jnp.bfloat16)

    rows_ref[...] = k_ref[...].astype(jnp.float32)

    def build(group, carry):
        kernel_rows = jnp.concatenate(
            [
                rows_ref[pl.ds(group * TAP_GROUP + j, pairs, stride=ambit), :]
                for j in range(TAP_GROUP)
            ],
            axis=0,
        ).astype(jnp.bfloat16)
        product = jnp.dot(
            kernel_rows, selector, preferred_element_type=jnp.float32
        ).astype(jnp.bfloat16)
        columns = [
            jnp.concatenate(
                [
                    product[j * pairs : (j + 1) * pairs, o * window : (o + 1) * window]
                    for o in range(width)
                ],
                axis=0,
            )
            for j in range(TAP_GROUP)
        ]
        taps_ref[:, pl.ds(pl.multiple_of(group * span, span), span)] = jnp.concatenate(
            columns, axis=1
        )
        return carry

    lax.fori_loop(0, groups // 4, build, 0)
    pl.semaphore_wait(barrier, count)

    def rows_for(source, dt, whole):
        height = source.shape[0]
        if dt == 0 or (abs(dt) == 1 and whole):
            return 0, height
        return (height - HALO, HALO) if dt < 0 else (0, HALO)

    plan = [(mask_ref, mask_slots, slot, offset, True) for slot, offset in enumerate(MASK_FROM)]
    plan += [(q_ref, q_slots, slot, offset, False) for slot, offset in enumerate(QUENCH_FROM)]
    copies = []
    for index, (source, slots, slot, (dt, dq), whole) in enumerate(plan):
        first, rows = rows_for(source, dt, whole)
        copy = pltpu.make_async_remote_copy(
            src_ref=source.at[pl.ds(first, rows)],
            dst_ref=slots.at[slot, pl.ds(first, rows)],
            send_sem=send_sems.at[index],
            recv_sem=recv_sems.at[index],
            device_id=device(-dt, -dq),
            device_id_type=pl.DeviceIdType.MESH,
        )

        @pl.when(exists(-dt, -dq))
        def _():
            copy.start()

        copies.append(copy)

    lax.fori_loop(groups // 4, groups, build, 0)

    def wait_for(kind):
        for copy, (source, slots, slot, (dt, dq), whole) in zip(copies, plan):
            if kind == "send":

                @pl.when(exists(-dt, -dq))
                def _():
                    copy.wait_send()

            elif (slots is mask_slots) == (kind == "mask"):

                @pl.when(exists(dt, dq))
                def _():
                    copy.wait_recv()

    wait_for("mask")

    def slot_rows(slots, slot, first, rows):
        dt, dq = (MASK_FROM if slots is mask_slots else QUENCH_FROM)[slot]
        value = slots[slot, pl.ds(first, rows), :]
        return jnp.where(exists(dt, dq), value, jnp.zeros_like(value))

    reach = HALO
    rows = jnp.concatenate(
        [
            slot_rows(mask_slots, 2, local_rows - reach, reach),
            slot_rows(mask_slots, 0, 0, local_rows),
            mask_ref[...],
            slot_rows(mask_slots, 1, 0, local_rows),
            slot_rows(mask_slots, 3, 0, reach),
        ],
        axis=0,
    ).astype(jnp.float32)
    total = rows.shape[1] + 128
    rows = jnp.concatenate([rows, jnp.zeros((rows.shape[0], 128), jnp.float32)], axis=1)
    lead = (win_ref.shape[0] // BLOCKS - out_rows) // 2 + halo
    for block in range(BLOCKS):
        start = kern * local_cols - lead + width * block
        part = pltpu.roll(rows, lax.rem(total - start, total), 1)[:, :window]
        for shift in range(SHIFTS):
            if block >= shift:
                shifted_ref[shift, pl.ds(block - shift, rows.shape[0], stride=BLOCKS), :] = part
            else:
                shifted_ref[
                    shift, pl.ds(BLOCKS + block - shift, rows.shape[0] - 1, stride=BLOCKS), :
                ] = part[1:]

    def band(left, middle, right):
        lane = lax.broadcasted_iota(jnp.int32, (middle.shape[0], lanes), 1)

        def widen(value):
            return jnp.concatenate(
                [value, jnp.zeros((value.shape[0], lanes - value.shape[1]), value.dtype)], axis=1
            )

        outer = lanes - (local_cols - halo)
        return jnp.where(
            lane < halo,
            pltpu.roll(widen(left), outer, 1),
            jnp.where(
                lane < halo + local_cols,
                pltpu.roll(widen(middle), halo, 1),
                jnp.where(lane < out_cols, pltpu.roll(widen(right), outer, 1), 0.0),
            ),
        )


    def accumulate(group, carry):
        pieces = []
        for offset in range(32):
            start = pl.multiple_of(
                (group * 32 + offset) * SHIFTS + (group * 32 + offset) // SHIFTS * SHIFTS, SHIFTS
            )
            pieces.append(
                shifted_ref[offset % SHIFTS, pl.ds(start, out_rows * BLOCKS), :].astype(jnp.bfloat16)
            )
        left = jnp.concatenate(pieces, axis=1)
        right = taps_ref[:, pl.ds(pl.multiple_of(group * 32 * window, 32 * window), 32 * window)]
        product = lax.dot_general(
            left, right, (((1,), (1,)), ((), ())), preferred_element_type=jnp.float32
        )
        if group == 0:
            acc_ref[...] = product
        else:
            acc_ref[...] += product
        return carry

    for group in range(ambit // 32):
        accumulate(group, 0)

    wait_for("quench")
    wait_for("send")
    low = local_rows - halo
    base = jnp.concatenate(
        [
            band(*(slot_rows(q_slots, s, low, halo) for s in (0, 1, 2))),
            band(slot_rows(q_slots, 3, 0, local_rows), q_ref[...], slot_rows(q_slots, 4, 0, local_rows)),
            band(*(slot_rows(q_slots, s, 0, halo) for s in (5, 6, 7))),
        ],
        axis=0,
    )


    kernel_of_lane = lax.broadcasted_iota(jnp.int32, (1, width_n), 1) % pairs // 2
    lane_weights = jnp.zeros((1, width_n), jnp.float32)
    for k in range(pairs // 2):
        lane_weights = jnp.where(kernel_of_lane == k, w_smem[k], lane_weights)
    summer = (
        lax.broadcasted_iota(jnp.int32, (width_n, window), 0) // pairs
        == lax.broadcasted_iota(jnp.int32, (width_n, window), 1)
    ).astype(jnp.float32)
    field = acc_ref[...]
    weighted = field * field * lane_weights
    high = weighted.astype(jnp.bfloat16)
    low = (weighted - high.astype(jnp.float32)).astype(jnp.bfloat16)
    summer = summer.astype(jnp.bfloat16)
    red_ref[...] = jnp.dot(high, summer, preferred_element_type=jnp.float32) + jnp.dot(
        low, summer, preferred_element_type=jnp.float32
    )
    intensity = jnp.zeros((out_rows, lanes), jnp.float32)
    for block in range(BLOCKS):
        part = red_ref[pl.ds(block, out_rows, stride=BLOCKS), :]
        part = jnp.concatenate([part, jnp.zeros_like(part)], axis=1)
        intensity = intensity + pltpu.roll(part, width * block, 1) if block else part
    r = tile * local_rows - halo + lax.broadcasted_iota(jnp.int32, (out_rows, lanes), 0)
    c = kern * local_cols - halo + lax.broadcasted_iota(jnp.int32, (out_rows, lanes), 1)
    keep = (r >= 0) & (r < tiles * local_rows) & (c >= 0) & (c < kerns * local_cols)
    keep = keep & (c < kern * local_cols - halo + out_cols)
    acid = jnp.where(keep, 1.0 - jnp.exp(-EXPOSURE * intensity), 0.0)
    for _ in range(STEPS):
        quenched = QUENCH_RATE * acid * base
        acid_next = acid + DIFFUSE_ACID * spread_of(acid) - quenched
        base_next = base + DIFFUSE_BASE * spread_of(base) - quenched
        acid = jnp.where(keep, acid_next, 0.0)
        base = jnp.where(keep, base_next, 0.0)
    for index, value in enumerate((intensity, acid, base)):
        o_ref[index] = pltpu.roll(value, lanes - halo, 1)[halo : halo + local_rows, :local_cols]


def on_device(mask, kernels, socs_weights, quencher):
    ambit = kernels.shape[2]
    half_ambit = ambit // 2
    kern_count = lax.axis_size("kern")
    kern_index = lax.axis_index("kern")
    tile_index = lax.axis_index("tile")
    local_rows = mask.shape[0]
    local_cols = quencher.shape[1]
    halo = HALO
    out_rows = local_rows + 2 * halo
    out_cols = local_cols + 2 * halo
    width = out_cols // BLOCKS
    window = 128
    lanes = 2 * window
    window_rows = out_rows + ambit

    pairs = kernels.shape[0] * kernels.shape[1]
    kernel_rows = kernels.reshape(pairs * ambit, ambit)

    vmem = pl.BlockSpec(memory_space=pltpu.VMEM)
    out = jax.ShapeDtypeStruct((3, local_rows, local_cols), jnp.float32)
    copies = len(MASK_FROM) + len(QUENCH_FROM)
    m_rows = out_rows * BLOCKS
    result = pl.pallas_call(
        functools.partial(fused_kernel, pairs=pairs, window=window, halo=halo, width=width),
        out_shape=out,
        in_specs=[vmem] * 3 + [pl.BlockSpec(memory_space=pltpu.SMEM)],
        out_specs=vmem,
        scratch_shapes=[
            pltpu.VMEM((len(MASK_FROM),) + mask.shape, mask.dtype),
            pltpu.VMEM((len(QUENCH_FROM),) + quencher.shape, quencher.dtype),
            pltpu.SemaphoreType.DMA((copies,)),
            pltpu.SemaphoreType.DMA((copies,)),
            pltpu.VMEM((width * pairs, ambit * window), jnp.bfloat16),
            pltpu.VMEM((window_rows * BLOCKS, window), jnp.float32),
            pltpu.VMEM((m_rows, width * pairs), jnp.float32),
            pltpu.VMEM((m_rows, window), jnp.float32),
            pltpu.VMEM((pairs * ambit, ambit), jnp.float32),
            pltpu.VMEM((SHIFTS, window_rows * BLOCKS, window), jnp.float32),
        ],
        compiler_params=pltpu.CompilerParams(
            collective_id=0, has_side_effects=True, vmem_limit_bytes=56 * 1024 * 1024
        ),
        cost_estimate=pl.CostEstimate(
            flops=2 * m_rows * ambit * window * width * pairs,
            transcendentals=0,
            bytes_accessed=kernel_rows.size * 2 + mask.size * 4 * 5,
        ),
    )(mask, quencher, kernel_rows, socs_weights)
    return result[0], result[1], result[2]


def solution(mesh):
    placed = (P("tile", None), P(), P(), P("tile", "kern"))
    return jax.shard_map(
        on_device,
        mesh=mesh,
        in_specs=placed,
        out_specs=(P("tile", "kern"), P("tile", "kern"), P("tile", "kern")),
        check_vma=False,
    )
```
